512 devices in a mesh: seq: 16 (over y, z_hi), tp: 32 (over z_lo, x, core).
Axes of the slice: x: 4, y: 8, z: 8 (z_hi: 2, z_lo: 4; z = z_hi * 4 + z_lo), core: 2. Of those that a mesh axis runs over, the one named last changes fastest.
Arguments:
- hidden_in: bfloat16 [4096, 5120], P('seq', 'tp'), may hold values from -16 to 16
- seg_ids: int32 [4096], P('seq'), may hold values from 0 to 3, never falling along the last dimension, each value on 1 to 2176 neighbouring positions
- positions: int32 [3, 4096], P(None, 'seq'), may hold values from 0 to 63
- mod_table: float32 [4, 3, 5120], P(None, None, 'tp'), may hold values from -4 to 4
- w_qkv: bfloat16 [5120, 3, 4096], P('seq', None, 'tp')
- q_gain: float32 [4096], P('tp'), may hold values from 0.5 to 3.5
- k_gain: float32 [4096], P('tp'), may hold values from 0.5 to 3.5
- w_out: bfloat16 [4096, 5120], P('tp', 'seq'), may hold values from -0.1875 to 0.1875
Outputs:
- hidden_out: bfloat16 [4096, 5120], P('seq', 'tp')
- k_cache: bfloat16 [4096, 4096], P('seq', 'tp')
- v_cache: bfloat16 [4096, 4096], P('seq', 'tp')
The draws below stay inside these ranges and needn't reach their ends.
Inputs may be any that keep to these rules, and one draw needn't show every extreme that they name: `seg_ids`: segment ids never fall along the stream; each segment holds 1 to 2176 tokens, and one holds exactly 2176.
All inputs are finite; a program needn't handle non-finite values.
Results may differ from the reference program's by a relative error of at most 0.018.
Values may be sent and summed in bfloat16 or wider, within the bound.
No kernel may reach another device: no remote copies, remote signals or barrier semaphores. Data moves between devices by JAX's collectives and lax.ppermute only.
A program may use at most 64 MiB of HBM per device.

```python
import math
import jax
import jax.numpy as jnp
import numpy as np
from jax import lax

D = 5120
HEADS = 32
HEAD_DIM = 128
SEGS = 4
TOKENS = 4096
HD = 4096
SEG_MAX = 2176
N_TP = 32


def draw_hidden_in(key, part):
    first_key = jax.random.fold_in(key, 0)
    third_key = jax.random.fold_in(key, 2)
    column = jnp.arange(D, dtype=jnp.float32) / D
    token_place = jnp.arange(TOKENS, dtype=jnp.float32) / TOKENS
    wave = jnp.cos(2.0 * math.pi * token_place)
    direction = jax.random.normal(third_key, (D,), jnp.float32)
    common = 2.0 * wave[:, None] * direction[None, :]
    base = jax.random.normal(first_key, (TOKENS, D), jnp.float32)
    values = base * jnp.exp(math.log(3.0) * column)[None, :] + common
    return jnp.clip(values, -16.0, 16.0).astype(jnp.bfloat16)


def draw_w_qkv(key, part):
    first_key = jax.random.fold_in(key, 0)
    head_place = (jnp.arange(HEADS * HEAD_DIM) // HEAD_DIM).astype(jnp.float32) / HEADS
    head_scale = jnp.exp(math.log(3.0) * head_place)
    base = jax.random.normal(first_key, (D, 3, HEADS * HEAD_DIM), jnp.float32) / math.sqrt(D)
    return (base * head_scale[None, None, :]).astype(jnp.bfloat16)


def gain_values(key):
    return jnp.exp(jax.random.uniform(key, (HEADS * HEAD_DIM,), jnp.float32, math.log(0.5), math.log(1.5)))


def draw_q_gain(key, part):
    return gain_values(jax.random.fold_in(key, 11))


def draw_k_gain(key, part):
    return gain_values(jax.random.fold_in(key, 23))


def set_ends(result, own_key, least, high):
    dims = result.shape
    place = [jax.random.randint(jax.random.fold_in(own_key, axis), (), 0, dims[axis]) for axis in range(len(dims))]
    result = result.at[tuple(place)].set(least)
    longest = dims.index(max(dims))
    place[longest] = (place[longest] + 1) % dims[longest]
    return result.at[tuple(place)].set(high)


def with_spikes(result, key, source, target, shards_of, factor):
    owner, partner = [(jnp.arange(result.shape[position]) // (result.shape[position] // shards_of)).reshape([-1 if axis == position else 1 for axis in range(result.ndim)]) for position in (source, target)]
    chosen = jax.random.permutation(key, shards_of)[partner]
    strong = (owner == chosen) | (owner == (partner + shards_of // 2) % shards_of)
    return jnp.where(strong, factor * result, result)


def block_scale(stream_key, dims, cuts, low, top_value):
    def one(axis_at, shards_of):
        steps = jax.random.uniform(jax.random.fold_in(jax.random.fold_in(stream_key, 6), axis_at), (shards_of,), jnp.float32, low / len(cuts), top_value / len(cuts))
        return jnp.repeat(jnp.exp(steps), dims[axis_at] // shards_of).reshape((-1,) + (1,) * (len(dims) - axis_at - 1))

    loudness = one(*cuts[0])
    for cut in cuts[1:]:
        loudness = loudness * one(*cut)
    return loudness


def split_up(count, total, bound, slope):
    weights = [(1 << 20) // math.isqrt(rank ** slope) + 1 for rank in range(2, count + 1)]
    spare, holding = total - bound - (count - 1), [1] * (count - 1)
    while spare > 0:
        movable = [i for i in range(count - 1) if holding[i] < bound]
        whole, left = sum([weights[i] for i in movable]), spare
        for i in movable:
            addition = min(bound - holding[i], max(1, left * weights[i] // whole), spare)
            holding[i] = holding[i] + addition
            spare = spare - addition
    return np.array([bound] + holding)


def uneven_parts(stream_key, count, total, most, lean):
    if count == 2:
        one = jax.random.randint(stream_key, (), max(1, total - most), min(most, total - 1) + 1)
        return jnp.stack([one, total - one])
    sizes = jnp.asarray(split_up(count, total, most, lean), jnp.int32)
    pairs = (count - 1) // 2
    source_of, sink = sizes[1:1 + 2 * pairs:2], sizes[2:2 + 2 * pairs:2]
    room = jnp.minimum(source_of - 1, most - sink)
    passed = jax.random.randint(jax.random.fold_in(stream_key, 1), (pairs,), 0, 1 << 20) % (room + 1)
    sizes = sizes.at[1:1 + 2 * pairs:2].set(source_of - passed).at[2:2 + 2 * pairs:2].set(sink + passed)
    return sizes[jax.random.permutation(jax.random.fold_in(stream_key, 2), count)]


def gaussian(stream_key, shape, deviation, most, cuts=(), kind=jnp.bfloat16):
    factor_of = block_scale(stream_key, shape, cuts, -0.22, 0.18) if cuts else 1.0
    values = jax.random.normal(stream_key, shape, jnp.float32) * deviation * factor_of
    return jnp.minimum(jnp.maximum(values, -most), most).astype(kind)


def noise_with(stream_key, dims, width, limit, cuts, heavy, held_as=jnp.bfloat16):
    values = width * jax.random.normal(stream_key, dims, jnp.float32)
    if cuts:
        values = values * block_scale(stream_key, dims, cuts, -0.22, 0.18)
    return jnp.clip(with_spikes(values, jax.random.fold_in(stream_key, 3), *heavy), -limit, limit).astype(held_as)


def setup_inputs(seed: int = 0) -> dict:
    key_of = jax.random.split(jax.random.key(seed), 9)
    return {
        "hidden_in": draw_hidden_in(jax.random.fold_in(key_of[8], 71), 0),
        "seg_ids": jnp.searchsorted(jnp.cumsum(uneven_parts(key_of[1], SEGS, TOKENS, SEG_MAX, 2)), jnp.arange(TOKENS), side="right").astype(jnp.int32),
        "positions": set_ends(jax.random.randint(key_of[2], (3, TOKENS), 0, 64), jax.random.fold_in(key_of[2], 1), 0, 63).astype(jnp.int32),
        "mod_table": gaussian(key_of[3], (SEGS, 3, D), 0.8, 4.0, ((2, 32),), jnp.float32),
        "w_qkv": draw_w_qkv(jax.random.fold_in(key_of[8], 71), 0),
        "q_gain": draw_q_gain(jax.random.fold_in(key_of[8], 71), 0),
        "k_gain": draw_k_gain(jax.random.fold_in(key_of[8], 71), 0),
        "w_out": noise_with(key_of[7], (HD, D), HD ** -0.5, 0.1875, ((0, 32), (1, 16)), (0, 1, 32, 2.75)),
    }


EPSILON = 1e-06
NEG_FILL = -1e+30

def rope_tables(positions):
    part_width = HEAD_DIM // 6
    widths = (HEAD_DIM - 4 * part_width, 2 * part_width, 2 * part_width)
    angle_list = []
    for axis_number in range(3):
        exponent = jnp.arange(0, widths[axis_number], 2, dtype=jnp.float32) / widths[axis_number]
        frequency = 1.0 / 10000.0 ** exponent
        angle_list.append(positions[axis_number].astype(jnp.float32)[:, None] * frequency[None, :])
    angle_all = jnp.concatenate(angle_list, axis=1)
    return (jnp.cos(angle_all), jnp.sin(angle_all))

def rotate_pairs(field, cosine, sine):
    even_part = field[..., 0::2]
    odd_part = field[..., 1::2]
    cos_wide = cosine[:, None, :]
    sin_wide = sine[:, None, :]
    new_even = even_part * cos_wide - odd_part * sin_wide
    new_odd = even_part * sin_wide + odd_part * cos_wide
    return jnp.stack([new_even, new_odd], axis=-1).reshape(field.shape)

def reference(hidden_in, seg_ids, positions, mod_table, w_qkv, q_gain, k_gain, w_out):
    token_count = hidden_in.shape[0]
    heads_width = HEADS * HEAD_DIM
    score_scale = 1.0 / math.sqrt(HEAD_DIM)
    x_float = hidden_in.astype(jnp.float32)
    row_sums = lax.optimization_barrier(jnp.sum(x_float, axis=1))
    row_squares = lax.optimization_barrier(jnp.sum(x_float * x_float, axis=1))
    mean_value = row_sums / D
    variance = row_squares / D - mean_value * mean_value
    normed = (x_float - mean_value[:, None]) * lax.rsqrt(variance[:, None] + EPSILON)
    modulation = mod_table[seg_ids]
    shift_mod = modulation[:, 0]
    scale_mod = modulation[:, 1]
    gate_mod = modulation[:, 2]
    modded = (normed * (1.0 + scale_mod) + shift_mod).astype(jnp.bfloat16)
    projected = jnp.dot(modded, w_qkv.reshape(D, 3 * heads_width), preferred_element_type=jnp.float32)
    query_f = projected[:, :heads_width]
    key_f = projected[:, heads_width:2 * heads_width]
    value_f = projected[:, 2 * heads_width:]
    query_n = query_f * lax.rsqrt(lax.optimization_barrier(jnp.mean(query_f * query_f, axis=1, keepdims=True)) + EPSILON) * q_gain[None, :]
    key_n = key_f * lax.rsqrt(lax.optimization_barrier(jnp.mean(key_f * key_f, axis=1, keepdims=True)) + EPSILON) * k_gain[None, :]
    cosine, sine = rope_tables(positions)
    q_rot = rotate_pairs(query_n.reshape(token_count, HEADS, HEAD_DIM), cosine, sine).astype(jnp.bfloat16)
    k_rot = rotate_pairs(key_n.reshape(token_count, HEADS, HEAD_DIM), cosine, sine).astype(jnp.bfloat16)
    v_cache = value_f.astype(jnp.bfloat16)
    v_heads = v_cache.reshape(token_count, HEADS, HEAD_DIM)
    same_seg = seg_ids[:, None] == seg_ids[None, :]

    def one_head(operands):
        q_head, k_head, v_head = operands
        scores = jnp.dot(q_head, k_head.T, preferred_element_type=jnp.float32) * score_scale
        masked = jnp.where(same_seg, scores, NEG_FILL)
        row_max = lax.optimization_barrier(jnp.max(masked, axis=1, keepdims=True))
        weights = jnp.where(same_seg, jnp.exp(masked - row_max), 0.0)
        denominator = lax.optimization_barrier(jnp.sum(weights, axis=1, keepdims=True))
        numerator = jnp.dot(weights.astype(jnp.bfloat16), v_head, preferred_element_type=jnp.float32)
        return numerator / denominator
    attended = lax.map(one_head, (q_rot.transpose(1, 0, 2), k_rot.transpose(1, 0, 2), v_heads.transpose(1, 0, 2)))
    attn_out = attended.transpose(1, 0, 2).reshape(token_count, heads_width).astype(jnp.bfloat16)
    per_device = heads_width // N_TP
    attn_blocks = attn_out.reshape(token_count, N_TP, per_device).transpose(1, 0, 2)
    out_blocks = w_out.reshape(N_TP, per_device, D)

    def add_partial(carry, operands):
        attn_part, weight_part = operands
        term = jnp.dot(attn_part, weight_part, preferred_element_type=jnp.float32).astype(jnp.bfloat16)
        term = lax.optimization_barrier(term)
        return (carry + term.astype(jnp.float32), None)
    mixed = lax.scan(add_partial, jnp.zeros((token_count, D), jnp.float32), (attn_blocks, out_blocks))[0]
    hidden_out = (x_float + gate_mod * mixed).astype(jnp.bfloat16)
    return (hidden_out, k_rot.reshape(token_count, heads_width), v_cache)
```

```python
import functools
import itertools
import math

import jax
import jax.numpy as jnp
import numpy as np
from jax import lax
from jax.experimental import pallas as pl
from jax.experimental.pallas import tpu as pltpu
from jax.sharding import Mesh
from jax.sharding import PartitionSpec as P

HEAD_DIM = 128
EPSILON = 1e-06
NEG_FILL = -1e30
LOG2E = 1.4426950408889634

SEQ = ("ya", "yb", "yc", "zh")
TP = ("zl", "xh", "xl", "c")
SIZES = {"ya": 2, "yb": 2, "yc": 2, "zh": 2, "zl": 4, "xh": 2, "xl": 2, "c": 2}

F32 = jnp.float32
BF16 = jnp.bfloat16
VMEM_LIMIT = 48 << 20


def permute(value, axes, move):
    sizes = [SIZES[a] for a in axes]
    pairs = []
    for at in itertools.product(*[range(n) for n in sizes]):
        to = move(*at)
        pairs.append((int(np.ravel_multi_index(at, sizes)), int(np.ravel_multi_index(to, sizes))))
    return lax.ppermute(value, axes, pairs)


def contract_first(lhs, rhs):
    return lax.dot_general(lhs, rhs, (((0,), (0,)), ((), ())), preferred_element_type=F32)


def call(kernel, out_shape, operands, scalars=None, scratch=(), name=None, cost=None):
    vmem = pl.BlockSpec(memory_space=pltpu.VMEM)
    smem = pl.BlockSpec(memory_space=pltpu.SMEM)
    specs = ([] if scalars is None else [smem]) + [vmem] * len(operands)
    args = ([] if scalars is None else [scalars]) + list(operands)
    return pl.pallas_call(
        kernel,
        out_shape=out_shape,
        in_specs=specs,
        out_specs=jax.tree.map(lambda _: vmem, out_shape),
        scratch_shapes=list(scratch),
        compiler_params=pltpu.CompilerParams(vmem_limit_bytes=VMEM_LIMIT),
        cost_estimate=cost,
        name=name,
    )(*args)


def shaped(shape, dtype):
    return jax.ShapeDtypeStruct(shape, dtype)


def project_kernel(at, *refs):
    xs, w, mine_q, mine_kv, message, meta, acc = refs[:8], refs[8], *refs[9:]
    zl, x, c, zh = at[0], at[1], at[2], at[3]
    acc[...] = jnp.zeros_like(acc)
    first = lax.rem(x, 2)
    for i in range(2):
        core = lax.rem(c + i, 2)
        for j in range(2):
            high = lax.rem(x // 2 + j, 2)
            left, right = xs[4 * i + 2 * j], xs[4 * i + 2 * j + 1]
            total = None
            for k in range(4):
                z_from = lax.rem(zl - k + 4, 4)
                both = jnp.concatenate([left[k, :160, :], right[k, :160, :]], axis=1)
                block = z_from * 2 + high
                weights = jnp.concatenate([w[block, p, core] for p in range(3)], axis=1)
                term = contract_first(weights, both)
                total = term if total is None else total + term
            acc[first] += total[:, :256]
            acc[1 - first] += total[:, 256:]
            if i == 0 and j == 0:
                meta[first] = left[0, 160:168, :].astype(F32)
                meta[1 - first] = right[0, 160:168, :].astype(F32)
    for block in range(2):
        part = acc[block]
        mine_q[block] = part[:128]
        message[block] = part[:128].astype(BF16)
    own = acc[zh]
    mine_kv[0] = own[128:256]
    mine_kv[1] = own[256:]
    other = acc[1 - zh]
    message[2] = other[128:256].astype(BF16)
    message[3] = other[256:].astype(BF16)


def square_kernel(mine_q, mine_kv, got, full_q, full_kv, stats):
    for block in range(2):
        full_q[block] = mine_q[block] + got[block].astype(F32)
        full_kv[block] = mine_kv[block] + got[2 + block].astype(F32)
    rows = []
    for value in (full_q[0], full_q[1], full_kv[0]):
        row = jnp.sum(value * value, axis=0, keepdims=True)
        rows += [row[:, :128], row[:, 128:]]
    rows += [jnp.zeros((2, 128), F32)]
    packed = jnp.concatenate(rows, axis=0)
    for t in range(stats.shape[0]):
        stats[t] = packed


def rotate_kernel(width, got, full_q, full_kv, cosine, sine, qg, kg, meta, at, q_out, k_cache, v_cache, message):
    totals = jnp.sum(got[...], axis=0)
    zh = at[0]
    even = lax.rem(lax.broadcasted_iota(jnp.int32, (HEAD_DIM, 256), 0), 2) == 0

    def rotated(value, gain, row, cos, sin):
        factor = jnp.concatenate([totals[row : row + 1], totals[row + 1 : row + 2]], axis=1)
        factor = lax.rsqrt(factor / width + EPSILON)
        normed = value * factor * gain
        after = pltpu.roll(normed, HEAD_DIM - 1, 0)
        before = pltpu.roll(normed, 1, 0)
        partner = jnp.where(even, -after, before)
        return normed * cos + partner * sin

    for block in range(2):
        q_out[:, 256 * block : 256 * block + 256] = rotated(
            full_q[block], qg[...], 2 * block, cosine[block], sine[block]
        ).astype(BF16)
    k_rot = rotated(full_kv[0], kg[...], 4, cosine[zh], sine[zh])
    value = full_kv[1]
    k_cache[...] = k_rot.T.astype(BF16)
    v_cache[...] = value.T.astype(BF16)
    k_low = k_rot.astype(BF16)
    v_low = value.astype(BF16)
    extra = jnp.concatenate([meta[zh], jnp.zeros((8, 256), F32)], axis=0).astype(BF16)
    for t in range(message.shape[0]):
        message[t, :128] = k_low
        message[t, 128:256] = v_low
        message[t, 256:272] = extra


def attend_kernel(at, q, meta, keys, mine, mine_lse, message, held):
    zh = at[0]
    count = keys.shape[0]
    scale = LOG2E / math.sqrt(HEAD_DIM)
    q_low = q[...]
    seg_q = jnp.concatenate([meta[0, 3:4], meta[1, 3:4]], axis=1)
    top = None
    for b in range(count):
        seg_k = keys[b, 256:272].astype(F32).T[:, 3:4]
        scores = contract_first(keys[b, :128], q_low) * scale
        scores = jnp.where(seg_k == seg_q, scores, NEG_FILL)
        held[b] = scores
        here = jnp.max(scores, axis=0, keepdims=True)
        top = here if top is None else jnp.maximum(top, here)
    top = jnp.maximum(top, -1e20)
    total = jnp.zeros((1, 512), F32)
    weighted = jnp.zeros((HEAD_DIM, 512), F32)
    for b in range(count):
        weights = jnp.exp2(held[b] - top)
        total = total + jnp.sum(weights, axis=0, keepdims=True)
        weighted = weighted + jnp.dot(
            keys[b, 128:256], weights.astype(BF16), preferred_element_type=F32
        )
    some = total > 0.0
    safe = jnp.where(some, total, 1.0)
    out = weighted / safe
    lse = jnp.where(some, top + jnp.log2(safe), NEG_FILL)
    first = zh == 0
    own = jnp.where(first, out[:, :256], out[:, 256:])
    other = jnp.where(first, out[:, 256:], out[:, :256])
    own_lse = jnp.where(first, lse[:, :256], lse[:, 256:])
    other_lse = jnp.where(first, lse[:, 256:], lse[:, :256])
    mine[...] = own
    mine_lse[...] = jnp.broadcast_to(own_lse, (8, 256))
    high = other_lse.astype(BF16)
    rest = other_lse - high.astype(F32)
    middle = rest.astype(BF16)
    low = (rest - middle.astype(F32)).astype(BF16)
    message[:128] = other.astype(BF16)
    message[128:144] = jnp.concatenate(
        [high.astype(F32), middle.astype(F32), low.astype(F32), jnp.zeros((13, 256), F32)], axis=0
    ).astype(BF16)


def merge_kernel(mine, mine_lse, got, out):
    rows = got[128:144].astype(F32)
    other_lse = rows[0:1] + rows[1:2] + rows[2:3]
    own_lse = mine_lse[0:1]
    top = jnp.maximum(own_lse, other_lse)
    own_weight = jnp.exp2(own_lse - top)
    other_weight = jnp.exp2(other_lse - top)
    both = own_weight + other_weight
    out[...] = (
        mine[...] * (own_weight / both) + got[:128].astype(F32) * (other_weight / both)
    ).astype(BF16)


def output_kernel(at, *refs):
    heads, w, mine, message, held = refs[:4], refs[4], *refs[5:]
    zl, x, c, zh = at[0], at[1], at[2], at[3]
    total = None
    for j in range(4):
        x_from = lax.rem(x // 2 + j // 2, 2) * 2 + lax.rem(x + j, 2)
        for k in range(4):
            chip = lax.rem(zl - k + 4, 4) * 4 + x_from
            flip = lax.rem(lax.rem(chip, 2) + zh, 2)
            term = jnp.dot(w[chip // 2, flip], heads[j][k], preferred_element_type=F32)
            total = term if total is None else total + term
    held[0] = total[:160]
    held[1] = total[160:]
    mine[...] = held[c]
    message[...] = held[1 - c]


def body(hidden_in, seg_ids, positions, mod_table, w_qkv, q_gain, k_gain, w_out):
    tok_rows, feat_local = hidden_in.shape
    model_width = feat_local * 32
    heads_width = 4096
    zl, c = lax.axis_index("zl"), lax.axis_index("c")
    zh = lax.axis_index("zh")
    x = lax.axis_index("xh") * 2 + lax.axis_index("xl")
    at = jnp.stack([zl, x, c, zh]).astype(jnp.int32)
    at_zh = jnp.stack([zh]).astype(jnp.int32)

    w_local = jnp.transpose(w_qkv, (1, 0, 2))
    w_all = lax.all_gather(w_local, ("ya", "yb", "yc"), axis=0, tiled=False)
    w_all = w_all.reshape(8, 3, 2, 160, 128)

    axes = SEQ + TP

    def turned(flip):
        def move(ya, yb, yc, zh, zl, xh, xl, c):
            s = (ya * 4 + yb * 2 + yc) * 2 + zh
            chip = (zl * 2 + xh) * 2 + xl
            to_s = chip ^ flip
            return (to_s >> 3, (to_s >> 2) & 1, (to_s >> 1) & 1, to_s & 1, s >> 2, (s >> 1) & 1, s & 1, c)

        return permute(w_out.T, axes, move)

    wo_pair = jnp.stack([turned(0), turned(1)])
    wo_all = lax.all_gather(wo_pair, ("ya", "yb", "yc"), axis=0, tiled=False)

    x_t = hidden_in.T.astype(F32)
    sums = jnp.stack([jnp.sum(x_t, axis=0), jnp.sum(x_t * x_t, axis=0)]).reshape(4, 128)
    sums = jnp.concatenate([sums, jnp.zeros((4, 128), F32)], axis=0)
    sums = lax.all_to_all(jnp.broadcast_to(sums, (32, 8, 128)), TP, 0, 0, tiled=True)
    sums = jnp.sum(sums, axis=0)[:4].reshape(2, tok_rows)
    mean_value = sums[0:1] / model_width
    variance = sums[1:2] / model_width - mean_value * mean_value
    normed = (x_t - mean_value) * lax.rsqrt(variance + EPSILON)
    segment_count = mod_table.shape[0]
    onehot = (seg_ids[None, :] == jnp.arange(segment_count, dtype=jnp.int32)[:, None]).astype(F32)
    modulation = lax.dot_general(
        mod_table.reshape(segment_count, 3 * feat_local),
        onehot,
        (((0,), (0,)), ((), ())),
        precision=lax.Precision.HIGHEST,
    ).reshape(3, feat_local, tok_rows)
    modded = (normed * (1.0 + modulation[1]) + modulation[0]).astype(BF16)
    marks = jnp.concatenate([positions, seg_ids[None, :], jnp.zeros((4, tok_rows), jnp.int32)], axis=0)
    packet = jnp.concatenate([modded, marks.astype(BF16)], axis=0)

    slots = [
        permute(
            packet,
            ("zh", "zl", "xh", "xl"),
            lambda zh, zl, xh, xl, k=k: (xl, (zl + k) % 4, xh, zh),
        )
        for k in range(4)
    ]
    held = jnp.stack(slots)
    along_x = [held] + [
        permute(held, ("xh", "xl"), lambda xh, xl, j=j: (xh ^ (j >> 1), xl ^ (j & 1)))
        for j in range(1, 4)
    ]
    swapped = [permute(part, ("c",), lambda c: (1 - c,)) for part in along_x]

    mine_q, mine_kv, message, meta = call(
        project_kernel,
        (
            shaped((2, 128, 256), F32),
            shaped((2, 128, 256), F32),
            shaped((4, 128, 256), BF16),
            shaped((2, 8, 256), F32),
        ),
        along_x + swapped + [w_all],
        scalars=at,
        scratch=[pltpu.VMEM((2, 384, 256), F32)],
        name="project",
        cost=pl.CostEstimate(flops=2 * 512 * 2560 * 384, bytes_accessed=5 << 20, transcendentals=0),
    )
    got = permute(message, ("zh",), lambda zh: (1 - zh,))

    part_width = HEAD_DIM // 6
    widths = (HEAD_DIM - 4 * part_width, 2 * part_width, 2 * part_width)
    angles = []
    for axis_number in range(3):
        width = widths[axis_number]
        exponent = jnp.arange(0, width, 2, dtype=F32) / width
        frequency = jnp.repeat(1.0 / 10000.0**exponent, 2)
        angles.append(meta[:, axis_number][:, None, :] * frequency[None, :, None])
    angle = jnp.concatenate(angles, axis=1)
    cosine, sine = jnp.cos(angle), jnp.sin(angle)

    full_q, full_kv, stats = call(
        square_kernel,
        (shaped((2, 128, 256), F32), shaped((2, 128, 256), F32), shaped((32, 8, 128), F32)),
        [mine_q, mine_kv, got],
        name="square",
    )
    stats = lax.all_to_all(stats, TP, 0, 0, tiled=True)
    q_rot, k_cache, v_cache, kv_message = call(
        lambda at, *refs: rotate_kernel(heads_width, *refs[:8], at, *refs[8:]),
        (
            shaped((128, 512), BF16),
            shaped((256, 128), BF16),
            shaped((256, 128), BF16),
            shaped((8, 272, 256), BF16),
        ),
        [stats, full_q, full_kv, cosine, sine, q_gain.reshape(128, 1), k_gain.reshape(128, 1), meta],
        scalars=at_zh,
        name="rotate",
    )
    keys = lax.all_to_all(kv_message, ("ya", "yb", "yc"), 0, 0, tiled=True)
    mine, mine_lse, o_message = call(
        attend_kernel,
        (shaped((128, 256), F32), shaped((8, 256), F32), shaped((144, 256), BF16)),
        [q_rot, meta, keys],
        scalars=at_zh,
        scratch=[pltpu.VMEM((8, 256, 512), F32)],
        name="attend",
    )
    o_got = permute(o_message, ("zh",), lambda zh: (1 - zh,))
    attention = call(merge_kernel, shaped((128, 256), BF16), [mine, mine_lse, o_got], name="merge")

    by_z = [attention] + [
        permute(attention, ("zl",), lambda zl, k=k: ((zl + k) % 4,)) for k in range(1, 4)
    ]
    by_z = jnp.stack(by_z)
    by_x = [by_z] + [
        permute(by_z, ("xh", "xl"), lambda xh, xl, j=j: (xh ^ (j >> 1), xl ^ (j & 1)))
        for j in range(1, 4)
    ]
    out_mine, out_message = call(
        output_kernel,
        (shaped((160, 256), F32), shaped((160, 256), F32)),
        by_x + [wo_all],
        scalars=at,
        scratch=[pltpu.VMEM((2, 160, 256), F32)],
        name="output",
    )
    out_got = permute(out_message, ("c",), lambda c: (1 - c,))
    mixed = out_mine + out_got
    hidden_out = (x_t + modulation[2] * mixed).T.astype(BF16)
    return (hidden_out, k_cache, v_cache)


def solution(mesh):
    split = Mesh(mesh.devices.reshape(tuple(SIZES.values())), tuple(SIZES))
    in_specs = (
        P(SEQ, TP),
        P(SEQ),
        P(None, SEQ),
        P(None, None, TP),
        P(SEQ, None, TP),
        P(TP),
        P(TP),
        P(TP, SEQ),
    )
    out_specs = (P(SEQ, TP), P(SEQ, TP), P(SEQ, TP))
    return jax.shard_map(body, mesh=split, in_specs=in_specs, out_specs=out_specs, check_vma=False)
```

```python
import functools
import itertools
import math

import jax
import jax.numpy as jnp
import numpy as np
from jax import lax
from jax.experimental import pallas as pl
from jax.experimental.pallas import tpu as pltpu
from jax.sharding import Mesh
from jax.sharding import PartitionSpec as P

HEAD_DIM = 128
EPSILON = 1e-06
NEG_FILL = -1e30
LOG2E = 1.4426950408889634

SEQ = ("ya", "yb", "yc", "zh")
TP = ("zl", "xh", "xl", "c")
SIZES = {"ya": 2, "yb": 2, "yc": 2, "zh": 2, "zl": 4, "xh": 2, "xl": 2, "c": 2}

F32 = jnp.float32
BF16 = jnp.bfloat16
VMEM_LIMIT = 48 << 20


def permute(value, axes, move):
    sizes = [SIZES[a] for a in axes]
    pairs = []
    for at in itertools.product(*[range(n) for n in sizes]):
        to = move(*at)
        pairs.append((int(np.ravel_multi_index(at, sizes)), int(np.ravel_multi_index(to, sizes))))
    return lax.ppermute(value, axes, pairs)


def contract_first(lhs, rhs):
    return lax.dot_general(lhs, rhs, (((0,), (0,)), ((), ())), preferred_element_type=F32)


def call(kernel, out_shape, operands, scalars=None, scratch=(), name=None, cost=None):
    vmem = pl.BlockSpec(memory_space=pltpu.VMEM)
    smem = pl.BlockSpec(memory_space=pltpu.SMEM)
    specs = ([] if scalars is None else [smem]) + [vmem] * len(operands)
    args = ([] if scalars is None else [scalars]) + list(operands)
    return pl.pallas_call(
        kernel,
        out_shape=out_shape,
        in_specs=specs,
        out_specs=jax.tree.map(lambda _: vmem, out_shape),
        scratch_shapes=list(scratch),
        compiler_params=pltpu.CompilerParams(vmem_limit_bytes=VMEM_LIMIT),
        cost_estimate=cost,
        name=name,
    )(*args)


def shaped(shape, dtype):
    return jax.ShapeDtypeStruct(shape, dtype)


def project_kernel(at, *refs):
    xs, w, mine_q, mine_kv, message, meta, acc = refs[:8], refs[8], *refs[9:]
    zl, x, c, yc = at[0], at[1], at[2], at[3]
    acc[...] = jnp.zeros_like(acc)
    for i in range(2):
        core = lax.rem(c + i, 2)
        for j in range(2):
            x_first = lax.rem(x - j + 4, 4)
            first = x_first // 2
            low = lax.rem(x_first, 2)
            left, right = xs[4 * i + j], xs[4 * i + j + 2]
            total = None
            for k in range(4):
                z_from = lax.rem(zl - k + 4, 4)
                both = jnp.concatenate([left[k, :160, :], right[k, :160, :]], axis=1)
                block = z_from * 2 + low
                weights = jnp.concatenate([w[block, p, core] for p in range(3)], axis=1)
                term = contract_first(weights, both)
                total = term if total is None else total + term
            acc[first] += total[:, :256]
            acc[1 - first] += total[:, 256:]
            if i == 0 and j == 0:
                meta[first] = left[0, 160:168, :].astype(F32)
                meta[1 - first] = right[0, 160:168, :].astype(F32)
    for block in range(2):
        part = acc[block]
        mine_q[block] = part[:128]
        message[block] = part[:128].astype(BF16)
    own = acc[yc]
    mine_kv[0] = own[128:256]
    mine_kv[1] = own[256:]
    other = acc[1 - yc]
    message[2] = other[128:256].astype(BF16)
    message[3] = other[256:].astype(BF16)


def square_kernel(mine_q, mine_kv, got, full_q, full_kv, stats):
    for block in range(2):
        full_q[block] = mine_q[block] + got[block].astype(F32)
        full_kv[block] = mine_kv[block] + got[2 + block].astype(F32)
    rows = []
    for value in (full_q[0], full_q[1], full_kv[0]):
        row = jnp.sum(value * value, axis=0, keepdims=True)
        rows += [row[:, :128], row[:, 128:]]
    rows += [jnp.zeros((2, 128), F32)]
    packed = jnp.concatenate(rows, axis=0)
    for t in range(stats.shape[0]):
        stats[t] = packed


def rotate_kernel(width, got, full_q, full_kv, cosine, sine, qg, kg, meta, at, q_out, k_cache, v_cache, message):
    totals = jnp.sum(got[...], axis=0)
    yc = at[0]
    even = lax.rem(lax.broadcasted_iota(jnp.int32, (HEAD_DIM, 256), 0), 2) == 0

    def rotated(value, gain, row, cos, sin):
        factor = jnp.concatenate([totals[row : row + 1], totals[row + 1 : row + 2]], axis=1)
        factor = lax.rsqrt(factor / width + EPSILON)
        normed = value * factor * gain
        after = pltpu.roll(normed, HEAD_DIM - 1, 0)
        before = pltpu.roll(normed, 1, 0)
        partner = jnp.where(even, -after, before)
        return normed * cos + partner * sin

    for block in range(2):
        here = pl.ds(256 * block, 256)
        q_out[128:144, here] = jnp.concatenate([meta[block], jnp.zeros((8, 256), F32)], axis=0).astype(BF16)
        q_out[:128, here] = rotated(
            full_q[block], qg[...], 2 * block, cosine[block], sine[block]
        ).astype(BF16)
    k_rot = rotated(full_kv[0], kg[...], 4, cosine[yc], sine[yc])
    value = full_kv[1]
    k_cache[...] = k_rot.T.astype(BF16)
    v_cache[...] = value.T.astype(BF16)
    k_low = k_rot.astype(BF16)
    v_low = value.astype(BF16)
    extra = jnp.concatenate([meta[yc], jnp.zeros((8, 256), F32)], axis=0).astype(BF16)
    for t in range(message.shape[0]):
        message[t, :128] = k_low
        message[t, 128:256] = v_low
        message[t, 256:272] = extra


def attend_kernel(at, q, q_got, keys, mine, mine_lse, m1, m2, m3, held):
    messages = (m1, m2, m3)
    yc = at[0]
    count = keys.shape[0]
    scale = LOG2E / math.sqrt(HEAD_DIM)
    q_low = jnp.concatenate([q[:128], q_got[:128]], axis=1)
    seg_q = jnp.concatenate([q[128:144], q_got[128:144]], axis=1).astype(F32)[3:4]
    top = None
    for b in range(count):
        seg_k = keys[b, 256:272].astype(F32).T[:, 3:4]
        scores = contract_first(keys[b, :128], q_low) * scale
        scores = jnp.where(seg_k == seg_q, scores, NEG_FILL)
        held[b] = scores
        here = jnp.max(scores, axis=0, keepdims=True)
        top = here if top is None else jnp.maximum(top, here)
    top = jnp.maximum(top, -1e20)
    total = jnp.zeros((1, 1024), F32)
    weighted = jnp.zeros((HEAD_DIM, 1024), F32)
    for b in range(count):
        weights = jnp.exp2(held[b] - top)
        total = total + jnp.sum(weights, axis=0, keepdims=True)
        weighted = weighted + jnp.dot(
            keys[b, 128:256], weights.astype(BF16), preferred_element_type=F32
        )
    some = total > 0.0
    safe = jnp.where(some, total, 1.0)
    out = weighted / safe
    lse = jnp.where(some, top + jnp.log2(safe), NEG_FILL)
    first = yc == 0
    for pair in range(2):
        a, b = slice(512 * pair, 512 * pair + 256), slice(512 * pair + 256, 512 * pair + 512)
        for swap in range(2):
            keep, give = (a, b) if swap == 0 else (b, a)
            part = jnp.where(first, out[:, keep], out[:, give])
            part_lse = jnp.where(first, lse[:, keep], lse[:, give])
            if pair == 0 and swap == 0:
                mine[...] = part
                mine_lse[...] = jnp.broadcast_to(part_lse, (8, 256))
                continue
            message = messages[2 * pair + swap - 1]
            high = part_lse.astype(BF16)
            rest = part_lse - high.astype(F32)
            middle = rest.astype(BF16)
            low = (rest - middle.astype(F32)).astype(BF16)
            message[:128] = part.astype(BF16)
            message[128:144] = jnp.concatenate(
                [high.astype(F32), middle.astype(F32), low.astype(F32), jnp.zeros((13, 256), F32)],
                axis=0,
            ).astype(BF16)


def merge_kernel(mine, mine_lse, *refs):
    gots, out = refs[:-1], refs[-1]
    parts = [(mine_lse[0:1], mine[...])]
    for got in gots:
        rows = got[128:144].astype(F32)
        parts.append((rows[0:1] + rows[1:2] + rows[2:3], got[:128].astype(F32)))
    top = functools.reduce(jnp.maximum, [lse for lse, _ in parts])
    weights = [jnp.exp2(lse - top) for lse, _ in parts]
    total = sum(weights[1:], weights[0])
    value = None
    for weight, (_, part) in zip(weights, parts, strict=True):
        term = part * (weight / total)
        value = term if value is None else value + term
    out[...] = value.astype(BF16)


def output_kernel(at, *refs):
    heads, w, mine, message, held = refs[:4], refs[4], *refs[5:]
    zl, x, c, zh = at[0], at[1], at[2], at[4]
    total = None
    for j in range(4):
        x_from = lax.rem(x - j + 4, 4)
        for k in range(4):
            chip = lax.rem(zl - k + 4, 4) * 4 + x_from
            flip = lax.rem(lax.rem(chip, 2) + zh, 2)
            term = jnp.dot(w[chip // 2, flip], heads[j][k], preferred_element_type=F32)
            total = term if total is None else total + term
    held[0] = total[:160]
    held[1] = total[160:]
    mine[...] = held[c]
    message[...] = held[1 - c]


def body(hidden_in, seg_ids, positions, mod_table, w_qkv, q_gain, k_gain, w_out):
    tok_rows, feat_local = hidden_in.shape
    model_width = feat_local * 32
    heads_width = 4096
    zl, c = lax.axis_index("zl"), lax.axis_index("c")
    yc, zh = lax.axis_index("yc"), lax.axis_index("zh")
    x = lax.axis_index("xh") * 2 + lax.axis_index("xl")
    at = jnp.stack([zl, x, c, yc, zh]).astype(jnp.int32)
    at_yc = jnp.stack([yc]).astype(jnp.int32)

    w_local = jnp.transpose(w_qkv, (1, 0, 2))
    w_all = lax.all_to_all(
        jnp.broadcast_to(w_local, (8,) + w_local.shape), ("ya", "yb", "zh"), 0, 0, tiled=True
    )
    w_all = w_all.reshape(8, 3, 2, 160, 128)

    axes = SEQ + TP

    def turned(flip):
        def move(ya, yb, yc, zh, zl, xh, xl, c):
            s = (ya * 4 + yb * 2 + yc) * 2 + zh
            chip = (zl * 2 + xh) * 2 + xl
            to_s = chip ^ flip
            return (to_s >> 3, (to_s >> 2) & 1, (to_s >> 1) & 1, to_s & 1, s >> 2, (s >> 1) & 1, s & 1, c)

        return permute(w_out.T, axes, move)

    wo_turned = (turned(0), turned(1))

    x_t = hidden_in.T.astype(F32)
    sums = jnp.stack([jnp.sum(x_t, axis=0), jnp.sum(x_t * x_t, axis=0)]).reshape(4, 128)
    sums = jnp.concatenate([sums, jnp.zeros((4, 128), F32)], axis=0)
    sums = lax.all_to_all(jnp.broadcast_to(sums, (32, 8, 128)), TP, 0, 0, tiled=True)
    sums, wo_turned = lax.optimization_barrier((sums, wo_turned))
    wo_all = lax.all_gather(jnp.stack(wo_turned), ("ya", "yb", "yc"), axis=0, tiled=False)
    sums = jnp.sum(sums, axis=0)[:4].reshape(2, tok_rows)
    mean_value = sums[0:1] / model_width
    variance = sums[1:2] / model_width - mean_value * mean_value
    normed = (x_t - mean_value) * lax.rsqrt(variance + EPSILON)
    segment_count = mod_table.shape[0]
    onehot = (seg_ids[None, :] == jnp.arange(segment_count, dtype=jnp.int32)[:, None]).astype(F32)
    modulation = lax.dot_general(
        mod_table.reshape(segment_count, 3 * feat_local),
        onehot,
        (((0,), (0,)), ((), ())),
        precision=lax.Precision.HIGHEST,
    ).reshape(3, feat_local, tok_rows)
    modded = (normed * (1.0 + modulation[1]) + modulation[0]).astype(BF16)
    marks = jnp.concatenate([positions, seg_ids[None, :], jnp.zeros((4, tok_rows), jnp.int32)], axis=0)
    packet = jnp.concatenate([modded, marks.astype(BF16)], axis=0)

    slots = [
        permute(
            packet,
            ("yc", "zl", "xh", "xl"),
            lambda yc, zl, xh, xl, k=k: (xh, (zl + k) % 4, yc, xl),
        )
        for k in range(4)
    ]
    held = jnp.stack(slots)
    along_x = [held] + [
        permute(held, ("xh", "xl"), lambda xh, xl, j=j: divmod((xh * 2 + xl + j) % 4, 2))
        for j in range(1, 4)
    ]
    swapped = [permute(part, ("c",), lambda c: (1 - c,)) for part in along_x]

    mine_q, mine_kv, message, meta = call(
        project_kernel,
        (
            shaped((2, 128, 256), F32),
            shaped((2, 128, 256), F32),
            shaped((4, 128, 256), BF16),
            shaped((2, 8, 256), F32),
        ),
        along_x + swapped + [w_all],
        scalars=at,
        scratch=[pltpu.VMEM((2, 384, 256), F32)],
        name="project",
        cost=pl.CostEstimate(flops=2 * 512 * 2560 * 384, bytes_accessed=5 << 20, transcendentals=0),
    )
    got = permute(message, ("yc",), lambda yc: (1 - yc,))

    part_width = HEAD_DIM // 6
    widths = (HEAD_DIM - 4 * part_width, 2 * part_width, 2 * part_width)
    angles = []
    for axis_number in range(3):
        width = widths[axis_number]
        exponent = jnp.arange(0, width, 2, dtype=F32) / width
        frequency = jnp.repeat(1.0 / 10000.0**exponent, 2)
        angles.append(meta[:, axis_number][:, None, :] * frequency[None, :, None])
    angle = jnp.concatenate(angles, axis=1)
    cosine, sine = jnp.cos(angle), jnp.sin(angle)

    full_q, full_kv, stats = call(
        square_kernel,
        (shaped((2, 128, 256), F32), shaped((2, 128, 256), F32), shaped((32, 8, 128), F32)),
        [mine_q, mine_kv, got],
        name="square",
    )
    stats = lax.all_to_all(stats, TP, 0, 0, tiled=True)
    q_rot, k_cache, v_cache, kv_message = call(
        lambda at, *refs: rotate_kernel(heads_width, *refs[:8], at, *refs[8:]),
        (
            shaped((144, 512), BF16),
            shaped((256, 128), BF16),
            shaped((256, 128), BF16),
            shaped((4, 272, 256), BF16),
        ),
        [stats, full_q, full_kv, cosine, sine, q_gain.reshape(128, 1), k_gain.reshape(128, 1), meta],
        scalars=at_yc,
        name="rotate",
    )
    q_got = permute(q_rot, ("yb",), lambda yb: (1 - yb,))
    keys = lax.all_to_all(kv_message, ("ya", "zh"), 0, 0, tiled=True)
    mine, mine_lse, *o_messages = call(
        attend_kernel,
        (shaped((128, 256), F32), shaped((8, 256), F32)) + (shaped((144, 256), BF16),) * 3,
        [q_rot, q_got, keys],
        scalars=at_yc,
        scratch=[pltpu.VMEM((4, 256, 1024), F32)],
        name="attend",
    )
    o_got = [
        permute(o, ("yb", "yc"), lambda yb, yc, d=d: (yb ^ (d >> 1), yc ^ (d & 1)))
        for d, o in enumerate(o_messages, 1)
    ]
    attention = call(merge_kernel, shaped((128, 256), BF16), [mine, mine_lse] + o_got, name="merge")

    by_z = [attention] + [
        permute(attention, ("zl",), lambda zl, k=k: ((zl + k) % 4,)) for k in range(1, 4)
    ]
    by_z = jnp.stack(by_z)
    by_x = [by_z] + [
        permute(by_z, ("xh", "xl"), lambda xh, xl, j=j: divmod((xh * 2 + xl + j) % 4, 2))
        for j in range(1, 4)
    ]
    out_mine, out_message = call(
        output_kernel,
        (shaped((160, 256), F32), shaped((160, 256), F32)),
        by_x + [wo_all],
        scalars=at,
        scratch=[pltpu.VMEM((2, 160, 256), F32)],
        name="output",
    )
    out_got = permute(out_message, ("c",), lambda c: (1 - c,))
    mixed = out_mine + out_got
    hidden_out = (x_t + modulation[2] * mixed).T.astype(BF16)
    return (hidden_out, k_cache, v_cache)


def solution(mesh):
    split = Mesh(mesh.devices.reshape(tuple(SIZES.values())), tuple(SIZES))
    in_specs = (
        P(SEQ, TP),
        P(SEQ),
        P(None, SEQ),
        P(None, None, TP),
        P(SEQ, None, TP),
        P(TP),
        P(TP),
        P(TP, SEQ),
    )
    out_specs = (P(SEQ, TP), P(SEQ, TP), P(SEQ, TP))
    return jax.shard_map(body, mesh=split, in_specs=in_specs, out_specs=out_specs, check_vma=False)
```

```python
import functools
import itertools
import math

import jax
import jax.numpy as jnp
import numpy as np
from jax import lax
from jax.experimental import pallas as pl
from jax.experimental.pallas import tpu as pltpu
from jax.sharding import Mesh
from jax.sharding import PartitionSpec as P

HEAD_DIM = 128
EPSILON = 1e-06
NEG_FILL = -1e30
LOG2E = 1.4426950408889634

SEQ = ("ya", "yb", "yc", "zh")
TP = ("zl", "xh", "xl", "c")
SIZES = {"ya": 2, "yb": 2, "yc": 2, "zh": 2, "zl": 4, "xh": 2, "xl": 2, "c": 2}

F32 = jnp.float32
BF16 = jnp.bfloat16
VMEM_LIMIT = 48 << 20


def permute(value, axes, move):
    sizes = [SIZES[a] for a in axes]
    pairs = []
    for at in itertools.product(*[range(n) for n in sizes]):
        to = move(*at)
        pairs.append((int(np.ravel_multi_index(at, sizes)), int(np.ravel_multi_index(to, sizes))))
    return lax.ppermute(value, axes, pairs)


def contract_first(lhs, rhs):
    return lax.dot_general(lhs, rhs, (((0,), (0,)), ((), ())), preferred_element_type=F32)


def call(kernel, out_shape, operands, scalars=None, scratch=(), name=None, cost=None):
    vmem = pl.BlockSpec(memory_space=pltpu.VMEM)
    smem = pl.BlockSpec(memory_space=pltpu.SMEM)
    specs = ([] if scalars is None else [smem]) + [vmem] * len(operands)
    args = ([] if scalars is None else [scalars]) + list(operands)
    return pl.pallas_call(
        kernel,
        out_shape=out_shape,
        in_specs=specs,
        out_specs=jax.tree.map(lambda _: vmem, out_shape),
        scratch_shapes=list(scratch),
        compiler_params=pltpu.CompilerParams(vmem_limit_bytes=VMEM_LIMIT),
        cost_estimate=cost,
        name=name,
    )(*args)


def shaped(shape, dtype):
    return jax.ShapeDtypeStruct(shape, dtype)


def project_kernel(at, *refs):
    xs, w, out_q, out_kv, stats = refs[:8], refs[8], *refs[9:]
    zl, x, c = at[0], at[1], at[2]
    total = None
    for i in range(2):
        core = lax.rem(c + i, 2)
        for j in range(4):
            x_from = lax.rem(x - j + 4, 4)
            for k in range(4):
                chip = lax.rem(zl - k + 4, 4) * 4 + x_from
                weights = jnp.concatenate([w[chip, p, core] for p in range(3)], axis=1)
                term = contract_first(weights, xs[4 * i + j][k])
                total = term if total is None else total + term
    query, key, value = total[:128], total[128:256], total[256:]
    out_q[...] = query
    out_kv[0] = key
    out_kv[1] = value
    rows = []
    for part in (query, key):
        row = jnp.sum(part * part, axis=0, keepdims=True)
        rows += [row[:, :128], row[:, 128:]]
    packed = jnp.concatenate(rows + [jnp.zeros((4, 128), F32)], axis=0)
    for t in range(stats.shape[0]):
        stats[t] = packed


def rotate_kernel(width, got, q, kv, cosine, sine, qg, kg, marks, q_out, k_cache, v_cache, message):
    totals = jnp.sum(got[...], axis=0)
    even = lax.rem(lax.broadcasted_iota(jnp.int32, (HEAD_DIM, 256), 0), 2) == 0
    cos, sin = cosine[...], sine[...]

    def rotated(value, gain, row):
        factor = jnp.concatenate([totals[row : row + 1], totals[row + 1 : row + 2]], axis=1)
        factor = lax.rsqrt(factor / width + EPSILON)
        normed = value * factor * gain
        after = pltpu.roll(normed, HEAD_DIM - 1, 0)
        before = pltpu.roll(normed, 1, 0)
        partner = jnp.where(even, -after, before)
        return normed * cos + partner * sin

    extra = marks[...].astype(BF16)
    q_out[:128] = rotated(q[...], qg[...], 0).astype(BF16)
    q_out[128:144] = extra
    k_rot = rotated(kv[0], kg[...], 2)
    value = kv[1]
    k_low = k_rot.astype(BF16)
    v_low = value.astype(BF16)
    for t in range(message.shape[0]):
        message[t, :128] = k_low
        message[t, 128:256] = v_low
        message[t, 256:272] = extra
    k_cache[...] = k_rot.T.astype(BF16)
    v_cache[...] = value.T.astype(BF16)


def attend_kernel(q, q_got, keys, mine, mine_lse, message, held):
    count = keys.shape[0]
    scale = LOG2E / math.sqrt(HEAD_DIM)
    q_low = jnp.concatenate([q[:128], q_got[:128]], axis=1)
    seg_q = jnp.concatenate([q[128:144], q_got[128:144]], axis=1).astype(F32)[:1]
    top = None
    for b in range(count):
        seg_k = keys[b, 256:272].astype(F32).T[:, :1]
        scores = contract_first(keys[b, :128], q_low) * scale
        scores = jnp.where(seg_k == seg_q, scores, NEG_FILL)
        held[b] = scores
        here = jnp.max(scores, axis=0, keepdims=True)
        top = here if top is None else jnp.maximum(top, here)
    top = jnp.maximum(top, -1e20)
    total = jnp.zeros((1, 512), F32)
    weighted = jnp.zeros((HEAD_DIM, 512), F32)
    for b in range(count):
        weights = jnp.exp2(held[b] - top)
        total = total + jnp.sum(weights, axis=0, keepdims=True)
        weighted = weighted + jnp.dot(
            keys[b, 128:256], weights.astype(BF16), preferred_element_type=F32
        )
    some = total > 0.0
    safe = jnp.where(some, total, 1.0)
    out = weighted / safe
    lse = jnp.where(some, top + jnp.log2(safe), NEG_FILL)
    mine[...] = out[:, :256]
    mine_lse[...] = jnp.broadcast_to(lse[:, :256], (8, 256))
    other_lse = lse[:, 256:]
    high = other_lse.astype(BF16)
    rest = other_lse - high.astype(F32)
    middle = rest.astype(BF16)
    low = (rest - middle.astype(F32)).astype(BF16)
    message[:128] = out[:, 256:].astype(BF16)
    message[128:144] = jnp.concatenate(
        [high.astype(F32), middle.astype(F32), low.astype(F32), jnp.zeros((13, 256), F32)], axis=0
    ).astype(BF16)


def merge_kernel(mine, mine_lse, *refs):
    gots, out = refs[:-1], refs[-1]
    parts = [(mine_lse[0:1], mine[...])]
    for got in gots:
        rows = got[128:144].astype(F32)
        parts.append((rows[0:1] + rows[1:2] + rows[2:3], got[:128].astype(F32)))
    top = functools.reduce(jnp.maximum, [lse for lse, _ in parts])
    weights = [jnp.exp2(lse - top) for lse, _ in parts]
    total = sum(weights[1:], weights[0])
    value = None
    for weight, (_, part) in zip(weights, parts, strict=True):
        term = part * (weight / total)
        value = term if value is None else value + term
    out[...] = value.astype(BF16)


def output_kernel(at, *refs):
    heads, w, mine, message, held = refs[:4], refs[4], *refs[5:]
    zl, x, c, zh = at[0], at[1], at[2], at[3]
    total = None
    for j in range(4):
        x_from = lax.rem(x - j + 4, 4)
        for k in range(4):
            chip = lax.rem(zl - k + 4, 4) * 4 + x_from
            flip = lax.rem(lax.rem(chip, 2) + zh, 2)
            term = jnp.dot(w[chip // 2, flip], heads[j][k], preferred_element_type=F32)
            total = term if total is None else total + term
    held[0] = total[:160]
    held[1] = total[160:]
    mine[...] = held[c]
    message[...] = held[1 - c]


def body(hidden_in, seg_ids, positions, mod_table, w_qkv, q_gain, k_gain, w_out):
    tok_rows, feat_local = hidden_in.shape
    model_width = feat_local * 32
    heads_width = 4096
    zl, c, zh = lax.axis_index("zl"), lax.axis_index("c"), lax.axis_index("zh")
    x = lax.axis_index("xh") * 2 + lax.axis_index("xl")
    at = jnp.stack([zl, x, c, zh]).astype(jnp.int32)

    w_pair = lax.all_gather(jnp.transpose(w_qkv, (1, 0, 2)), "zh", axis=0, tiled=False)
    w_all = lax.all_gather(w_pair, ("ya", "yb", "yc"), axis=0, tiled=False)
    w_all = w_all.reshape(16, 3, 2, 160, 128)

    x_t = hidden_in.T.astype(F32)
    sums = jnp.stack([jnp.sum(x_t, axis=0), jnp.sum(x_t * x_t, axis=0)]).reshape(4, 128)
    sums = jnp.concatenate([sums, jnp.zeros((4, 128), F32)], axis=0)
    sums, w_pair = lax.optimization_barrier((sums, w_pair))
    sums = lax.all_to_all(jnp.broadcast_to(sums, (32, 8, 128)), TP, 0, 0, tiled=True)
    sums = jnp.sum(sums, axis=0)[:4].reshape(2, tok_rows)
    mean_value = sums[0:1] / model_width
    variance = sums[1:2] / model_width - mean_value * mean_value
    normed = (x_t - mean_value) * lax.rsqrt(variance + EPSILON)
    segment_count = mod_table.shape[0]
    onehot = (seg_ids[None, :] == jnp.arange(segment_count, dtype=jnp.int32)[:, None]).astype(F32)
    modulation = lax.dot_general(
        mod_table.reshape(segment_count, 3 * feat_local),
        onehot,
        (((0,), (0,)), ((), ())),
        precision=lax.Precision.HIGHEST,
    ).reshape(3, feat_local, tok_rows)
    packet = (normed * (1.0 + modulation[1]) + modulation[0]).astype(BF16)

    held = jnp.stack(
        [packet]
        + [permute(packet, ("zl",), lambda zl, k=k: ((zl + k) % 4,)) for k in range(1, 4)]
    )
    along_x = [held] + [
        permute(held, ("xh", "xl"), lambda xh, xl, j=j: divmod((xh * 2 + xl + j) % 4, 2))
        for j in range(1, 4)
    ]
    swapped = [permute(part, ("c",), lambda c: (1 - c,)) for part in along_x]

    part_width = HEAD_DIM // 6
    widths = (HEAD_DIM - 4 * part_width, 2 * part_width, 2 * part_width)
    angles = []
    for axis_number in range(3):
        width = widths[axis_number]
        exponent = jnp.arange(0, width, 2, dtype=F32) / width
        frequency = jnp.repeat(1.0 / 10000.0**exponent, 2)
        angles.append(positions[axis_number].astype(F32)[None, :] * frequency[:, None])
    angle = jnp.concatenate(angles, axis=0)
    cosine, sine = jnp.cos(angle), jnp.sin(angle)
    marks = jnp.broadcast_to(seg_ids[None, :].astype(F32), (16, tok_rows))

    query, key_value, stats = call(
        project_kernel,
        (shaped((128, 256), F32), shaped((2, 128, 256), F32), shaped((32, 8, 128), F32)),
        along_x + swapped + [w_all],
        scalars=at,
        name="project",
        cost=pl.CostEstimate(flops=2 * 256 * 5120 * 384, bytes_accessed=6 << 20, transcendentals=0),
    )
    stats = lax.all_to_all(stats, TP, 0, 0, tiled=True)
    q_rot, k_cache, v_cache, kv_message = call(
        functools.partial(rotate_kernel, heads_width),
        (
            shaped((144, 256), BF16),
            shaped((256, 128), BF16),
            shaped((256, 128), BF16),
            shaped((8, 272, 256), BF16),
        ),
        [stats, query, key_value, cosine, sine, q_gain.reshape(128, 1), k_gain.reshape(128, 1), marks],
        name="rotate",
    )
    keys = lax.all_to_all(kv_message, ("ya", "yb", "yc"), 0, 0, tiled=True)
    q_got = permute(q_rot, ("zh",), lambda zh: (1 - zh,))

    def turned(value, flip):
        def move(ya, yb, yc, zh, zl, xh, xl, c):
            s = (ya * 4 + yb * 2 + yc) * 2 + zh
            chip = (zl * 2 + xh) * 2 + xl
            to_s = chip ^ flip
            return (to_s >> 3, (to_s >> 2) & 1, (to_s >> 1) & 1, to_s & 1, s >> 2, (s >> 1) & 1, s & 1, c)

        return permute(value, SEQ + TP, move)

    wo_local, q_got = lax.optimization_barrier((w_out.T, q_got))
    wo_pair = jnp.stack([turned(wo_local, 0), turned(wo_local, 1)])
    wo_pair, keys = lax.optimization_barrier((wo_pair, keys))
    wo_all = lax.all_gather(wo_pair, ("ya", "yb", "yc"), axis=0, tiled=False)

    mine, mine_lse, o_message = call(
        attend_kernel,
        (shaped((128, 256), F32), shaped((8, 256), F32), shaped((144, 256), BF16)),
        [q_rot, q_got, keys],
        scratch=[pltpu.VMEM((8, 256, 512), F32)],
        name="attend",
    )
    o_got = permute(o_message, ("zh",), lambda zh: (1 - zh,))
    attention = call(merge_kernel, shaped((128, 256), BF16), [mine, mine_lse, o_got], name="merge")

    by_z = [attention] + [
        permute(attention, ("zl",), lambda zl, k=k: ((zl + k) % 4,)) for k in range(1, 4)
    ]
    by_z = jnp.stack(by_z)
    by_x = [by_z] + [
        permute(by_z, ("xh", "xl"), lambda xh, xl, j=j: divmod((xh * 2 + xl + j) % 4, 2))
        for j in range(1, 4)
    ]
    out_mine, out_message = call(
        output_kernel,
        (shaped((160, 256), F32), shaped((160, 256), F32)),
        by_x + [wo_all],
        scalars=at,
        scratch=[pltpu.VMEM((2, 160, 256), F32)],
        name="output",
    )
    out_got = permute(out_message, ("c",), lambda c: (1 - c,))
    mixed = out_mine + out_got
    hidden_out = (x_t + modulation[2] * mixed).T.astype(BF16)
    return (hidden_out, k_cache, v_cache)


def solution(mesh):
    split = Mesh(mesh.devices.reshape(tuple(SIZES.values())), tuple(SIZES))
    in_specs = (
        P(SEQ, TP),
        P(SEQ),
        P(None, SEQ),
        P(None, None, TP),
        P(SEQ, None, TP),
        P(TP),
        P(TP),
        P(TP, SEQ),
    )
    out_specs = (P(SEQ, TP), P(SEQ, TP), P(SEQ, TP))
    return jax.shard_map(body, mesh=split, in_specs=in_specs, out_specs=out_specs, check_vma=False)
```

```python
import functools
import itertools
import math

import jax
import jax.numpy as jnp
import numpy as np
from jax import lax
from jax.experimental import pallas as pl
from jax.experimental.pallas import tpu as pltpu
from jax.sharding import Mesh
from jax.sharding import PartitionSpec as P

HEAD_DIM = 128
EPSILON = 1e-06
NEG_FILL = -1e30
LOG2E = 1.4426950408889634

SEQ = ("ya", "yb", "yc", "zh")
TP = ("zl", "xh", "xl", "c")
SIZES = {"ya": 2, "yb": 2, "yc": 2, "zh": 2, "zl": 4, "xh": 2, "xl": 2, "c": 2}

F32 = jnp.float32
BF16 = jnp.bfloat16
VMEM_LIMIT = 48 << 20


def permute(value, axes, move):
    sizes = [SIZES[a] for a in axes]
    pairs = []
    for at in itertools.product(*[range(n) for n in sizes]):
        to = move(*at)
        pairs.append((int(np.ravel_multi_index(at, sizes)), int(np.ravel_multi_index(to, sizes))))
    return lax.ppermute(value, axes, pairs)


def contract_first(lhs, rhs):
    return lax.dot_general(lhs, rhs, (((0,), (0,)), ((), ())), preferred_element_type=F32)


def call(kernel, out_shape, operands, scalars=None, scratch=(), name=None, cost=None):
    vmem = pl.BlockSpec(memory_space=pltpu.VMEM)
    smem = pl.BlockSpec(memory_space=pltpu.SMEM)
    specs = ([] if scalars is None else [smem]) + [vmem] * len(operands)
    args = ([] if scalars is None else [scalars]) + list(operands)
    return pl.pallas_call(
        kernel,
        out_shape=out_shape,
        in_specs=specs,
        out_specs=jax.tree.map(lambda _: vmem, out_shape),
        scratch_shapes=list(scratch),
        compiler_params=pltpu.CompilerParams(vmem_limit_bytes=VMEM_LIMIT),
        cost_estimate=cost,
        name=name,
    )(*args)


def shaped(shape, dtype):
    return jax.ShapeDtypeStruct(shape, dtype)


def project_kernel(at, *refs):
    xs, w, out_q, out_kv, stats = refs[:8], refs[8], *refs[9:]
    zl, x, c = at[0], at[1], at[2]
    total = None
    for i in range(2):
        core = lax.rem(c + i, 2)
        for j in range(4):
            x_from = lax.rem(x - j + 4, 4)
            for k in range(4):
                chip = lax.rem(zl - k + 4, 4) * 4 + x_from
                weights = jnp.concatenate([w[chip, p, core] for p in range(3)], axis=1)
                term = contract_first(weights, xs[4 * i + j][k])
                total = term if total is None else total + term
    query, key, value = total[:128], total[128:256], total[256:]
    out_q[...] = query
    out_kv[0] = key
    out_kv[1] = value
    rows = []
    for part in (query, key):
        row = jnp.sum(part * part, axis=0, keepdims=True)
        rows += [row[:, :128], row[:, 128:]]
    packed = jnp.concatenate(rows + [jnp.zeros((4, 128), F32)], axis=0)
    for t in range(stats.shape[0]):
        stats[t] = packed


def rotate_kernel(width, got, q, kv, cosine, sine, qg, kg, marks, q_out, k_cache, v_cache, message):
    totals = jnp.sum(got[...], axis=0)
    even = lax.rem(lax.broadcasted_iota(jnp.int32, (HEAD_DIM, 256), 0), 2) == 0
    cos, sin = cosine[...], sine[...]

    def rotated(value, gain, row):
        factor = jnp.concatenate([totals[row : row + 1], totals[row + 1 : row + 2]], axis=1)
        factor = lax.rsqrt(factor / width + EPSILON)
        normed = value * factor * gain
        after = pltpu.roll(normed, HEAD_DIM - 1, 0)
        before = pltpu.roll(normed, 1, 0)
        partner = jnp.where(even, -after, before)
        return normed * cos + partner * sin

    extra = marks[...].astype(BF16)
    q_out[:128] = rotated(q[...], qg[...], 0).astype(BF16)
    q_out[128:144] = extra
    k_rot = rotated(kv[0], kg[...], 2)
    value = kv[1]
    k_low = k_rot.astype(BF16)
    v_low = value.astype(BF16)
    for t in range(message.shape[0]):
        message[t, :128] = k_low
        message[t, 128:256] = v_low
        message[t, 256:272] = extra
    k_cache[...] = k_rot.T.astype(BF16)
    v_cache[...] = value.T.astype(BF16)


def attend_kernel(q, q_got, keys, mine, mine_lse, message, held):
    count = keys.shape[0]
    scale = LOG2E / math.sqrt(HEAD_DIM)
    q_low = jnp.concatenate([q[:128], q_got[:128]], axis=1)
    seg_q = jnp.concatenate([q[128:144], q_got[128:144]], axis=1).astype(F32)[:1]
    top = None
    for b in range(count):
        seg_k = keys[b, 256:272].astype(F32).T[:, :1]
        scores = contract_first(keys[b, :128], q_low) * scale
        scores = jnp.where(seg_k == seg_q, scores, NEG_FILL)
        held[b] = scores
        here = jnp.max(scores, axis=0, keepdims=True)
        top = here if top is None else jnp.maximum(top, here)
    top = jnp.maximum(top, -1e20)
    total = jnp.zeros((1, 512), F32)
    weighted = jnp.zeros((HEAD_DIM, 512), F32)
    for b in range(count):
        weights = jnp.exp2(held[b] - top)
        total = total + jnp.sum(weights, axis=0, keepdims=True)
        weighted = weighted + jnp.dot(
            keys[b, 128:256], weights.astype(BF16), preferred_element_type=F32
        )
    some = total > 0.0
    safe = jnp.where(some, total, 1.0)
    out = weighted / safe
    lse = jnp.where(some, top + jnp.log2(safe), NEG_FILL)
    mine[...] = out[:, :256]
    mine_lse[...] = jnp.broadcast_to(lse[:, :256], (8, 256))
    other_lse = lse[:, 256:]
    high = other_lse.astype(BF16)
    rest = other_lse - high.astype(F32)
    middle = rest.astype(BF16)
    low = (rest - middle.astype(F32)).astype(BF16)
    message[:128] = out[:, 256:].astype(BF16)
    message[128:144] = jnp.concatenate(
        [high.astype(F32), middle.astype(F32), low.astype(F32), jnp.zeros((13, 256), F32)], axis=0
    ).astype(BF16)


def merge_kernel(mine, mine_lse, *refs):
    gots, out = refs[:-1], refs[-1]
    parts = [(mine_lse[0:1], mine[...])]
    for got in gots:
        rows = got[128:144].astype(F32)
        parts.append((rows[0:1] + rows[1:2] + rows[2:3], got[:128].astype(F32)))
    top = functools.reduce(jnp.maximum, [lse for lse, _ in parts])
    weights = [jnp.exp2(lse - top) for lse, _ in parts]
    total = sum(weights[1:], weights[0])
    value = None
    for weight, (_, part) in zip(weights, parts, strict=True):
        term = part * (weight / total)
        value = term if value is None else value + term
    out[...] = value.astype(BF16)


def output_kernel(at, *refs):
    heads, w, mine, message, held = refs[:4], refs[4], *refs[5:]
    zl, x, c, zh = at[0], at[1], at[2], at[3]
    total = None
    for j in range(4):
        x_from = lax.rem(x - j + 4, 4)
        for k in range(4):
            chip = lax.rem(zl - k + 4, 4) * 4 + x_from
            flip = lax.rem(lax.rem(chip, 2) + zh, 2)
            term = jnp.dot(w[chip // 2, flip], heads[j][k], preferred_element_type=F32)
            total = term if total is None else total + term
    held[0] = total[:160]
    held[1] = total[160:]
    mine[...] = held[c]
    message[...] = held[1 - c]


def body(hidden_in, seg_ids, positions, mod_table, w_qkv, q_gain, k_gain, w_out):
    tok_rows, feat_local = hidden_in.shape
    model_width = feat_local * 32
    heads_width = 4096
    zl, c, zh = lax.axis_index("zl"), lax.axis_index("c"), lax.axis_index("zh")
    x = lax.axis_index("xh") * 2 + lax.axis_index("xl")
    at = jnp.stack([zl, x, c, zh]).astype(jnp.int32)

    w_pair = lax.all_gather(jnp.transpose(w_qkv, (1, 0, 2)), "zh", axis=0, tiled=False)
    w_all = lax.all_gather(w_pair, ("ya", "yb", "yc"), axis=0, tiled=False)
    w_all = w_all.reshape(16, 3, 2, 160, 128)

    def turned(flip):
        def move(ya, yb, yc, zh, zl, xh, xl, c):
            s = (ya * 4 + yb * 2 + yc) * 2 + zh
            chip = (zl * 2 + xh) * 2 + xl
            to_s = chip ^ flip
            return (to_s >> 3, (to_s >> 2) & 1, (to_s >> 1) & 1, to_s & 1, s >> 2, (s >> 1) & 1, s & 1, c)

        return permute(w_out.T, SEQ + TP, move)

    wo_turned = (turned(0), turned(1))

    x_t = hidden_in.T.astype(F32)
    sums = jnp.stack([jnp.sum(x_t, axis=0), jnp.sum(x_t * x_t, axis=0)]).reshape(4, 128)
    sums = jnp.concatenate([sums, jnp.zeros((4, 128), F32)], axis=0)
    sums, w_pair = lax.optimization_barrier((sums, w_pair))
    sums = lax.all_to_all(jnp.broadcast_to(sums, (32, 8, 128)), TP, 0, 0, tiled=True)
    sums = jnp.sum(sums, axis=0)[:4].reshape(2, tok_rows)
    mean_value = sums[0:1] / model_width
    variance = sums[1:2] / model_width - mean_value * mean_value
    normed = (x_t - mean_value) * lax.rsqrt(variance + EPSILON)
    segment_count = mod_table.shape[0]
    onehot = (seg_ids[None, :] == jnp.arange(segment_count, dtype=jnp.int32)[:, None]).astype(F32)
    modulation = lax.dot_general(
        mod_table.reshape(segment_count, 3 * feat_local),
        onehot,
        (((0,), (0,)), ((), ())),
        precision=lax.Precision.HIGHEST,
    ).reshape(3, feat_local, tok_rows)
    packet = (normed * (1.0 + modulation[1]) + modulation[0]).astype(BF16)
    packet, wo_turned = lax.optimization_barrier((packet, wo_turned))

    held = jnp.stack(
        [packet]
        + [permute(packet, ("zl",), lambda zl, k=k: ((zl + k) % 4,)) for k in range(1, 4)]
    )
    along_x = [held] + [
        permute(held, ("xh", "xl"), lambda xh, xl, j=j: divmod((xh * 2 + xl + j) % 4, 2))
        for j in range(1, 4)
    ]
    swapped = [permute(part, ("c",), lambda c: (1 - c,)) for part in along_x]

    part_width = HEAD_DIM // 6
    widths = (HEAD_DIM - 4 * part_width, 2 * part_width, 2 * part_width)
    angles = []
    for axis_number in range(3):
        width = widths[axis_number]
        exponent = jnp.arange(0, width, 2, dtype=F32) / width
        frequency = jnp.repeat(1.0 / 10000.0**exponent, 2)
        angles.append(positions[axis_number].astype(F32)[None, :] * frequency[:, None])
    angle = jnp.concatenate(angles, axis=0)
    cosine, sine = jnp.cos(angle), jnp.sin(angle)
    marks = jnp.broadcast_to(seg_ids[None, :].astype(F32), (16, tok_rows))

    query, key_value, stats = call(
        project_kernel,
        (shaped((128, 256), F32), shaped((2, 128, 256), F32), shaped((32, 8, 128), F32)),
        along_x + swapped + [w_all],
        scalars=at,
        name="project",
        cost=pl.CostEstimate(flops=2 * 256 * 5120 * 384, bytes_accessed=6 << 20, transcendentals=0),
    )
    stats = lax.all_to_all(stats, TP, 0, 0, tiled=True)
    q_rot, k_cache, v_cache, kv_message = call(
        functools.partial(rotate_kernel, heads_width),
        (
            shaped((144, 256), BF16),
            shaped((256, 128), BF16),
            shaped((256, 128), BF16),
            shaped((8, 272, 256), BF16),
        ),
        [stats, query, key_value, cosine, sine, q_gain.reshape(128, 1), k_gain.reshape(128, 1), marks],
        name="rotate",
    )
    keys = lax.all_to_all(kv_message, ("ya", "yb", "yc"), 0, 0, tiled=True)
    q_got = permute(q_rot, ("zh",), lambda zh: (1 - zh,))

    wo_pair, keys, q_got = lax.optimization_barrier((jnp.stack(wo_turned), keys, q_got))
    wo_all = lax.all_gather(wo_pair, ("ya", "yb", "yc"), axis=0, tiled=False)

    mine, mine_lse, o_message = call(
        attend_kernel,
        (shaped((128, 256), F32), shaped((8, 256), F32), shaped((144, 256), BF16)),
        [q_rot, q_got, keys],
        scratch=[pltpu.VMEM((8, 256, 512), F32)],
        name="attend",
    )
    o_got = permute(o_message, ("zh",), lambda zh: (1 - zh,))
    attention = call(merge_kernel, shaped((128, 256), BF16), [mine, mine_lse, o_got], name="merge")

    by_z = [attention] + [
        permute(attention, ("zl",), lambda zl, k=k: ((zl + k) % 4,)) for k in range(1, 4)
    ]
    by_z = jnp.stack(by_z)
    by_x = [by_z] + [
        permute(by_z, ("xh", "xl"), lambda xh, xl, j=j: divmod((xh * 2 + xl + j) % 4, 2))
        for j in range(1, 4)
    ]
    out_mine, out_message = call(
        output_kernel,
        (shaped((160, 256), F32), shaped((160, 256), F32)),
        by_x + [wo_all],
        scalars=at,
        scratch=[pltpu.VMEM((2, 160, 256), F32)],
        name="output",
    )
    out_got = permute(out_message, ("c",), lambda c: (1 - c,))
    mixed = out_mine + out_got
    hidden_out = (x_t + modulation[2] * mixed).T.astype(BF16)
    return (hidden_out, k_cache, v_cache)


def solution(mesh):
    split = Mesh(mesh.devices.reshape(tuple(SIZES.values())), tuple(SIZES))
    in_specs = (
        P(SEQ, TP),
        P(SEQ),
        P(None, SEQ),
        P(None, None, TP),
        P(SEQ, None, TP),
        P(TP),
        P(TP),
        P(TP, SEQ),
    )
    out_specs = (P(SEQ, TP), P(SEQ, TP), P(SEQ, TP))
    return jax.shard_map(body, mesh=split, in_specs=in_specs, out_specs=out_specs, check_vma=False)
```

```python
import functools
import itertools
import math

import jax
import jax.numpy as jnp
import numpy as np
from jax import lax
from jax.experimental import pallas as pl
from jax.experimental.pallas import tpu as pltpu
from jax.sharding import Mesh
from jax.sharding import PartitionSpec as P

HEAD_DIM = 128
EPSILON = 1e-06
NEG_FILL = -1e30
LOG2E = 1.4426950408889634

SEQ = ("ya", "yb", "yc", "zh")
TP = ("zl", "xh", "xl", "c")
SIZES = {"ya": 2, "yb": 2, "yc": 2, "zh": 2, "zl": 4, "xh": 2, "xl": 2, "c": 2}

F32 = jnp.float32
BF16 = jnp.bfloat16
VMEM_LIMIT = 48 << 20


def permute(value, axes, move):
    sizes = [SIZES[a] for a in axes]
    pairs = []
    for at in itertools.product(*[range(n) for n in sizes]):
        to = move(*at)
        pairs.append((int(np.ravel_multi_index(at, sizes)), int(np.ravel_multi_index(to, sizes))))
    return lax.ppermute(value, axes, pairs)


def contract_first(lhs, rhs):
    return lax.dot_general(lhs, rhs, (((0,), (0,)), ((), ())), preferred_element_type=F32)


def call(kernel, out_shape, operands, scalars=None, scratch=(), name=None, cost=None):
    vmem = pl.BlockSpec(memory_space=pltpu.VMEM)
    smem = pl.BlockSpec(memory_space=pltpu.SMEM)
    specs = ([] if scalars is None else [smem]) + [vmem] * len(operands)
    args = ([] if scalars is None else [scalars]) + list(operands)
    return pl.pallas_call(
        kernel,
        out_shape=out_shape,
        in_specs=specs,
        out_specs=jax.tree.map(lambda _: vmem, out_shape),
        scratch_shapes=list(scratch),
        compiler_params=pltpu.CompilerParams(vmem_limit_bytes=VMEM_LIMIT),
        cost_estimate=cost,
        name=name,
    )(*args)


def shaped(shape, dtype):
    return jax.ShapeDtypeStruct(shape, dtype)


def project_kernel(at, *refs):
    xs, w, out_q, out_kv, stats = refs[:8], refs[8], *refs[9:]
    zl, x, c = at[0], at[1], at[2]
    total = None
    for i in range(2):
        core = lax.rem(c + i, 2)
        for j in range(4):
            x_from = lax.rem(x - j + 4, 4)
            for k in range(4):
                chip = lax.rem(zl - k + 4, 4) * 4 + x_from
                weights = jnp.concatenate([w[chip, p, core] for p in range(3)], axis=1)
                term = contract_first(weights, xs[4 * i + j][k])
                total = term if total is None else total + term
    query, key, value = total[:128], total[128:256], total[256:]
    out_q[...] = query
    out_kv[0] = key
    out_kv[1] = value
    rows = []
    for part in (query, key):
        row = jnp.sum(part * part, axis=0, keepdims=True)
        rows += [row[:, :128], row[:, 128:]]
    packed = jnp.concatenate(rows + [jnp.zeros((4, 128), F32)], axis=0)
    for t in range(stats.shape[0]):
        stats[t] = packed


def rotate_kernel(width, got, q, kv, cosine, sine, qg, kg, marks, q_out, k_cache, v_cache, message):
    totals = jnp.sum(got[...], axis=0)
    even = lax.rem(lax.broadcasted_iota(jnp.int32, (HEAD_DIM, 256), 0), 2) == 0
    cos, sin = cosine[...], sine[...]

    def rotated(value, gain, row):
        factor = jnp.concatenate([totals[row : row + 1], totals[row + 1 : row + 2]], axis=1)
        factor = lax.rsqrt(factor / width + EPSILON)
        normed = value * factor * gain
        after = pltpu.roll(normed, HEAD_DIM - 1, 0)
        before = pltpu.roll(normed, 1, 0)
        partner = jnp.where(even, -after, before)
        return normed * cos + partner * sin

    extra = marks[...].astype(BF16)
    q_out[:128] = rotated(q[...], qg[...], 0).astype(BF16)
    q_out[128:144] = extra
    k_rot = rotated(kv[0], kg[...], 2)
    value = kv[1]
    k_low = k_rot.astype(BF16)
    v_low = value.astype(BF16)
    for t in range(message.shape[0]):
        message[t, :128] = k_low
        message[t, 128:256] = v_low
        message[t, 256:272] = extra
    k_cache[...] = k_rot.T.astype(BF16)
    v_cache[...] = value.T.astype(BF16)


def attend_kernel(q, q1, q2, q3, keys, mine, mine_lse, m1, m2, m3, held):
    count = keys.shape[0]
    scale = LOG2E / math.sqrt(HEAD_DIM)
    parts = (q, q1, q2, q3)
    q_low = jnp.concatenate([part[:128] for part in parts], axis=1)
    seg_q = jnp.concatenate([part[128:144] for part in parts], axis=1).astype(F32)[:1]
    top = None
    for b in range(count):
        seg_k = keys[b, 256:272].astype(F32).T[:, :1]
        scores = contract_first(keys[b, :128], q_low) * scale
        scores = jnp.where(seg_k == seg_q, scores, NEG_FILL)
        held[b] = scores
        here = jnp.max(scores, axis=0, keepdims=True)
        top = here if top is None else jnp.maximum(top, here)
    top = jnp.maximum(top, -1e20)
    total = jnp.zeros((1, 1024), F32)
    weighted = jnp.zeros((HEAD_DIM, 1024), F32)
    for b in range(count):
        weights = jnp.exp2(held[b] - top)
        total = total + jnp.sum(weights, axis=0, keepdims=True)
        weighted = weighted + jnp.dot(
            keys[b, 128:256], weights.astype(BF16), preferred_element_type=F32
        )
    some = total > 0.0
    safe = jnp.where(some, total, 1.0)
    out = weighted / safe
    lse = jnp.where(some, top + jnp.log2(safe), NEG_FILL)
    mine[...] = out[:, :256]
    mine_lse[...] = jnp.broadcast_to(lse[:, :256], (8, 256))
    for d, message in enumerate((m1, m2, m3), 1):
        here = slice(256 * d, 256 * d + 256)
        high = lse[:, here].astype(BF16)
        rest = lse[:, here] - high.astype(F32)
        middle = rest.astype(BF16)
        low = (rest - middle.astype(F32)).astype(BF16)
        message[:128] = out[:, here].astype(BF16)
        message[128:144] = jnp.concatenate(
            [high.astype(F32), middle.astype(F32), low.astype(F32), jnp.zeros((13, 256), F32)], axis=0
        ).astype(BF16)


def merge_kernel(mine, mine_lse, *refs):
    gots, out = refs[:-1], refs[-1]
    parts = [(mine_lse[0:1], mine[...])]
    for got in gots:
        rows = got[128:144].astype(F32)
        parts.append((rows[0:1] + rows[1:2] + rows[2:3], got[:128].astype(F32)))
    top = functools.reduce(jnp.maximum, [lse for lse, _ in parts])
    weights = [jnp.exp2(lse - top) for lse, _ in parts]
    total = sum(weights[1:], weights[0])
    value = None
    for weight, (_, part) in zip(weights, parts, strict=True):
        term = part * (weight / total)
        value = term if value is None else value + term
    out[...] = value.astype(BF16)


def partial_kernel(at, own, other, w, mine, *messages):
    x = at[1]
    heads = jnp.concatenate([own[...], other[...]], axis=0)
    for j in range(4):
        x_to = lax.rem(x + j, 4)
        high, low = x_to // 2, lax.rem(x_to, 2)
        for z in range(4):
            block = 2 * z + high
            weights = jnp.concatenate([w[block, 0, low], w[block, 1, low]], axis=1)
            term = jnp.dot(weights, heads, preferred_element_type=F32)
            if j == 0:
                mine[z] = term
            else:
                messages[j - 1][z] = term.astype(BF16)


def along_z_kernel(at, own, g1, g2, g3, mine, m1, m2, m3):
    zl = at[0]
    for k in range(4):
        z = lax.rem(zl + k, 4)
        total = own[z]
        for got in (g1, g2, g3):
            total = total + got[z].astype(F32)
        if k == 0:
            mine[...] = total
        else:
            (m1, m2, m3)[k - 1][...] = total.astype(BF16)


def body(hidden_in, seg_ids, positions, mod_table, w_qkv, q_gain, k_gain, w_out):
    tok_rows, feat_local = hidden_in.shape
    model_width = feat_local * 32
    heads_width = 4096
    zl, c, zh = lax.axis_index("zl"), lax.axis_index("c"), lax.axis_index("zh")
    x = lax.axis_index("xh") * 2 + lax.axis_index("xl")
    at = jnp.stack([zl, x, c, zh]).astype(jnp.int32)

    local = jnp.concatenate([jnp.transpose(w_qkv, (1, 0, 2)), w_out.T[None]], axis=0)
    pair = lax.all_gather(local, "zh", axis=0, tiled=False)
    w_pair, wo_pair = pair[:, :3], pair[:, 3].reshape(2, 2, 160, 128)
    w_all = lax.all_gather(w_pair, ("ya", "yb", "yc"), axis=0, tiled=False)
    w_all = w_all.reshape(16, 3, 2, 160, 128)

    x_t = hidden_in.T.astype(F32)
    sums = jnp.stack([jnp.sum(x_t, axis=0), jnp.sum(x_t * x_t, axis=0)]).reshape(4, 128)
    sums = jnp.concatenate([sums, jnp.zeros((4, 128), F32)], axis=0)
    sums, w_pair = lax.optimization_barrier((sums, w_pair))
    sums = lax.all_to_all(jnp.broadcast_to(sums, (32, 8, 128)), TP, 0, 0, tiled=True)
    sums = jnp.sum(sums, axis=0)[:4].reshape(2, tok_rows)
    mean_value = sums[0:1] / model_width
    variance = sums[1:2] / model_width - mean_value * mean_value
    normed = (x_t - mean_value) * lax.rsqrt(variance + EPSILON)
    segment_count = mod_table.shape[0]
    onehot = (seg_ids[None, :] == jnp.arange(segment_count, dtype=jnp.int32)[:, None]).astype(F32)
    modulation = lax.dot_general(
        mod_table.reshape(segment_count, 3 * feat_local),
        onehot,
        (((0,), (0,)), ((), ())),
        precision=lax.Precision.HIGHEST,
    ).reshape(3, feat_local, tok_rows)
    packet = (normed * (1.0 + modulation[1]) + modulation[0]).astype(BF16)

    held = jnp.stack(
        [packet]
        + [permute(packet, ("zl",), lambda zl, k=k: ((zl + k) % 4,)) for k in range(1, 4)]
    )
    along_x = [held] + [
        permute(held, ("xh", "xl"), lambda xh, xl, j=j: divmod((xh * 2 + xl + j) % 4, 2))
        for j in range(1, 4)
    ]
    swapped = [permute(part, ("c",), lambda c: (1 - c,)) for part in along_x]

    part_width = HEAD_DIM // 6
    widths = (HEAD_DIM - 4 * part_width, 2 * part_width, 2 * part_width)
    angles = []
    for axis_number in range(3):
        width = widths[axis_number]
        exponent = jnp.arange(0, width, 2, dtype=F32) / width
        frequency = jnp.repeat(1.0 / 10000.0**exponent, 2)
        angles.append(positions[axis_number].astype(F32)[None, :] * frequency[:, None])
    angle = jnp.concatenate(angles, axis=0)
    cosine, sine = jnp.cos(angle), jnp.sin(angle)
    marks = jnp.broadcast_to(seg_ids[None, :].astype(F32), (16, tok_rows))

    query, key_value, stats = call(
        project_kernel,
        (shaped((128, 256), F32), shaped((2, 128, 256), F32), shaped((32, 8, 128), F32)),
        along_x + swapped + [w_all],
        scalars=at,
        name="project",
        cost=pl.CostEstimate(flops=2 * 256 * 5120 * 384, bytes_accessed=6 << 20, transcendentals=0),
    )
    stats = lax.all_to_all(stats, TP, 0, 0, tiled=True)
    q_rot, k_cache, v_cache, kv_message = call(
        functools.partial(rotate_kernel, heads_width),
        (
            shaped((144, 256), BF16),
            shaped((256, 128), BF16),
            shaped((256, 128), BF16),
            shaped((4, 272, 256), BF16),
        ),
        [stats, query, key_value, cosine, sine, q_gain.reshape(128, 1), k_gain.reshape(128, 1), marks],
        name="rotate",
    )
    keys = lax.all_to_all(kv_message, ("ya", "yb"), 0, 0, tiled=True)
    q_gots = [
        permute(q_rot, ("yc", "zh"), lambda yc, zh, d=d: (yc ^ (d & 1), zh ^ (d >> 1)))
        for d in (2, 3, 1)
    ]

    give = lax.dynamic_index_in_dim(wo_pair, 1 - c, axis=1, keepdims=False)
    keep = lax.dynamic_index_in_dim(wo_pair, c, axis=1, keepdims=False)
    take = permute(give, ("c",), lambda c: (1 - c,))
    wo_all = lax.all_gather(jnp.stack([keep, take]), ("ya", "yb", "yc"), axis=0, tiled=False)

    mine, mine_lse, *o_messages = call(
        attend_kernel,
        (shaped((128, 256), F32), shaped((8, 256), F32)) + (shaped((144, 256), BF16),) * 3,
        [q_rot] + q_gots + [keys],
        scratch=[pltpu.VMEM((4, 256, 1024), F32)],
        name="attend",
    )
    o_gots = [
        permute(o, ("yc", "zh"), lambda yc, zh, d=d: (yc ^ (d & 1), zh ^ (d >> 1)))
        for d, o in zip((2, 3, 1), o_messages, strict=True)
    ]
    attention = call(merge_kernel, shaped((128, 256), BF16), [mine, mine_lse] + o_gots, name="merge")
    other = permute(attention, ("c",), lambda c: (1 - c,))

    own, *messages = call(
        partial_kernel,
        (shaped((4, 160, 256), F32),) + (shaped((4, 160, 256), BF16),) * 3,
        [attention, other, wo_all],
        scalars=at,
        name="partial",
    )
    gots = [
        permute(part, ("xh", "xl"), lambda xh, xl, j=j: divmod((xh * 2 + xl + j) % 4, 2))
        for j, part in enumerate(messages, 1)
    ]
    own, *messages = call(
        along_z_kernel,
        (shaped((160, 256), F32),) + (shaped((160, 256), BF16),) * 3,
        [own] + gots,
        scalars=at,
        name="along_z",
    )
    mixed = own
    for k, part in enumerate(messages, 1):
        mixed = mixed + permute(part, ("zl",), lambda zl, k=k: ((zl + k) % 4,)).astype(F32)
    hidden_out = (x_t + modulation[2] * mixed).T.astype(BF16)
    return (hidden_out, k_cache, v_cache)


def solution(mesh):
    split = Mesh(mesh.devices.reshape(tuple(SIZES.values())), tuple(SIZES))
    in_specs = (
        P(SEQ, TP),
        P(SEQ),
        P(None, SEQ),
        P(None, None, TP),
        P(SEQ, None, TP),
        P(TP),
        P(TP),
        P(TP, SEQ),
    )
    out_specs = (P(SEQ, TP), P(SEQ, TP), P(SEQ, TP))
    return jax.shard_map(body, mesh=split, in_specs=in_specs, out_specs=out_specs, check_vma=False)
```

```python
import functools
import itertools
import math

import jax
import jax.numpy as jnp
import numpy as np
from jax import lax
from jax.experimental import pallas as pl
from jax.experimental.pallas import tpu as pltpu
from jax.sharding import Mesh
from jax.sharding import PartitionSpec as P

HEAD_DIM = 128
EPSILON = 1e-06
NEG_FILL = -1e30
LOG2E = 1.4426950408889634

SEQ = ("ya", "yb", "yc", "zh")
TP = ("zl", "xh", "xl", "c")
SIZES = {"ya": 2, "yb": 2, "yc": 2, "zh": 2, "zl": 4, "xh": 2, "xl": 2, "c": 2}

F32 = jnp.float32
BF16 = jnp.bfloat16
VMEM_LIMIT = 48 << 20


def permute(value, axes, move):
    sizes = [SIZES[a] for a in axes]
    pairs = []
    for at in itertools.product(*[range(n) for n in sizes]):
        to = move(*at)
        pairs.append((int(np.ravel_multi_index(at, sizes)), int(np.ravel_multi_index(to, sizes))))
    return lax.ppermute(value, axes, pairs)


def contract_first(lhs, rhs):
    return lax.dot_general(lhs, rhs, (((0,), (0,)), ((), ())), preferred_element_type=F32)


def call(kernel, out_shape, operands, scalars=None, scratch=(), name=None, cost=None):
    vmem = pl.BlockSpec(memory_space=pltpu.VMEM)
    smem = pl.BlockSpec(memory_space=pltpu.SMEM)
    specs = ([] if scalars is None else [smem]) + [vmem] * len(operands)
    args = ([] if scalars is None else [scalars]) + list(operands)
    return pl.pallas_call(
        kernel,
        out_shape=out_shape,
        in_specs=specs,
        out_specs=jax.tree.map(lambda _: vmem, out_shape),
        scratch_shapes=list(scratch),
        compiler_params=pltpu.CompilerParams(vmem_limit_bytes=VMEM_LIMIT),
        cost_estimate=cost,
        name=name,
    )(*args)


def shaped(shape, dtype):
    return jax.ShapeDtypeStruct(shape, dtype)


def project_kernel(at, *refs):
    xs, w, out_q, out_kv, stats = refs[:8], refs[8], *refs[9:]
    zl, x, c, zh = at[0], at[1], at[2], at[3]
    total = None
    for i in range(2):
        core = lax.rem(c + i, 2)
        for j in range(4):
            x_from = lax.rem(x - j + 4, 4)
            swap = lax.rem(x_from + zh, 2)
            for k in range(4):
                block = lax.rem(zl - k + 4, 4) * 2 + x_from // 2
                weights = jnp.concatenate([w[block, swap, p, core] for p in range(3)], axis=1)
                term = contract_first(weights, xs[4 * i + j][k])
                total = term if total is None else total + term
    query, key, value = total[:128], total[128:256], total[256:]
    out_q[...] = query
    out_kv[0] = key
    out_kv[1] = value
    rows = []
    for part in (query, key):
        row = jnp.sum(part * part, axis=0, keepdims=True)
        rows += [row[:, :128], row[:, 128:]]
    packed = jnp.concatenate(rows + [jnp.zeros((4, 128), F32)], axis=0)
    for t in range(stats.shape[0]):
        stats[t] = packed


def rotate_kernel(width, got, q, kv, cosine, sine, qg, kg, marks, q_out, k_cache, v_cache, message):
    totals = jnp.sum(got[...], axis=0)
    even = lax.rem(lax.broadcasted_iota(jnp.int32, (HEAD_DIM, 256), 0), 2) == 0
    cos, sin = cosine[...], sine[...]

    def rotated(value, gain, row):
        factor = jnp.concatenate([totals[row : row + 1], totals[row + 1 : row + 2]], axis=1)
        factor = lax.rsqrt(factor / width + EPSILON)
        normed = value * factor * gain
        after = pltpu.roll(normed, HEAD_DIM - 1, 0)
        before = pltpu.roll(normed, 1, 0)
        partner = jnp.where(even, -after, before)
        return normed * cos + partner * sin

    extra = marks[...].astype(BF16)
    q_out[:128] = rotated(q[...], qg[...], 0).astype(BF16)
    q_out[128:144] = extra
    k_rot = rotated(kv[0], kg[...], 2)
    value = kv[1]
    k_low = k_rot.astype(BF16)
    v_low = value.astype(BF16)
    for t in range(message.shape[0]):
        message[t, :128] = k_low
        message[t, 128:256] = v_low
        message[t, 256:272] = extra
    k_cache[...] = k_rot.T.astype(BF16)
    v_cache[...] = value.T.astype(BF16)


def attend_kernel(q, q1, q2, q3, keys, mine, mine_lse, m1, m2, m3, held):
    count = keys.shape[0]
    scale = LOG2E / math.sqrt(HEAD_DIM)
    parts = (q, q1, q2, q3)
    q_low = jnp.concatenate([part[:128] for part in parts], axis=1)
    seg_q = jnp.concatenate([part[128:144] for part in parts], axis=1).astype(F32)[:1]
    top = None
    for b in range(count):
        seg_k = keys[b, 256:272].astype(F32).T[:, :1]
        scores = contract_first(keys[b, :128], q_low) * scale
        scores = jnp.where(seg_k == seg_q, scores, NEG_FILL)
        held[b] = scores
        here = jnp.max(scores, axis=0, keepdims=True)
        top = here if top is None else jnp.maximum(top, here)
    top = jnp.maximum(top, -1e20)
    total = jnp.zeros((1, 1024), F32)
    weighted = jnp.zeros((HEAD_DIM, 1024), F32)
    for b in range(count):
        weights = jnp.exp2(held[b] - top)
        total = total + jnp.sum(weights, axis=0, keepdims=True)
        weighted = weighted + jnp.dot(
            keys[b, 128:256], weights.astype(BF16), preferred_element_type=F32
        )
    some = total > 0.0
    safe = jnp.where(some, total, 1.0)
    out = weighted / safe
    lse = jnp.where(some, top + jnp.log2(safe), NEG_FILL)
    mine[...] = out[:, :256]
    mine_lse[...] = jnp.broadcast_to(lse[:, :256], (8, 256))
    for d, message in enumerate((m1, m2, m3), 1):
        here = slice(256 * d, 256 * d + 256)
        high = lse[:, here].astype(BF16)
        rest = lse[:, here] - high.astype(F32)
        middle = rest.astype(BF16)
        low = (rest - middle.astype(F32)).astype(BF16)
        message[:128] = out[:, here].astype(BF16)
        message[128:144] = jnp.concatenate(
            [high.astype(F32), middle.astype(F32), low.astype(F32), jnp.zeros((13, 256), F32)], axis=0
        ).astype(BF16)


def merge_kernel(mine, mine_lse, *refs):
    gots, out = refs[:-1], refs[-1]
    parts = [(mine_lse[0:1], mine[...])]
    for got in gots:
        rows = got[128:144].astype(F32)
        parts.append((rows[0:1] + rows[1:2] + rows[2:3], got[:128].astype(F32)))
    top = functools.reduce(jnp.maximum, [lse for lse, _ in parts])
    weights = [jnp.exp2(lse - top) for lse, _ in parts]
    total = sum(weights[1:], weights[0])
    value = None
    for weight, (_, part) in zip(weights, parts, strict=True):
        term = part * (weight / total)
        value = term if value is None else value + term
    out[...] = value.astype(BF16)


def partial_kernel(at, heads, w, mine, *messages):
    zl, x, zh = at[0], at[1], at[3]
    for j in range(4):
        x_to = lax.rem(x + j, 4)
        total = None
        for k in range(4):
            z_from = lax.rem(zl - k + 4, 4)
            term = jnp.dot(w[z_from * 2 + x_to // 2, lax.rem(x_to + zh, 2)], heads[k], preferred_element_type=F32)
            total = term if total is None else total + term
        if j == 0:
            mine[...] = total
        else:
            messages[j - 1][...] = total.astype(BF16)


def halves_kernel(at, own, *refs):
    gots, mine, message, held = refs[:3], *refs[3:]
    c = at[2]
    total = own[...]
    for got in gots:
        total = total + got[...].astype(F32)
    held[0] = total[:160]
    held[1] = total[160:]
    mine[...] = held[c]
    message[...] = held[1 - c]


def body(hidden_in, seg_ids, positions, mod_table, w_qkv, q_gain, k_gain, w_out):
    tok_rows, feat_local = hidden_in.shape
    model_width = feat_local * 32
    heads_width = 4096
    zl, c, zh = lax.axis_index("zl"), lax.axis_index("c"), lax.axis_index("zh")
    x = lax.axis_index("xh") * 2 + lax.axis_index("xl")
    at = jnp.stack([zl, x, c, zh]).astype(jnp.int32)

    w_local = jnp.transpose(w_qkv, (1, 0, 2))
    wo_local = w_out.T
    got = permute(jnp.concatenate([w_local, wo_local[None]], axis=0), ("zh",), lambda zh: (1 - zh,))

    x_t = hidden_in.T.astype(F32)
    sums = jnp.stack([jnp.sum(x_t, axis=0), jnp.sum(x_t * x_t, axis=0)]).reshape(4, 128)
    sums = jnp.concatenate([sums, jnp.zeros((4, 128), F32)], axis=0)
    sums = jnp.broadcast_to(sums, (32, 8, 128))
    segment_count = mod_table.shape[0]
    onehot = (seg_ids[None, :] == jnp.arange(segment_count, dtype=jnp.int32)[:, None]).astype(F32)
    modulation = lax.dot_general(
        mod_table.reshape(segment_count, 3 * feat_local),
        onehot,
        (((0,), (0,)), ((), ())),
        precision=lax.Precision.HIGHEST,
    ).reshape(3, feat_local, tok_rows)
    part_width = HEAD_DIM // 6
    widths = (HEAD_DIM - 4 * part_width, 2 * part_width, 2 * part_width)
    angles = []
    for axis_number in range(3):
        width = widths[axis_number]
        exponent = jnp.arange(0, width, 2, dtype=F32) / width
        frequency = jnp.repeat(1.0 / 10000.0**exponent, 2)
        angles.append(positions[axis_number].astype(F32)[None, :] * frequency[:, None])
    angle = jnp.concatenate(angles, axis=0)
    cosine, sine = jnp.cos(angle), jnp.sin(angle)
    marks = jnp.broadcast_to(seg_ids[None, :].astype(F32), (16, tok_rows))
    sums, got, modulation, cosine, sine, marks = lax.optimization_barrier(
        (sums, got, modulation, cosine, sine, marks)
    )
    sums = lax.all_to_all(sums, TP, 0, 0, tiled=True)
    w_all = lax.all_gather(jnp.stack([w_local, got[:3]]), ("ya", "yb", "yc"), axis=0, tiled=False)
    w_all = w_all.reshape(8, 2, 3, 2, 160, 128)
    sums = jnp.sum(sums, axis=0)[:4].reshape(2, tok_rows)
    mean_value = sums[0:1] / model_width
    variance = sums[1:2] / model_width - mean_value * mean_value
    normed = (x_t - mean_value) * lax.rsqrt(variance + EPSILON)
    packet = (normed * (1.0 + modulation[1]) + modulation[0]).astype(BF16)
    packet, wo_pair = lax.optimization_barrier((packet, jnp.stack([wo_local, got[3]])))

    held = jnp.stack(
        [packet]
        + [permute(packet, ("zl",), lambda zl, k=k: ((zl + k) % 4,)) for k in range(1, 4)]
    )
    along_x = [held] + [
        permute(held, ("xh", "xl"), lambda xh, xl, j=j: divmod((xh * 2 + xl + j) % 4, 2))
        for j in range(1, 4)
    ]
    wo_turned = permute(
        wo_pair, ("ya", "yb", "zl"), lambda ya, yb, zl: (zl >> 1, zl & 1, ya * 2 + yb)
    )
    along_x[2], wo_turned = lax.optimization_barrier((along_x[2], wo_turned))
    swapped = [permute(part, ("c",), lambda c: (1 - c,)) for part in along_x]

    query, key_value, stats = call(
        project_kernel,
        (shaped((128, 256), F32), shaped((2, 128, 256), F32), shaped((32, 8, 128), F32)),
        along_x + swapped + [w_all],
        scalars=at,
        name="project",
        cost=pl.CostEstimate(flops=2 * 256 * 5120 * 384, bytes_accessed=6 << 20, transcendentals=0),
    )
    stats = lax.all_to_all(stats, TP, 0, 0, tiled=True)
    stats, wo_turned = lax.optimization_barrier((stats, wo_turned))
    wo_all = lax.all_gather(wo_turned, ("ya", "yb", "yc"), axis=0, tiled=False)
    q_rot, k_cache, v_cache, kv_message = call(
        functools.partial(rotate_kernel, heads_width),
        (
            shaped((144, 256), BF16),
            shaped((256, 128), BF16),
            shaped((256, 128), BF16),
            shaped((4, 272, 256), BF16),
        ),
        [stats, query, key_value, cosine, sine, q_gain.reshape(128, 1), k_gain.reshape(128, 1), marks],
        name="rotate",
    )
    keys = lax.all_to_all(kv_message, ("ya", "yb"), 0, 0, tiled=True)
    q_gots = [
        permute(q_rot, ("yc", "zh"), lambda yc, zh, d=d: (yc ^ (d & 1), zh ^ (d >> 1)))
        for d in (2, 3, 1)
    ]

    mine, mine_lse, *o_messages = call(
        attend_kernel,
        (shaped((128, 256), F32), shaped((8, 256), F32)) + (shaped((144, 256), BF16),) * 3,
        [q_rot] + q_gots + [keys],
        scratch=[pltpu.VMEM((4, 256, 1024), F32)],
        name="attend",
    )
    o_gots = [
        permute(o, ("yc", "zh"), lambda yc, zh, d=d: (yc ^ (d & 1), zh ^ (d >> 1)))
        for d, o in zip((2, 3, 1), o_messages, strict=True)
    ]
    attention = call(merge_kernel, shaped((128, 256), BF16), [mine, mine_lse] + o_gots, name="merge")
    by_z = [attention] + [
        permute(attention, ("zl",), lambda zl, k=k: ((zl + k) % 4,)) for k in range(1, 4)
    ]
    by_z = jnp.stack(by_z)
    own, *partials = call(
        partial_kernel,
        (shaped((320, 256), F32),) + (shaped((320, 256), BF16),) * 3,
        [by_z, wo_all],
        scalars=at,
        name="partial",
    )
    gots = [
        permute(part, ("xh", "xl"), lambda xh, xl, j=j: divmod((xh * 2 + xl + j) % 4, 2))
        for j, part in enumerate(partials, 1)
    ]
    out_mine, out_message = call(
        halves_kernel,
        (shaped((160, 256), F32), shaped((160, 256), F32)),
        [own] + gots,
        scalars=at,
        scratch=[pltpu.VMEM((2, 160, 256), F32)],
        name="halves",
    )
    out_got = permute(out_message, ("c",), lambda c: (1 - c,))
    mixed = out_mine + out_got
    hidden_out = (x_t + modulation[2] * mixed).T.astype(BF16)
    return (hidden_out, k_cache, v_cache)


def solution(mesh):
    split = Mesh(mesh.devices.reshape(tuple(SIZES.values())), tuple(SIZES))
    in_specs = (
        P(SEQ, TP),
        P(SEQ),
        P(None, SEQ),
        P(None, None, TP),
        P(SEQ, None, TP),
        P(TP),
        P(TP),
        P(TP, SEQ),
    )
    out_specs = (P(SEQ, TP), P(SEQ, TP), P(SEQ, TP))
    return jax.shard_map(body, mesh=split, in_specs=in_specs, out_specs=out_specs, check_vma=False)
```

```python
import functools
import itertools
import math

import jax
import jax.numpy as jnp
import numpy as np
from jax import lax
from jax.experimental import pallas as pl
from jax.experimental.pallas import tpu as pltpu
from jax.sharding import Mesh
from jax.sharding import PartitionSpec as P

HEAD_DIM = 128
EPSILON = 1e-06
NEG_FILL = -1e30
LOG2E = 1.4426950408889634

SEQ = ("ya", "yb", "yc", "zh")
TP = ("zl", "xh", "xl", "c")
SIZES = {"ya": 2, "yb": 2, "yc": 2, "zh": 2, "zl": 4, "xh": 2, "xl": 2, "c": 2}

F32 = jnp.float32
BF16 = jnp.bfloat16
VMEM_LIMIT = 48 << 20


def permute(value, axes, move):
    sizes = [SIZES[a] for a in axes]
    pairs = []
    for at in itertools.product(*[range(n) for n in sizes]):
        to = move(*at)
        pairs.append((int(np.ravel_multi_index(at, sizes)), int(np.ravel_multi_index(to, sizes))))
    return lax.ppermute(value, axes, pairs)


def contract_first(lhs, rhs):
    return lax.dot_general(lhs, rhs, (((0,), (0,)), ((), ())), preferred_element_type=F32)


def call(kernel, out_shape, operands, scalars=None, scratch=(), name=None, cost=None):
    vmem = pl.BlockSpec(memory_space=pltpu.VMEM)
    smem = pl.BlockSpec(memory_space=pltpu.SMEM)
    specs = ([] if scalars is None else [smem]) + [vmem] * len(operands)
    args = ([] if scalars is None else [scalars]) + list(operands)
    return pl.pallas_call(
        kernel,
        out_shape=out_shape,
        in_specs=specs,
        out_specs=jax.tree.map(lambda _: vmem, out_shape),
        scratch_shapes=list(scratch),
        compiler_params=pltpu.CompilerParams(vmem_limit_bytes=VMEM_LIMIT),
        cost_estimate=cost,
        name=name,
    )(*args)


def shaped(shape, dtype):
    return jax.ShapeDtypeStruct(shape, dtype)


def project_kernel(at, mine, theirs, w, out_q, out_kv, stats):
    c = at[0]
    total = None
    for i, held in enumerate((mine, theirs)):
        core = lax.rem(c + i, 2)
        for x in range(4):
            for z in range(4):
                block, low = 2 * z + x // 2, x % 2
                weights = jnp.concatenate([w[block, low, p, core] for p in range(3)], axis=1)
                term = contract_first(weights, held[x, z])
                total = term if total is None else total + term
    query, key, value = total[:128], total[128:256], total[256:]
    out_q[...] = query
    out_kv[0] = key
    out_kv[1] = value
    rows = []
    for part in (query, key):
        row = jnp.sum(part * part, axis=0, keepdims=True)
        rows += [row[:, :128], row[:, 128:]]
    packed = jnp.concatenate(rows + [jnp.zeros((4, 128), F32)], axis=0)
    for t in range(stats.shape[0]):
        stats[t] = packed


def rotate_kernel(width, got, q, kv, cosine, sine, qg, kg, marks, q_out, k_cache, v_cache, message):
    totals = jnp.sum(got[...], axis=0)
    even = lax.rem(lax.broadcasted_iota(jnp.int32, (HEAD_DIM, 256), 0), 2) == 0
    cos, sin = cosine[...], sine[...]

    def rotated(value, gain, row):
        factor = jnp.concatenate([totals[row : row + 1], totals[row + 1 : row + 2]], axis=1)
        factor = lax.rsqrt(factor / width + EPSILON)
        normed = value * factor * gain
        after = pltpu.roll(normed, HEAD_DIM - 1, 0)
        before = pltpu.roll(normed, 1, 0)
        partner = jnp.where(even, -after, before)
        return normed * cos + partner * sin

    extra = marks[...].astype(BF16)
    q_low = rotated(q[...], qg[...], 0).astype(BF16)
    for t in range(q_out.shape[0]):
        q_out[t, :128] = q_low
        q_out[t, 128:144] = extra
    k_rot = rotated(kv[0], kg[...], 2)
    value = kv[1]
    k_low = k_rot.astype(BF16)
    v_low = value.astype(BF16)
    for t in range(message.shape[0]):
        message[t, :128] = k_low
        message[t, 128:256] = v_low
        message[t, 256:272] = extra
    k_cache[...] = k_rot.T.astype(BF16)
    v_cache[...] = value.T.astype(BF16)


def attend_kernel(q, keys, messages, held):
    count = keys.shape[0]
    scale = LOG2E / math.sqrt(HEAD_DIM)
    q_low = jnp.concatenate([q[d, :128] for d in range(4)], axis=1)
    seg_q = jnp.concatenate([q[d, 128:144] for d in range(4)], axis=1).astype(F32)[:1]
    top = None
    for b in range(count):
        seg_k = keys[b, 256:272].astype(F32).T[:, :1]
        scores = contract_first(keys[b, :128], q_low) * scale
        scores = jnp.where(seg_k == seg_q, scores, NEG_FILL)
        held[b] = scores
        here = jnp.max(scores, axis=0, keepdims=True)
        top = here if top is None else jnp.maximum(top, here)
    top = jnp.maximum(top, -1e20)
    total = jnp.zeros((1, 1024), F32)
    weighted = jnp.zeros((HEAD_DIM, 1024), F32)
    for b in range(count):
        weights = jnp.exp2(held[b] - top)
        total = total + jnp.sum(weights, axis=0, keepdims=True)
        weighted = weighted + jnp.dot(
            keys[b, 128:256], weights.astype(BF16), preferred_element_type=F32
        )
    some = total > 0.0
    safe = jnp.where(some, total, 1.0)
    out = weighted / safe
    lse = jnp.where(some, top + jnp.log2(safe), NEG_FILL)
    high = lse.astype(BF16)
    rest = lse - high.astype(F32)
    middle = rest.astype(BF16)
    low = (rest - middle.astype(F32)).astype(BF16)
    rows = jnp.concatenate(
        [high.astype(F32), middle.astype(F32), low.astype(F32), jnp.zeros((13, 1024), F32)], axis=0
    ).astype(BF16)
    for d in range(4):
        here = slice(256 * d, 256 * d + 256)
        messages[d, :128] = out[:, here].astype(BF16)
        messages[d, 128:144] = rows[:, here]


def merge_kernel(got, out):
    lses, parts = [], []
    for d in range(4):
        rows = got[d, 128:144].astype(F32)
        lses.append(rows[0:1] + rows[1:2] + rows[2:3])
        parts.append(got[d, :128].astype(F32))
    top = functools.reduce(jnp.maximum, lses)
    weights = [jnp.exp2(lse - top) for lse in lses]
    total = sum(weights[1:], weights[0])
    value = None
    for weight, part in zip(weights, parts, strict=True):
        term = part * (weight / total)
        value = term if value is None else value + term
    value = value.astype(BF16)
    for t in range(out.shape[0]):
        out[t] = value


def partial_kernel(heads, w, messages):
    for x in range(4):
        total = None
        for z in range(4):
            term = jnp.dot(w[2 * z + x // 2, x % 2], heads[z], preferred_element_type=F32)
            total = term if total is None else total + term
        messages[2 * x] = total[:160].astype(BF16)
        messages[2 * x + 1] = total[160:].astype(BF16)


def exchange(value, axes):
    return lax.all_to_all(value, axes, 0, 0, tiled=True)


def spread(value, axes):
    count = math.prod(SIZES[a] for a in axes)
    return exchange(jnp.broadcast_to(value, (count,) + value.shape), axes)


def body(hidden_in, seg_ids, positions, mod_table, w_qkv, q_gain, k_gain, w_out):
    tok_rows, feat_local = hidden_in.shape
    model_width = feat_local * 32
    heads_width = 4096
    at = jnp.stack([lax.axis_index("c")]).astype(jnp.int32)

    local = jnp.concatenate([jnp.transpose(w_qkv, (1, 0, 2)), w_out.T[None]], axis=0)
    pair = spread(local, ("zh",))

    x_t = hidden_in.T.astype(F32)
    sums = jnp.stack([jnp.sum(x_t, axis=0), jnp.sum(x_t * x_t, axis=0)]).reshape(4, 128)
    sums = jnp.concatenate([sums, jnp.zeros((4, 128), F32)], axis=0)
    sums = jnp.broadcast_to(sums, (32, 8, 128))
    segment_count = mod_table.shape[0]
    onehot = (seg_ids[None, :] == jnp.arange(segment_count, dtype=jnp.int32)[:, None]).astype(F32)
    modulation = lax.dot_general(
        mod_table.reshape(segment_count, 3 * feat_local),
        onehot,
        (((0,), (0,)), ((), ())),
        precision=lax.Precision.HIGHEST,
    ).reshape(3, feat_local, tok_rows)
    part_width = HEAD_DIM // 6
    widths = (HEAD_DIM - 4 * part_width, 2 * part_width, 2 * part_width)
    angles = []
    for axis_number in range(3):
        width = widths[axis_number]
        exponent = jnp.arange(0, width, 2, dtype=F32) / width
        frequency = jnp.repeat(1.0 / 10000.0**exponent, 2)
        angles.append(positions[axis_number].astype(F32)[None, :] * frequency[:, None])
    angle = jnp.concatenate(angles, axis=0)
    cosine, sine = jnp.cos(angle), jnp.sin(angle)
    marks = jnp.broadcast_to(seg_ids[None, :].astype(F32), (16, tok_rows))
    sums, pair, modulation, cosine, sine, marks = lax.optimization_barrier(
        (sums, pair, modulation, cosine, sine, marks)
    )
    sums = exchange(sums, TP)
    w_all = lax.all_gather(pair[:, :3], ("ya", "yb", "yc"), axis=0, tiled=False)
    w_all = w_all.reshape(8, 2, 3, 2, 160, 128)
    sums = jnp.sum(sums, axis=0)[:4].reshape(2, tok_rows)
    mean_value = sums[0:1] / model_width
    variance = sums[1:2] / model_width - mean_value * mean_value
    normed = (x_t - mean_value) * lax.rsqrt(variance + EPSILON)
    packet = (normed * (1.0 + modulation[1]) + modulation[0]).astype(BF16)

    held = spread(spread(packet, ("zl",)), ("xh", "xl"))
    theirs = permute(held, ("c",), lambda c: (1 - c,))

    query, key_value, stats = call(
        project_kernel,
        (shaped((128, 256), F32), shaped((2, 128, 256), F32), shaped((32, 8, 128), F32)),
        [held, theirs, w_all],
        scalars=at,
        name="project",
        cost=pl.CostEstimate(flops=2 * 256 * 5120 * 384, bytes_accessed=6 << 20, transcendentals=0),
    )
    wo_pair, stats = lax.optimization_barrier((pair[:, 3], stats))
    stats = exchange(stats, TP)
    wo_turned = permute(
        wo_pair, ("ya", "yb", "zl"), lambda ya, yb, zl: (zl >> 1, zl & 1, ya * 2 + yb)
    )
    stats, wo_turned = lax.optimization_barrier((stats, wo_turned))
    wo_all = lax.all_gather(wo_turned, ("ya", "yb", "yc"), axis=0, tiled=False)

    q_message, k_cache, v_cache, kv_message = call(
        functools.partial(rotate_kernel, heads_width),
        (
            shaped((4, 144, 256), BF16),
            shaped((256, 128), BF16),
            shaped((256, 128), BF16),
            shaped((4, 272, 256), BF16),
        ),
        [stats, query, key_value, cosine, sine, q_gain.reshape(128, 1), k_gain.reshape(128, 1), marks],
        name="rotate",
    )
    keys = exchange(kv_message, ("ya", "yb"))
    queries = exchange(q_message, ("yc", "zh"))
    o_messages = call(
        attend_kernel,
        shaped((4, 144, 256), BF16),
        [queries, keys],
        scratch=[pltpu.VMEM((4, 256, 1024), F32)],
        name="attend",
    )
    heads = call(
        merge_kernel, shaped((4, 128, 256), BF16), [exchange(o_messages, ("yc", "zh"))], name="merge"
    )
    partials = call(
        partial_kernel, shaped((8, 160, 256), BF16), [exchange(heads, ("zl",)), wo_all], name="partial"
    )
    mixed = jnp.sum(exchange(partials, ("xh", "xl", "c")).astype(F32), axis=0)
    hidden_out = (x_t + modulation[2] * mixed).T.astype(BF16)
    return (hidden_out, k_cache, v_cache)


def solution(mesh):
    split = Mesh(mesh.devices.reshape(tuple(SIZES.values())), tuple(SIZES))
    in_specs = (
        P(SEQ, TP),
        P(SEQ),
        P(None, SEQ),
        P(None, None, TP),
        P(SEQ, None, TP),
        P(TP),
        P(TP),
        P(TP, SEQ),
    )
    out_specs = (P(SEQ, TP), P(SEQ, TP), P(SEQ, TP))
    return jax.shard_map(body, mesh=split, in_specs=in_specs, out_specs=out_specs, check_vma=False)
```

```python
import functools
import itertools
import math

import jax
import jax.numpy as jnp
import numpy as np
from jax import lax
from jax.experimental import pallas as pl
from jax.experimental.pallas import tpu as pltpu
from jax.sharding import Mesh
from jax.sharding import PartitionSpec as P

HEAD_DIM = 128
EPSILON = 1e-06
NEG_FILL = -1e30
LOG2E = 1.4426950408889634

SEQ = ("ya", "yb", "yc", "zh")
TP = ("zl", "xh", "xl", "c")
SIZES = {"ya": 2, "yb": 2, "yc": 2, "zh": 2, "zl": 4, "xh": 2, "xl": 2, "c": 2}

F32 = jnp.float32
BF16 = jnp.bfloat16
VMEM_LIMIT = 48 << 20


def permute(value, axes, move):
    sizes = [SIZES[a] for a in axes]
    pairs = []
    for at in itertools.product(*[range(n) for n in sizes]):
        to = move(*at)
        pairs.append((int(np.ravel_multi_index(at, sizes)), int(np.ravel_multi_index(to, sizes))))
    return lax.ppermute(value, axes, pairs)


def contract_first(lhs, rhs):
    return lax.dot_general(lhs, rhs, (((0,), (0,)), ((), ())), preferred_element_type=F32)


def call(kernel, out_shape, operands, scalars=None, scratch=(), name=None, cost=None):
    vmem = pl.BlockSpec(memory_space=pltpu.VMEM)
    smem = pl.BlockSpec(memory_space=pltpu.SMEM)
    specs = ([] if scalars is None else [smem]) + [vmem] * len(operands)
    args = ([] if scalars is None else [scalars]) + list(operands)
    return pl.pallas_call(
        kernel,
        out_shape=out_shape,
        in_specs=specs,
        out_specs=jax.tree.map(lambda _: vmem, out_shape),
        scratch_shapes=list(scratch),
        compiler_params=pltpu.CompilerParams(vmem_limit_bytes=VMEM_LIMIT),
        cost_estimate=cost,
        name=name,
    )(*args)


def shaped(shape, dtype):
    return jax.ShapeDtypeStruct(shape, dtype)


def project_kernel(at, mine, theirs, w, out_q, out_kv, stats):
    c = at[0]
    total = None
    for i, held in enumerate((mine, theirs)):
        core = lax.rem(c + i, 2)
        for x in range(4):
            for z in range(4):
                block, low = 2 * z + x // 2, x % 2
                weights = jnp.concatenate([w[block, low, p, core] for p in range(3)], axis=1)
                term = contract_first(weights, held[x, z])
                total = term if total is None else total + term
    query, key, value = total[:128], total[128:256], total[256:]
    out_q[...] = query
    out_kv[0] = key
    out_kv[1] = value
    rows = []
    for part in (query, key):
        row = jnp.sum(part * part, axis=0, keepdims=True)
        rows += [row[:, :128], row[:, 128:]]
    packed = jnp.concatenate(rows + [jnp.zeros((4, 128), F32)], axis=0)
    for t in range(stats.shape[0]):
        stats[t] = packed


def rotate_kernel(width, got, q, kv, cosine, sine, qg, kg, marks, q_out, k_cache, v_cache, message):
    totals = jnp.sum(got[...], axis=0)
    even = lax.rem(lax.broadcasted_iota(jnp.int32, (HEAD_DIM, 256), 0), 2) == 0
    cos, sin = cosine[...], sine[...]

    def rotated(value, gain, row):
        factor = jnp.concatenate([totals[row : row + 1], totals[row + 1 : row + 2]], axis=1)
        factor = lax.rsqrt(factor / width + EPSILON)
        normed = value * factor * gain
        after = pltpu.roll(normed, HEAD_DIM - 1, 0)
        before = pltpu.roll(normed, 1, 0)
        partner = jnp.where(even, -after, before)
        return normed * cos + partner * sin

    extra = marks[...].astype(BF16)
    q_low = rotated(q[...], qg[...], 0).astype(BF16)
    q_out[:128] = q_low
    q_out[128:144] = extra
    k_rot = rotated(kv[0], kg[...], 2)
    value = kv[1]
    k_low = k_rot.astype(BF16)
    v_low = value.astype(BF16)
    for t in range(message.shape[0]):
        message[t, :128] = k_low
        message[t, 128:256] = v_low
        message[t, 256:272] = extra
    k_cache[...] = k_rot.T.astype(BF16)
    v_cache[...] = value.T.astype(BF16)


def attend_kernel(order, at, q0, q1, q2, q3, keys, messages, held):
    count = keys.shape[0]
    scale = LOG2E / math.sqrt(HEAD_DIM)
    parts = (q0, q1, q2, q3)
    q_low = jnp.concatenate([q[:128] for q in parts], axis=1)
    seg_q = jnp.concatenate([q[128:144] for q in parts], axis=1).astype(F32)[:1]
    top = None
    for b in range(count):
        seg_k = keys[b, 256:272].astype(F32).T[:, :1]
        scores = contract_first(keys[b, :128], q_low) * scale
        scores = jnp.where(seg_k == seg_q, scores, NEG_FILL)
        held[b] = scores
        here = jnp.max(scores, axis=0, keepdims=True)
        top = here if top is None else jnp.maximum(top, here)
    top = jnp.maximum(top, -1e20)
    total = jnp.zeros((1, 1024), F32)
    weighted = jnp.zeros((HEAD_DIM, 1024), F32)
    for b in range(count):
        weights = jnp.exp2(held[b] - top)
        total = total + jnp.sum(weights, axis=0, keepdims=True)
        weighted = weighted + jnp.dot(
            keys[b, 128:256], weights.astype(BF16), preferred_element_type=F32
        )
    some = total > 0.0
    safe = jnp.where(some, total, 1.0)
    out = weighted / safe
    lse = jnp.where(some, top + jnp.log2(safe), NEG_FILL)
    high = lse.astype(BF16)
    rest = lse - high.astype(F32)
    middle = rest.astype(BF16)
    low = (rest - middle.astype(F32)).astype(BF16)
    rows = jnp.concatenate(
        [high.astype(F32), middle.astype(F32), low.astype(F32), jnp.zeros((13, 1024), F32)], axis=0
    ).astype(BF16)
    for place, d in enumerate(order):
        here = slice(256 * place, 256 * place + 256)
        target = jnp.bitwise_xor(at[1], d)
        for core in range(2):
            messages[2 * target + core, :128] = out[:, here].astype(BF16)
            messages[2 * target + core, 128:144] = rows[:, here]


def merge_kernel(got, out):
    for head in range(2):
        lses, parts = [], []
        for d in range(4):
            rows = got[2 * d + head, 128:144].astype(F32)
            lses.append(rows[0:1] + rows[1:2] + rows[2:3])
            parts.append(got[2 * d + head, :128].astype(F32))
        top = functools.reduce(jnp.maximum, lses)
        weights = [jnp.exp2(lse - top) for lse in lses]
        total = sum(weights[1:], weights[0])
        value = None
        for weight, part in zip(weights, parts, strict=True):
            term = part * (weight / total)
            value = term if value is None else value + term
        out[128 * head : 128 * head + 128] = value.astype(BF16)


def partial_kernel(heads, w, messages):
    both = heads[...]
    for x in range(4):
        for z in range(4):
            block, low = 2 * z + x // 2, x % 2
            weights = jnp.concatenate([w[block, 0, low], w[block, 1, low]], axis=1)
            messages[x, z] = jnp.dot(weights, both, preferred_element_type=F32).astype(BF16)


def along_x_kernel(got, out):
    for z in range(4):
        total = got[0, z].astype(F32)
        for x in range(1, 4):
            total = total + got[x, z].astype(F32)
        out[z] = total.astype(BF16)


def exchange(value, axes):
    return lax.all_to_all(value, axes, 0, 0, tiled=True)


def spread(value, axes):
    count = math.prod(SIZES[a] for a in axes)
    return exchange(jnp.broadcast_to(value, (count,) + value.shape), axes)


def body(hidden_in, seg_ids, positions, mod_table, w_qkv, q_gain, k_gain, w_out):
    tok_rows, feat_local = hidden_in.shape
    model_width = feat_local * 32
    heads_width = 4096
    at = jnp.stack(
        [lax.axis_index("c"), lax.axis_index("yc") * 2 + lax.axis_index("zh")]
    ).astype(jnp.int32)

    local = jnp.concatenate([jnp.transpose(w_qkv, (1, 0, 2)), w_out.T[None]], axis=0)
    pair = spread(local, ("zh",))

    x_t = hidden_in.T.astype(F32)
    sums = jnp.stack([jnp.sum(x_t, axis=0), jnp.sum(x_t * x_t, axis=0)]).reshape(4, 128)
    sums = jnp.concatenate([sums, jnp.zeros((4, 128), F32)], axis=0)
    sums = jnp.broadcast_to(sums, (32, 8, 128))
    segment_count = mod_table.shape[0]
    onehot = (seg_ids[None, :] == jnp.arange(segment_count, dtype=jnp.int32)[:, None]).astype(F32)
    modulation = lax.dot_general(
        mod_table.reshape(segment_count, 3 * feat_local),
        onehot,
        (((0,), (0,)), ((), ())),
        precision=lax.Precision.HIGHEST,
    ).reshape(3, feat_local, tok_rows)
    part_width = HEAD_DIM // 6
    widths = (HEAD_DIM - 4 * part_width, 2 * part_width, 2 * part_width)
    angles = []
    for axis_number in range(3):
        width = widths[axis_number]
        exponent = jnp.arange(0, width, 2, dtype=F32) / width
        frequency = jnp.repeat(1.0 / 10000.0**exponent, 2)
        angles.append(positions[axis_number].astype(F32)[None, :] * frequency[:, None])
    angle = jnp.concatenate(angles, axis=0)
    cosine, sine = jnp.cos(angle), jnp.sin(angle)
    marks = jnp.broadcast_to(seg_ids[None, :].astype(F32), (16, tok_rows))
    sums, pair, modulation, cosine, sine, marks = lax.optimization_barrier(
        (sums, pair, modulation, cosine, sine, marks)
    )
    sums = exchange(sums, TP)
    w_all = lax.all_gather(pair[:, :3], ("ya", "yb", "yc"), axis=0, tiled=False)
    w_all = w_all.reshape(8, 2, 3, 2, 160, 128)
    wo_pair = jnp.swapaxes(pair[:, 3].reshape(2, 2, 160, 128), 0, 1)
    wo_all = lax.all_gather(exchange(wo_pair, ("c",)), ("ya", "yb", "yc"), axis=0, tiled=False)
    sums = jnp.sum(sums, axis=0)[:4].reshape(2, tok_rows)
    mean_value = sums[0:1] / model_width
    variance = sums[1:2] / model_width - mean_value * mean_value
    normed = (x_t - mean_value) * lax.rsqrt(variance + EPSILON)
    packet = (normed * (1.0 + modulation[1]) + modulation[0]).astype(BF16)

    held = spread(spread(packet, ("zl",)), ("xh", "xl"))
    theirs = permute(held, ("c",), lambda c: (1 - c,))

    query, key_value, stats = call(
        project_kernel,
        (shaped((128, 256), F32), shaped((2, 128, 256), F32), shaped((32, 8, 128), F32)),
        [held, theirs, w_all],
        scalars=at,
        name="project",
        cost=pl.CostEstimate(flops=2 * 256 * 5120 * 384, bytes_accessed=6 << 20, transcendentals=0),
    )
    stats = exchange(stats, TP)
    q_message, k_cache, v_cache, kv_message = call(
        functools.partial(rotate_kernel, heads_width),
        (
            shaped((144, 256), BF16),
            shaped((256, 128), BF16),
            shaped((256, 128), BF16),
            shaped((4, 272, 256), BF16),
        ),
        [stats, query, key_value, cosine, sine, q_gain.reshape(128, 1), k_gain.reshape(128, 1), marks],
        name="rotate",
    )
    keys = exchange(kv_message, ("ya", "yb"))
    order = (0, 1, 3, 2)
    queries = [q_message] + [
        permute(q_message, ("yc", "zh"), lambda yc, zh, d=d: (yc ^ (d >> 1), zh ^ (d & 1)))
        for d in order[1:]
    ]
    o_messages = call(
        functools.partial(attend_kernel, order),
        shaped((8, 144, 256), BF16),
        queries + [keys],
        scalars=at,
        scratch=[pltpu.VMEM((4, 256, 1024), F32)],
        name="attend",
    )
    heads = call(
        merge_kernel, shaped((256, 256), BF16), [exchange(o_messages, ("yc", "zh", "c"))], name="merge"
    )
    partials = call(partial_kernel, shaped((4, 4, 160, 256), BF16), [heads, wo_all], name="partial")
    partials = call(
        along_x_kernel,
        shaped((4, 160, 256), BF16),
        [exchange(partials, ("xh", "xl"))],
        name="along_x",
    )
    mixed = jnp.sum(exchange(partials, ("zl",)).astype(F32), axis=0)
    hidden_out = (x_t + modulation[2] * mixed).T.astype(BF16)
    return (hidden_out, k_cache, v_cache)


def solution(mesh):
    split = Mesh(mesh.devices.reshape(tuple(SIZES.values())), tuple(SIZES))
    in_specs = (
        P(SEQ, TP),
        P(SEQ),
        P(None, SEQ),
        P(None, None, TP),
        P(SEQ, None, TP),
        P(TP),
        P(TP),
        P(TP, SEQ),
    )
    out_specs = (P(SEQ, TP), P(SEQ, TP), P(SEQ, TP))
    return jax.shard_map(body, mesh=split, in_specs=in_specs, out_specs=out_specs, check_vma=False)
```

```python
import functools
import itertools
import math

import jax
import jax.numpy as jnp
import numpy as np
from jax import lax
from jax.experimental import pallas as pl
from jax.experimental.pallas import tpu as pltpu
from jax.sharding import Mesh
from jax.sharding import PartitionSpec as P

HEAD_DIM = 128
EPSILON = 1e-06
NEG_FILL = -1e30
LOG2E = 1.4426950408889634

SEQ = ("ya", "yb", "yc", "zh")
TP = ("zl", "xh", "xl", "c")
SIZES = {"ya": 2, "yb": 2, "yc": 2, "zh": 2, "zl": 4, "xh": 2, "xl": 2, "c": 2}

F32 = jnp.float32
BF16 = jnp.bfloat16
VMEM_LIMIT = 48 << 20


def permute(value, axes, move):
    sizes = [SIZES[a] for a in axes]
    pairs = []
    for at in itertools.product(*[range(n) for n in sizes]):
        to = move(*at)
        pairs.append((int(np.ravel_multi_index(at, sizes)), int(np.ravel_multi_index(to, sizes))))
    return lax.ppermute(value, axes, pairs)


def contract_first(lhs, rhs):
    return lax.dot_general(lhs, rhs, (((0,), (0,)), ((), ())), preferred_element_type=F32)


def call(kernel, out_shape, operands, scalars=None, scratch=(), name=None, cost=None):
    vmem = pl.BlockSpec(memory_space=pltpu.VMEM)
    smem = pl.BlockSpec(memory_space=pltpu.SMEM)
    specs = ([] if scalars is None else [smem]) + [vmem] * len(operands)
    args = ([] if scalars is None else [scalars]) + list(operands)
    return pl.pallas_call(
        kernel,
        out_shape=out_shape,
        in_specs=specs,
        out_specs=jax.tree.map(lambda _: vmem, out_shape),
        scratch_shapes=list(scratch),
        compiler_params=pltpu.CompilerParams(vmem_limit_bytes=VMEM_LIMIT),
        cost_estimate=cost,
        name=name,
    )(*args)


def shaped(shape, dtype):
    return jax.ShapeDtypeStruct(shape, dtype)


def project_kernel(at, mine, theirs, w, out_q, out_kv, stats):
    c = at[0]
    total = None
    for i, held in enumerate((mine, theirs)):
        core = lax.rem(c + i, 2)
        for x in range(4):
            for z in range(4):
                block, low = 2 * z + x // 2, x % 2
                weights = jnp.concatenate([w[block, low, p, core] for p in range(3)], axis=1)
                term = contract_first(weights, held[x, z])
                total = term if total is None else total + term
    query, key, value = total[:128], total[128:256], total[256:]
    out_q[...] = query
    out_kv[0] = key
    out_kv[1] = value
    rows = []
    for part in (query, key):
        row = jnp.sum(part * part, axis=0, keepdims=True)
        rows += [row[:, :128], row[:, 128:]]
    packed = jnp.concatenate(rows + [jnp.zeros((4, 128), F32)], axis=0)
    for t in range(stats.shape[0]):
        stats[t] = packed


def rotate_kernel(width, got, q, kv, cosine, sine, qg, kg, marks, q_out, k_cache, v_cache, message):
    totals = jnp.sum(got[...], axis=0)
    even = lax.rem(lax.broadcasted_iota(jnp.int32, (HEAD_DIM, 256), 0), 2) == 0
    cos, sin = cosine[...], sine[...]

    def rotated(value, gain, row):
        factor = jnp.concatenate([totals[row : row + 1], totals[row + 1 : row + 2]], axis=1)
        factor = lax.rsqrt(factor / width + EPSILON)
        normed = value * factor * gain
        after = pltpu.roll(normed, HEAD_DIM - 1, 0)
        before = pltpu.roll(normed, 1, 0)
        partner = jnp.where(even, -after, before)
        return normed * cos + partner * sin

    extra = marks[...].astype(BF16)
    q_low = rotated(q[...], qg[...], 0).astype(BF16)
    q_out[:128] = q_low
    q_out[128:144] = extra
    k_rot = rotated(kv[0], kg[...], 2)
    value = kv[1]
    k_low = k_rot.astype(BF16)
    v_low = value.astype(BF16)
    for t in range(message.shape[0]):
        message[t, :128] = k_low
        message[t, 128:256] = v_low
        message[t, 256:272] = extra
    k_cache[...] = k_rot.T.astype(BF16)
    v_cache[...] = value.T.astype(BF16)


def attend_kernel(order, at, q0, q1, q2, q3, keys, messages, held):
    count = keys.shape[0]
    scale = LOG2E / math.sqrt(HEAD_DIM)
    parts = (q0, q1, q2, q3)
    q_low = jnp.concatenate([q[:128] for q in parts], axis=1)
    seg_q = jnp.concatenate([q[128:144] for q in parts], axis=1).astype(F32)[:1]
    top = None
    for b in range(count):
        seg_k = keys[b, 256:272].astype(F32).T[:, :1]
        scores = contract_first(keys[b, :128], q_low) * scale
        scores = jnp.where(seg_k == seg_q, scores, NEG_FILL)
        held[b] = scores
        here = jnp.max(scores, axis=0, keepdims=True)
        top = here if top is None else jnp.maximum(top, here)
    top = jnp.maximum(top, -1e20)
    total = jnp.zeros((1, 1024), F32)
    weighted = jnp.zeros((HEAD_DIM, 1024), F32)
    for b in range(count):
        weights = jnp.exp2(held[b] - top)
        total = total + jnp.sum(weights, axis=0, keepdims=True)
        weighted = weighted + jnp.dot(
            keys[b, 128:256], weights.astype(BF16), preferred_element_type=F32
        )
    some = total > 0.0
    safe = jnp.where(some, total, 1.0)
    out = weighted / safe
    lse = jnp.where(some, top + jnp.log2(safe), NEG_FILL)
    high = lse.astype(BF16)
    rest = lse - high.astype(F32)
    middle = rest.astype(BF16)
    low = (rest - middle.astype(F32)).astype(BF16)
    rows = jnp.concatenate(
        [high.astype(F32), middle.astype(F32), low.astype(F32), jnp.zeros((13, 1024), F32)], axis=0
    ).astype(BF16)
    for place, d in enumerate(order):
        here = slice(256 * place, 256 * place + 256)
        target = jnp.bitwise_xor(at[1], d)
        messages[target, :128] = out[:, here].astype(BF16)
        messages[target, 128:144] = rows[:, here]


def merge_kernel(got, out):
    lses, parts = [], []
    for d in range(4):
        rows = got[d, 128:144].astype(F32)
        lses.append(rows[0:1] + rows[1:2] + rows[2:3])
        parts.append(got[d, :128].astype(F32))
    top = functools.reduce(jnp.maximum, lses)
    weights = [jnp.exp2(lse - top) for lse in lses]
    total = sum(weights[1:], weights[0])
    value = None
    for weight, part in zip(weights, parts, strict=True):
        term = part * (weight / total)
        value = term if value is None else value + term
    out[...] = value.astype(BF16)


def partial_kernel(own, other, w_own, w_other, messages):
    both = jnp.concatenate([own[...], other[...]], axis=0)
    for x in range(4):
        for z in range(4):
            block, low = 2 * z + x // 2, x % 2
            weights = jnp.concatenate([w_own[block, low], w_other[block, low]], axis=1)
            messages[x, z] = jnp.dot(weights, both, preferred_element_type=F32).astype(BF16)


def along_x_kernel(got, out):
    for z in range(4):
        total = got[0, z].astype(F32)
        for x in range(1, 4):
            total = total + got[x, z].astype(F32)
        out[z] = total.astype(BF16)


def exchange(value, axes):
    return lax.all_to_all(value, axes, 0, 0, tiled=True)


def spread(value, axes):
    count = math.prod(SIZES[a] for a in axes)
    return exchange(jnp.broadcast_to(value, (count,) + value.shape), axes)


def body(hidden_in, seg_ids, positions, mod_table, w_qkv, q_gain, k_gain, w_out):
    tok_rows, feat_local = hidden_in.shape
    model_width = feat_local * 32
    heads_width = 4096
    at = jnp.stack(
        [lax.axis_index("c"), lax.axis_index("yb") * 2 + lax.axis_index("yc")]
    ).astype(jnp.int32)

    local = jnp.concatenate([jnp.transpose(w_qkv, (1, 0, 2)), w_out.T[None]], axis=0)
    pair = lax.all_gather(local, "zh", axis=0, tiled=False)

    w_all = lax.all_gather(pair, ("ya", "yb", "yc"), axis=0, tiled=False)
    w_all = w_all.reshape(8, 2, 4, 2, 160, 128)

    x_t = hidden_in.T.astype(F32)
    sums = jnp.stack([jnp.sum(x_t, axis=0), jnp.sum(x_t * x_t, axis=0)]).reshape(4, 128)
    sums = jnp.concatenate([sums, jnp.zeros((4, 128), F32)], axis=0)
    sums = jnp.broadcast_to(sums, (32, 8, 128))
    segment_count = mod_table.shape[0]
    onehot = (seg_ids[None, :] == jnp.arange(segment_count, dtype=jnp.int32)[:, None]).astype(F32)
    modulation = lax.dot_general(
        mod_table.reshape(segment_count, 3 * feat_local),
        onehot,
        (((0,), (0,)), ((), ())),
        precision=lax.Precision.HIGHEST,
    ).reshape(3, feat_local, tok_rows)
    part_width = HEAD_DIM // 6
    widths = (HEAD_DIM - 4 * part_width, 2 * part_width, 2 * part_width)
    angles = []
    for axis_number in range(3):
        width = widths[axis_number]
        exponent = jnp.arange(0, width, 2, dtype=F32) / width
        frequency = jnp.repeat(1.0 / 10000.0**exponent, 2)
        angles.append(positions[axis_number].astype(F32)[None, :] * frequency[:, None])
    angle = jnp.concatenate(angles, axis=0)
    cosine, sine = jnp.cos(angle), jnp.sin(angle)
    marks = jnp.broadcast_to(seg_ids[None, :].astype(F32), (16, tok_rows))
    sums = exchange(sums, TP)
    sums = jnp.sum(sums, axis=0)[:4].reshape(2, tok_rows)
    mean_value = sums[0:1] / model_width
    variance = sums[1:2] / model_width - mean_value * mean_value
    normed = (x_t - mean_value) * lax.rsqrt(variance + EPSILON)
    packet = (normed * (1.0 + modulation[1]) + modulation[0]).astype(BF16)

    held = spread(spread(packet, ("zl",)), ("xh", "xl"))
    theirs = permute(held, ("c",), lambda c: (1 - c,))

    query, key_value, stats = call(
        project_kernel,
        (shaped((128, 256), F32), shaped((2, 128, 256), F32), shaped((32, 8, 128), F32)),
        [held, theirs, w_all],
        scalars=at,
        name="project",
        cost=pl.CostEstimate(flops=2 * 256 * 5120 * 384, bytes_accessed=6 << 20, transcendentals=0),
    )
    stats = exchange(stats, TP)
    core = lax.axis_index("c")
    wo_own = lax.dynamic_index_in_dim(w_all[:, :, 3], core, axis=2, keepdims=False)
    wo_other = lax.dynamic_index_in_dim(w_all[:, :, 3], 1 - core, axis=2, keepdims=False)
    stats, wo_own, wo_other = lax.optimization_barrier((stats, wo_own, wo_other))
    wo_other = permute(wo_other, ("c",), lambda c: (1 - c,))
    q_message, k_cache, v_cache, kv_message = call(
        functools.partial(rotate_kernel, heads_width),
        (
            shaped((144, 256), BF16),
            shaped((256, 128), BF16),
            shaped((256, 128), BF16),
            shaped((4, 272, 256), BF16),
        ),
        [stats, query, key_value, cosine, sine, q_gain.reshape(128, 1), k_gain.reshape(128, 1), marks],
        name="rotate",
    )
    keys = exchange(kv_message, ("ya", "zh"))
    keys, wo_own, wo_other = lax.optimization_barrier((keys, wo_own, wo_other))
    order = (0, 1, 3, 2)
    queries = [q_message] + [
        permute(q_message, ("yb", "yc"), lambda yb, yc, d=d: (yb ^ (d >> 1), yc ^ (d & 1)))
        for d in order[1:]
    ]
    o_messages = call(
        functools.partial(attend_kernel, order),
        shaped((4, 144, 256), BF16),
        queries + [keys],
        scalars=at,
        scratch=[pltpu.VMEM((4, 256, 1024), F32)],
        name="attend",
    )
    own = call(
        merge_kernel, shaped((128, 256), BF16), [exchange(o_messages, ("yb", "yc"))], name="merge"
    )
    other = permute(own, ("c",), lambda c: (1 - c,))
    partials = call(
        partial_kernel, shaped((4, 4, 160, 256), BF16), [own, other, wo_own, wo_other], name="partial"
    )
    partials = call(
        along_x_kernel,
        shaped((4, 160, 256), BF16),
        [exchange(partials, ("xh", "xl"))],
        name="along_x",
    )
    mixed = jnp.sum(exchange(partials, ("zl",)).astype(F32), axis=0)
    hidden_out = (x_t + modulation[2] * mixed).T.astype(BF16)
    return (hidden_out, k_cache, v_cache)


def solution(mesh):
    split = Mesh(mesh.devices.reshape(tuple(SIZES.values())), tuple(SIZES))
    in_specs = (
        P(SEQ, TP),
        P(SEQ),
        P(None, SEQ),
        P(None, None, TP),
        P(SEQ, None, TP),
        P(TP),
        P(TP),
        P(TP, SEQ),
    )
    out_specs = (P(SEQ, TP), P(SEQ, TP), P(SEQ, TP))
    return jax.shard_map(body, mesh=split, in_specs=in_specs, out_specs=out_specs, check_vma=False)
```

```python
import functools
import itertools
import math

import jax
import jax.numpy as jnp
import numpy as np
from jax import lax
from jax.experimental import pallas as pl
from jax.experimental.pallas import tpu as pltpu
from jax.sharding import Mesh
from jax.sharding import PartitionSpec as P

HEAD_DIM = 128
EPSILON = 1e-06
NEG_FILL = -1e30
LOG2E = 1.4426950408889634

SEQ = ("ya", "yb", "yc", "zh")
TP = ("zl", "xh", "xl", "c")
SIZES = {"ya": 2, "yb": 2, "yc": 2, "zh": 2, "zl": 4, "xh": 2, "xl": 2, "c": 2}

F32 = jnp.float32
BF16 = jnp.bfloat16
VMEM_LIMIT = 48 << 20


def permute(value, axes, move):
    sizes = [SIZES[a] for a in axes]
    pairs = []
    for at in itertools.product(*[range(n) for n in sizes]):
        to = move(*at)
        pairs.append((int(np.ravel_multi_index(at, sizes)), int(np.ravel_multi_index(to, sizes))))
    return lax.ppermute(value, axes, pairs)


def contract_first(lhs, rhs):
    return lax.dot_general(lhs, rhs, (((0,), (0,)), ((), ())), preferred_element_type=F32)


def call(kernel, out_shape, operands, scalars=None, scratch=(), name=None, cost=None):
    vmem = pl.BlockSpec(memory_space=pltpu.VMEM)
    smem = pl.BlockSpec(memory_space=pltpu.SMEM)
    specs = ([] if scalars is None else [smem]) + [vmem] * len(operands)
    args = ([] if scalars is None else [scalars]) + list(operands)
    return pl.pallas_call(
        kernel,
        out_shape=out_shape,
        in_specs=specs,
        out_specs=jax.tree.map(lambda _: vmem, out_shape),
        scratch_shapes=list(scratch),
        compiler_params=pltpu.CompilerParams(vmem_limit_bytes=VMEM_LIMIT),
        cost_estimate=cost,
        name=name,
    )(*args)


def shaped(shape, dtype):
    return jax.ShapeDtypeStruct(shape, dtype)


def project_kernel(at, mine, theirs, w, out_q, out_kv, stats):
    c = at[0]
    total = None
    for i, held in enumerate((mine, theirs)):
        core = lax.rem(c + i, 2)
        for x in range(4):
            for z in range(4):
                block, low = 2 * z + x // 2, x % 2
                weights = jnp.concatenate([w[block, low, p, core] for p in range(3)], axis=1)
                term = contract_first(weights, held[x, z])
                total = term if total is None else total + term
    query, key, value = total[:128], total[128:256], total[256:]
    out_q[...] = query
    out_kv[0] = key
    out_kv[1] = value
    rows = []
    for part in (query, key):
        row = jnp.sum(part * part, axis=0, keepdims=True)
        rows += [row[:, :128], row[:, 128:]]
    packed = jnp.concatenate(rows + [jnp.zeros((4, 128), F32)], axis=0)
    for t in range(stats.shape[0]):
        stats[t] = packed


def rotate_kernel(width, got, q, kv, cosine, sine, qg, kg, marks, q_out, k_cache, v_cache, message):
    totals = jnp.sum(got[...], axis=0)
    even = lax.rem(lax.broadcasted_iota(jnp.int32, (HEAD_DIM, 256), 0), 2) == 0
    cos, sin = cosine[...], sine[...]

    def rotated(value, gain, row):
        factor = jnp.concatenate([totals[row : row + 1], totals[row + 1 : row + 2]], axis=1)
        factor = lax.rsqrt(factor / width + EPSILON)
        normed = value * factor * gain
        after = pltpu.roll(normed, HEAD_DIM - 1, 0)
        before = pltpu.roll(normed, 1, 0)
        partner = jnp.where(even, -after, before)
        return normed * cos + partner * sin

    extra = marks[...].astype(BF16)
    q_low = rotated(q[...], qg[...], 0).astype(BF16)
    q_out[:128] = q_low
    q_out[128:144] = extra
    k_rot = rotated(kv[0], kg[...], 2)
    value = kv[1]
    k_low = k_rot.astype(BF16)
    v_low = value.astype(BF16)
    for t in range(message.shape[0]):
        message[t, :128] = k_low
        message[t, 128:256] = v_low
        message[t, 256:272] = extra
    k_cache[...] = k_rot.T.astype(BF16)
    v_cache[...] = value.T.astype(BF16)


def attend_kernel(order, at, q0, q1, q2, q3, keys, messages, held):
    count = keys.shape[0]
    scale = LOG2E / math.sqrt(HEAD_DIM)
    parts = (q0, q1, q2, q3)
    q_low = jnp.concatenate([q[:128] for q in parts], axis=1)
    seg_q = jnp.concatenate([q[128:144] for q in parts], axis=1).astype(F32)[:1]
    top = None
    for b in range(count):
        seg_k = keys[b, 256:272].astype(F32).T[:, :1]
        scores = contract_first(keys[b, :128], q_low) * scale
        scores = jnp.where(seg_k == seg_q, scores, NEG_FILL)
        held[b] = scores
        here = jnp.max(scores, axis=0, keepdims=True)
        top = here if top is None else jnp.maximum(top, here)
    top = jnp.maximum(top, -1e20)
    total = jnp.zeros((1, 1024), F32)
    weighted = jnp.zeros((HEAD_DIM, 1024), F32)
    for b in range(count):
        weights = jnp.exp2(held[b] - top)
        total = total + jnp.sum(weights, axis=0, keepdims=True)
        weighted = weighted + jnp.dot(
            keys[b, 128:256], weights.astype(BF16), preferred_element_type=F32
        )
    some = total > 0.0
    safe = jnp.where(some, total, 1.0)
    out = weighted / safe
    lse = jnp.where(some, top + jnp.log2(safe), NEG_FILL)
    high = lse.astype(BF16)
    rest = lse - high.astype(F32)
    middle = rest.astype(BF16)
    low = (rest - middle.astype(F32)).astype(BF16)
    rows = jnp.concatenate(
        [high.astype(F32), middle.astype(F32), low.astype(F32), jnp.zeros((13, 1024), F32)], axis=0
    ).astype(BF16)
    for place, d in enumerate(order):
        here = slice(256 * place, 256 * place + 256)
        target = jnp.bitwise_xor(at[1], d)
        messages[target, :128] = out[:, here].astype(BF16)
        messages[target, 128:144] = rows[:, here]


def merge_kernel(got, out):
    lses, parts = [], []
    for d in range(4):
        rows = got[d, 128:144].astype(F32)
        lses.append(rows[0:1] + rows[1:2] + rows[2:3])
        parts.append(got[d, :128].astype(F32))
    top = functools.reduce(jnp.maximum, lses)
    weights = [jnp.exp2(lse - top) for lse in lses]
    total = sum(weights[1:], weights[0])
    value = None
    for weight, part in zip(weights, parts, strict=True):
        term = part * (weight / total)
        value = term if value is None else value + term
    out[...] = value.astype(BF16)


def partial_kernel(own, other, w, messages):
    both = jnp.concatenate([own[...], other[...]], axis=0)
    for x in range(4):
        for z in range(4):
            block, low = 2 * z + x // 2, x % 2
            weights = jnp.concatenate([w[block, 0, low], w[block, 1, low]], axis=1)
            messages[x, z] = jnp.dot(weights, both, preferred_element_type=F32).astype(BF16)


def along_x_kernel(got, out):
    for z in range(4):
        total = got[0, z].astype(F32)
        for x in range(1, 4):
            total = total + got[x, z].astype(F32)
        out[z] = total.astype(BF16)


def exchange(value, axes):
    return lax.all_to_all(value, axes, 0, 0, tiled=True)


def spread(value, axes):
    count = math.prod(SIZES[a] for a in axes)
    return exchange(jnp.broadcast_to(value, (count,) + value.shape), axes)


def body(hidden_in, seg_ids, positions, mod_table, w_qkv, q_gain, k_gain, w_out):
    tok_rows, feat_local = hidden_in.shape
    model_width = feat_local * 32
    heads_width = 4096
    at = jnp.stack(
        [lax.axis_index("c"), lax.axis_index("yb") * 2 + lax.axis_index("yc")]
    ).astype(jnp.int32)

    local = jnp.concatenate([jnp.transpose(w_qkv, (1, 0, 2)), w_out.T[None]], axis=0)
    pair = lax.all_gather(local, "zh", axis=0, tiled=False)

    w_all = lax.all_gather(pair[:, :3], ("ya", "yb", "yc"), axis=0, tiled=False)
    w_all = w_all.reshape(8, 2, 3, 2, 160, 128)

    x_t = hidden_in.T.astype(F32)
    sums = jnp.stack([jnp.sum(x_t, axis=0), jnp.sum(x_t * x_t, axis=0)]).reshape(4, 128)
    sums = jnp.concatenate([sums, jnp.zeros((4, 128), F32)], axis=0)
    sums = jnp.broadcast_to(sums, (32, 8, 128))
    segment_count = mod_table.shape[0]
    onehot = (seg_ids[None, :] == jnp.arange(segment_count, dtype=jnp.int32)[:, None]).astype(F32)
    modulation = lax.dot_general(
        mod_table.reshape(segment_count, 3 * feat_local),
        onehot,
        (((0,), (0,)), ((), ())),
        precision=lax.Precision.HIGHEST,
    ).reshape(3, feat_local, tok_rows)
    part_width = HEAD_DIM // 6
    widths = (HEAD_DIM - 4 * part_width, 2 * part_width, 2 * part_width)
    angles = []
    for axis_number in range(3):
        width = widths[axis_number]
        exponent = jnp.arange(0, width, 2, dtype=F32) / width
        frequency = jnp.repeat(1.0 / 10000.0**exponent, 2)
        angles.append(positions[axis_number].astype(F32)[None, :] * frequency[:, None])
    angle = jnp.concatenate(angles, axis=0)
    cosine, sine = jnp.cos(angle), jnp.sin(angle)
    marks = jnp.broadcast_to(seg_ids[None, :].astype(F32), (16, tok_rows))
    sums = exchange(sums, TP)
    sums = jnp.sum(sums, axis=0)[:4].reshape(2, tok_rows)
    mean_value = sums[0:1] / model_width
    variance = sums[1:2] / model_width - mean_value * mean_value
    normed = (x_t - mean_value) * lax.rsqrt(variance + EPSILON)
    packet = (normed * (1.0 + modulation[1]) + modulation[0]).astype(BF16)

    core = lax.axis_index("c")
    wo_pair = pair[:, 3].reshape(2, 2, 160, 128)
    wo_own = lax.dynamic_index_in_dim(wo_pair, core, axis=1, keepdims=False)
    wo_give = lax.dynamic_index_in_dim(wo_pair, 1 - core, axis=1, keepdims=False)
    packet, wo_own, wo_give = lax.optimization_barrier((packet, wo_own, wo_give))
    wo_other = permute(wo_give, ("c",), lambda c: (1 - c,))
    wo_all = lax.all_gather(jnp.stack([wo_own, wo_other]), ("ya", "yb", "yc"), axis=0, tiled=False)

    held = spread(spread(packet, ("zl",)), ("xh", "xl"))
    theirs = permute(held, ("c",), lambda c: (1 - c,))

    query, key_value, stats = call(
        project_kernel,
        (shaped((128, 256), F32), shaped((2, 128, 256), F32), shaped((32, 8, 128), F32)),
        [held, theirs, w_all],
        scalars=at,
        name="project",
        cost=pl.CostEstimate(flops=2 * 256 * 5120 * 384, bytes_accessed=6 << 20, transcendentals=0),
    )
    stats = exchange(stats, TP)
    q_message, k_cache, v_cache, kv_message = call(
        functools.partial(rotate_kernel, heads_width),
        (
            shaped((144, 256), BF16),
            shaped((256, 128), BF16),
            shaped((256, 128), BF16),
            shaped((4, 272, 256), BF16),
        ),
        [stats, query, key_value, cosine, sine, q_gain.reshape(128, 1), k_gain.reshape(128, 1), marks],
        name="rotate",
    )
    keys = exchange(kv_message, ("ya", "zh"))
    order = (0, 1, 3, 2)
    queries = [q_message] + [
        permute(q_message, ("yb", "yc"), lambda yb, yc, d=d: (yb ^ (d >> 1), yc ^ (d & 1)))
        for d in order[1:]
    ]
    o_messages = call(
        functools.partial(attend_kernel, order),
        shaped((4, 144, 256), BF16),
        queries + [keys],
        scalars=at,
        scratch=[pltpu.VMEM((4, 256, 1024), F32)],
        name="attend",
    )
    own = call(
        merge_kernel, shaped((128, 256), BF16), [exchange(o_messages, ("yb", "yc"))], name="merge"
    )
    other = permute(own, ("c",), lambda c: (1 - c,))
    partials = call(
        partial_kernel, shaped((4, 4, 160, 256), BF16), [own, other, wo_all], name="partial"
    )
    partials = call(
        along_x_kernel,
        shaped((4, 160, 256), BF16),
        [exchange(partials, ("xh", "xl"))],
        name="along_x",
    )
    mixed = jnp.sum(exchange(partials, ("zl",)).astype(F32), axis=0)
    hidden_out = (x_t + modulation[2] * mixed).T.astype(BF16)
    return (hidden_out, k_cache, v_cache)


def solution(mesh):
    split = Mesh(mesh.devices.reshape(tuple(SIZES.values())), tuple(SIZES))
    in_specs = (
        P(SEQ, TP),
        P(SEQ),
        P(None, SEQ),
        P(None, None, TP),
        P(SEQ, None, TP),
        P(TP),
        P(TP),
        P(TP, SEQ),
    )
    out_specs = (P(SEQ, TP), P(SEQ, TP), P(SEQ, TP))
    return jax.shard_map(body, mesh=split, in_specs=in_specs, out_specs=out_specs, check_vma=False)
```

```python
import functools
import itertools
import math

import jax
import jax.numpy as jnp
import numpy as np
from jax import lax
from jax.experimental import pallas as pl
from jax.experimental.pallas import tpu as pltpu
from jax.sharding import Mesh
from jax.sharding import PartitionSpec as P

HEAD_DIM = 128
EPSILON = 1e-06
NEG_FILL = -1e30
LOG2E = 1.4426950408889634

SEQ = ("ya", "yb", "yc", "zh")
TP = ("zl", "xh", "xl", "c")
SIZES = {"ya": 2, "yb": 2, "yc": 2, "zh": 2, "zl": 4, "xh": 2, "xl": 2, "c": 2}

F32 = jnp.float32
BF16 = jnp.bfloat16
VMEM_LIMIT = 48 << 20


def permute(value, axes, move):
    sizes = [SIZES[a] for a in axes]
    pairs = []
    for at in itertools.product(*[range(n) for n in sizes]):
        to = move(*at)
        pairs.append((int(np.ravel_multi_index(at, sizes)), int(np.ravel_multi_index(to, sizes))))
    return lax.ppermute(value, axes, pairs)


def contract_first(lhs, rhs):
    return lax.dot_general(lhs, rhs, (((0,), (0,)), ((), ())), preferred_element_type=F32)


def call(kernel, out_shape, operands, scalars=None, scratch=(), name=None, cost=None):
    vmem = pl.BlockSpec(memory_space=pltpu.VMEM)
    smem = pl.BlockSpec(memory_space=pltpu.SMEM)
    specs = ([] if scalars is None else [smem]) + [vmem] * len(operands)
    args = ([] if scalars is None else [scalars]) + list(operands)
    return pl.pallas_call(
        kernel,
        out_shape=out_shape,
        in_specs=specs,
        out_specs=jax.tree.map(lambda _: vmem, out_shape),
        scratch_shapes=list(scratch),
        compiler_params=pltpu.CompilerParams(vmem_limit_bytes=VMEM_LIMIT),
        cost_estimate=cost,
        name=name,
    )(*args)


def shaped(shape, dtype):
    return jax.ShapeDtypeStruct(shape, dtype)


def project_kernel(at, mine, theirs, w, out_q, out_kv, stats):
    c = at[0]
    total = None
    for i, held in enumerate((mine, theirs)):
        core = lax.rem(c + i, 2)
        for x in range(4):
            for z in range(4):
                block, low = 2 * z + x // 2, x % 2
                weights = jnp.concatenate([w[block, low, p, core] for p in range(3)], axis=1)
                term = contract_first(weights, held[x, z])
                total = term if total is None else total + term
    query, key, value = total[:128], total[128:256], total[256:]
    out_q[...] = query
    out_kv[0] = key
    out_kv[1] = value
    rows = []
    for part in (query, key):
        row = jnp.sum(part * part, axis=0, keepdims=True)
        rows += [row[:, :128], row[:, 128:]]
    packed = jnp.concatenate(rows + [jnp.zeros((4, 128), F32)], axis=0)
    for t in range(stats.shape[0]):
        stats[t] = packed


def rotate_kernel(width, got, q, kv, cosine, sine, qg, kg, marks, q_out, k_cache, v_cache, message):
    totals = jnp.sum(got[...], axis=0)
    even = lax.rem(lax.broadcasted_iota(jnp.int32, (HEAD_DIM, 256), 0), 2) == 0
    cos, sin = cosine[...], sine[...]

    def rotated(value, gain, row):
        factor = jnp.concatenate([totals[row : row + 1], totals[row + 1 : row + 2]], axis=1)
        factor = lax.rsqrt(factor / width + EPSILON)
        normed = value * factor * gain
        after = pltpu.roll(normed, HEAD_DIM - 1, 0)
        before = pltpu.roll(normed, 1, 0)
        partner = jnp.where(even, -after, before)
        return normed * cos + partner * sin

    extra = marks[...].astype(BF16)
    q_low = rotated(q[...], qg[...], 0).astype(BF16)
    q_out[:128] = q_low
    q_out[128:144] = extra
    k_rot = rotated(kv[0], kg[...], 2)
    value = kv[1]
    k_low = k_rot.astype(BF16)
    v_low = value.astype(BF16)
    for t in range(message.shape[0]):
        message[t, :128] = k_low
        message[t, 128:256] = v_low
        message[t, 256:272] = extra
    k_cache[...] = k_rot.T.astype(BF16)
    v_cache[...] = value.T.astype(BF16)


def attend_kernel(order, at, q0, q1, q2, q3, keys, messages, held):
    count = keys.shape[0]
    scale = LOG2E / math.sqrt(HEAD_DIM)
    parts = (q0, q1, q2, q3)
    q_low = jnp.concatenate([q[:128] for q in parts], axis=1)
    seg_q = jnp.concatenate([q[128:144] for q in parts], axis=1).astype(F32)[:1]
    top = None
    for b in range(count):
        seg_k = keys[b, 256:272].astype(F32).T[:, :1]
        scores = contract_first(keys[b, :128], q_low) * scale
        scores = jnp.where(seg_k == seg_q, scores, NEG_FILL)
        held[b] = scores
        here = jnp.max(scores, axis=0, keepdims=True)
        top = here if top is None else jnp.maximum(top, here)
    top = jnp.maximum(top, -1e20)
    total = jnp.zeros((1, 1024), F32)
    weighted = jnp.zeros((HEAD_DIM, 1024), F32)
    for b in range(count):
        weights = jnp.exp2(held[b] - top)
        total = total + jnp.sum(weights, axis=0, keepdims=True)
        weighted = weighted + jnp.dot(
            keys[b, 128:256], weights.astype(BF16), preferred_element_type=F32
        )
    some = total > 0.0
    safe = jnp.where(some, total, 1.0)
    out = weighted / safe
    lse = jnp.where(some, top + jnp.log2(safe), NEG_FILL)
    high = lse.astype(BF16)
    rest = lse - high.astype(F32)
    middle = rest.astype(BF16)
    low = (rest - middle.astype(F32)).astype(BF16)
    rows = jnp.concatenate(
        [high.astype(F32), middle.astype(F32), low.astype(F32), jnp.zeros((13, 1024), F32)], axis=0
    ).astype(BF16)
    for place, d in enumerate(order):
        here = slice(256 * place, 256 * place + 256)
        target = lax.rem(at[1] + 4 - d, 4)
        messages[target, :128] = out[:, here].astype(BF16)
        messages[target, 128:144] = rows[:, here]


def merge_kernel(got, out):
    lses, parts = [], []
    for d in range(4):
        rows = got[d, 128:144].astype(F32)
        lses.append(rows[0:1] + rows[1:2] + rows[2:3])
        parts.append(got[d, :128].astype(F32))
    top = functools.reduce(jnp.maximum, lses)
    weights = [jnp.exp2(lse - top) for lse in lses]
    total = sum(weights[1:], weights[0])
    value = None
    for weight, part in zip(weights, parts, strict=True):
        term = part * (weight / total)
        value = term if value is None else value + term
    out[...] = value.astype(BF16)


def partial_kernel(own, other, w, messages):
    both = jnp.concatenate([own[...], other[...]], axis=0)
    for x in range(4):
        for z in range(4):
            block, low = 2 * z + x // 2, x % 2
            weights = jnp.concatenate([w[block, 0, low], w[block, 1, low]], axis=1)
            messages[x, z] = jnp.dot(weights, both, preferred_element_type=F32).astype(BF16)


def along_x_kernel(got, out):
    for z in range(4):
        total = got[0, z].astype(F32)
        for x in range(1, 4):
            total = total + got[x, z].astype(F32)
        out[z] = total.astype(BF16)


def exchange(value, axes):
    return lax.all_to_all(value, axes, 0, 0, tiled=True)


def spread(value, axes):
    count = math.prod(SIZES[a] for a in axes)
    return exchange(jnp.broadcast_to(value, (count,) + value.shape), axes)


def body(hidden_in, seg_ids, positions, mod_table, w_qkv, q_gain, k_gain, w_out):
    tok_rows, feat_local = hidden_in.shape
    model_width = feat_local * 32
    heads_width = 4096
    at = jnp.stack(
        [lax.axis_index("c"), lax.axis_index("ya") * 2 + lax.axis_index("yb")]
    ).astype(jnp.int32)

    local = jnp.concatenate([jnp.transpose(w_qkv, (1, 0, 2)), w_out.T[None]], axis=0)
    pair = lax.all_gather(local, "zh", axis=0, tiled=False)
    w_all = lax.all_gather(pair[:, :3], ("ya", "yb", "yc"), axis=0, tiled=False)
    w_all = w_all.reshape(8, 2, 3, 2, 160, 128)

    x_t = hidden_in.T.astype(F32)
    sums = jnp.stack([jnp.sum(x_t, axis=0), jnp.sum(x_t * x_t, axis=0)]).reshape(4, 128)
    sums = jnp.concatenate([sums, jnp.zeros((4, 128), F32)], axis=0)
    sums = jnp.broadcast_to(sums, (32, 8, 128))
    segment_count = mod_table.shape[0]
    onehot = (seg_ids[None, :] == jnp.arange(segment_count, dtype=jnp.int32)[:, None]).astype(F32)
    modulation = lax.dot_general(
        mod_table.reshape(segment_count, 3 * feat_local),
        onehot,
        (((0,), (0,)), ((), ())),
        precision=lax.Precision.HIGHEST,
    ).reshape(3, feat_local, tok_rows)
    part_width = HEAD_DIM // 6
    widths = (HEAD_DIM - 4 * part_width, 2 * part_width, 2 * part_width)
    angles = []
    for axis_number in range(3):
        width = widths[axis_number]
        exponent = jnp.arange(0, width, 2, dtype=F32) / width
        frequency = jnp.repeat(1.0 / 10000.0**exponent, 2)
        angles.append(positions[axis_number].astype(F32)[None, :] * frequency[:, None])
    angle = jnp.concatenate(angles, axis=0)
    cosine, sine = jnp.cos(angle), jnp.sin(angle)
    marks = jnp.broadcast_to(seg_ids[None, :].astype(F32), (16, tok_rows))
    sums = exchange(sums, TP)
    sums = jnp.sum(sums, axis=0)[:4].reshape(2, tok_rows)
    mean_value = sums[0:1] / model_width
    variance = sums[1:2] / model_width - mean_value * mean_value
    normed = (x_t - mean_value) * lax.rsqrt(variance + EPSILON)
    packet = (normed * (1.0 + modulation[1]) + modulation[0]).astype(BF16)

    core = lax.axis_index("c")
    wo_pair = pair[:, 3].reshape(2, 2, 160, 128)
    wo_own = lax.dynamic_index_in_dim(wo_pair, core, axis=1, keepdims=False)
    wo_give = lax.dynamic_index_in_dim(wo_pair, 1 - core, axis=1, keepdims=False)
    packet, wo_own, wo_give = lax.optimization_barrier((packet, wo_own, wo_give))
    wo_other = permute(wo_give, ("c",), lambda c: (1 - c,))
    wo_all = lax.all_gather(jnp.stack([wo_own, wo_other]), ("ya", "yb", "yc"), axis=0, tiled=False)

    held = spread(spread(packet, ("zl",)), ("xh", "xl"))
    theirs = permute(held, ("c",), lambda c: (1 - c,))

    query, key_value, stats = call(
        project_kernel,
        (shaped((128, 256), F32), shaped((2, 128, 256), F32), shaped((32, 8, 128), F32)),
        [held, theirs, w_all],
        scalars=at,
        name="project",
        cost=pl.CostEstimate(flops=2 * 256 * 5120 * 384, bytes_accessed=6 << 20, transcendentals=0),
    )
    stats = exchange(stats, TP)
    q_message, k_cache, v_cache, kv_message = call(
        functools.partial(rotate_kernel, heads_width),
        (
            shaped((144, 256), BF16),
            shaped((256, 128), BF16),
            shaped((256, 128), BF16),
            shaped((4, 272, 256), BF16),
        ),
        [stats, query, key_value, cosine, sine, q_gain.reshape(128, 1), k_gain.reshape(128, 1), marks],
        name="rotate",
    )
    keys = exchange(kv_message, ("yc", "zh"))
    order = (0, 1, 3, 2)
    queries = [q_message] + [
        permute(q_message, ("ya", "yb"), lambda ya, yb, d=d: divmod((ya * 2 + yb + d) % 4, 2))
        for d in order[1:]
    ]
    o_messages = call(
        functools.partial(attend_kernel, order),
        shaped((4, 144, 256), BF16),
        queries + [keys],
        scalars=at,
        scratch=[pltpu.VMEM((4, 256, 1024), F32)],
        name="attend",
    )
    own = call(
        merge_kernel, shaped((128, 256), BF16), [exchange(o_messages, ("ya", "yb"))], name="merge"
    )
    other = permute(own, ("c",), lambda c: (1 - c,))
    partials = call(
        partial_kernel, shaped((4, 4, 160, 256), BF16), [own, other, wo_all], name="partial"
    )
    partials = call(
        along_x_kernel,
        shaped((4, 160, 256), BF16),
        [exchange(partials, ("xh", "xl"))],
        name="along_x",
    )
    mixed = jnp.sum(exchange(partials, ("zl",)).astype(F32), axis=0)
    hidden_out = (x_t + modulation[2] * mixed).T.astype(BF16)
    return (hidden_out, k_cache, v_cache)


def solution(mesh):
    split = Mesh(mesh.devices.reshape(tuple(SIZES.values())), tuple(SIZES))
    in_specs = (
        P(SEQ, TP),
        P(SEQ),
        P(None, SEQ),
        P(None, None, TP),
        P(SEQ, None, TP),
        P(TP),
        P(TP),
        P(TP, SEQ),
    )
    out_specs = (P(SEQ, TP), P(SEQ, TP), P(SEQ, TP))
    return jax.shard_map(body, mesh=split, in_specs=in_specs, out_specs=out_specs, check_vma=False)
```

```python
import functools
import itertools
import math

import jax
import jax.numpy as jnp
import numpy as np
from jax import lax
from jax.experimental import pallas as pl
from jax.experimental.pallas import tpu as pltpu
from jax.sharding import Mesh
from jax.sharding import PartitionSpec as P

HEAD_DIM = 128
EPSILON = 1e-06
NEG_FILL = -1e30
LOG2E = 1.4426950408889634

SEQ = ("ya", "yb", "yc", "zh")
TP = ("zl", "xh", "xl", "c")
SIZES = {"ya": 2, "yb": 2, "yc": 2, "zh": 2, "zl": 4, "xh": 2, "xl": 2, "c": 2}

F32 = jnp.float32
BF16 = jnp.bfloat16
VMEM_LIMIT = 48 << 20


def permute(value, axes, move):
    sizes = [SIZES[a] for a in axes]
    pairs = []
    for at in itertools.product(*[range(n) for n in sizes]):
        to = move(*at)
        pairs.append((int(np.ravel_multi_index(at, sizes)), int(np.ravel_multi_index(to, sizes))))
    return lax.ppermute(value, axes, pairs)


def contract_first(lhs, rhs):
    return lax.dot_general(lhs, rhs, (((0,), (0,)), ((), ())), preferred_element_type=F32)


def call(kernel, out_shape, operands, scalars=None, scratch=(), name=None, cost=None):
    vmem = pl.BlockSpec(memory_space=pltpu.VMEM)
    smem = pl.BlockSpec(memory_space=pltpu.SMEM)
    specs = ([] if scalars is None else [smem]) + [vmem] * len(operands)
    args = ([] if scalars is None else [scalars]) + list(operands)
    return pl.pallas_call(
        kernel,
        out_shape=out_shape,
        in_specs=specs,
        out_specs=jax.tree.map(lambda _: vmem, out_shape),
        scratch_shapes=list(scratch),
        compiler_params=pltpu.CompilerParams(vmem_limit_bytes=VMEM_LIMIT),
        cost_estimate=cost,
        name=name,
    )(*args)


def shaped(shape, dtype):
    return jax.ShapeDtypeStruct(shape, dtype)


def project_kernel(at, mine, theirs, w, out_q, out_kv, stats):
    c = at[0]
    total = None
    for i, held in enumerate((mine, theirs)):
        core = lax.rem(c + i, 2)
        for x in range(4):
            rows = [w.at[2 * z + x // 2, x % 2] for z in range(4)]
            weights = jnp.concatenate(
                [jnp.concatenate([part[p, core] for part in rows], axis=0) for p in range(3)], axis=1
            )
            features = jnp.concatenate([held[x, z] for z in range(4)], axis=0)
            term = contract_first(weights, features)
            total = term if total is None else total + term
    query, key, value = total[:128], total[128:256], total[256:]
    out_q[...] = query
    out_kv[0] = key
    out_kv[1] = value
    rows = []
    for part in (query, key):
        row = jnp.sum(part * part, axis=0, keepdims=True)
        rows += [row[:, :128], row[:, 128:]]
    packed = jnp.concatenate(rows + [jnp.zeros((4, 128), F32)], axis=0)
    for t in range(stats.shape[0]):
        stats[t] = packed


def rotated(value, gain, totals, cos, sin, width):
    even = lax.rem(lax.broadcasted_iota(jnp.int32, (HEAD_DIM, 256), 0), 2) == 0
    factor = jnp.concatenate([totals[0:1], totals[1:2]], axis=1)
    factor = lax.rsqrt(factor / width + EPSILON)
    normed = value * factor * gain
    after = pltpu.roll(normed, HEAD_DIM - 1, 0)
    before = pltpu.roll(normed, 1, 0)
    partner = jnp.where(even, -after, before)
    return normed * cos + partner * sin


def keys_kernel(width, got, kv, cosine, sine, kg, marks, k_cache, v_cache, message):
    totals = jnp.sum(got[...], axis=0)[2:4]
    k_rot = rotated(kv[0], kg[...], totals, cosine[...], sine[...], width)
    value = kv[1]
    k_low = k_rot.astype(BF16)
    v_low = value.astype(BF16)
    extra = marks[...].astype(BF16)
    for t in range(message.shape[0]):
        message[t, :128] = k_low
        message[t, 128:256] = v_low
        message[t, 256:272] = extra
    k_cache[...] = k_rot.T.astype(BF16)
    v_cache[...] = value.T.astype(BF16)


def queries_kernel(width, got, q, cosine, sine, qg, marks, message):
    totals = jnp.sum(got[...], axis=0)[:2]
    q_low = rotated(q[...], qg[...], totals, cosine[...], sine[...], width).astype(BF16)
    extra = marks[...].astype(BF16)
    message[:128] = q_low
    message[128:144] = extra


def attend_kernel(order, at, q0, q1, q2, q3, keys, messages, held):
    count = keys.shape[0]
    scale = LOG2E / math.sqrt(HEAD_DIM)
    parts = (q0, q1, q2, q3)
    q_low = jnp.concatenate([q[:128] for q in parts], axis=1)
    seg_q = jnp.concatenate([q[128:144] for q in parts], axis=1).astype(F32)[:1]
    top = None
    for b in range(count):
        seg_k = keys[b, 256:272].astype(F32).T[:, :1]
        scores = contract_first(keys[b, :128], q_low) * scale
        scores = jnp.where(seg_k == seg_q, scores, NEG_FILL)
        held[b] = scores
        here = jnp.max(scores, axis=0, keepdims=True)
        top = here if top is None else jnp.maximum(top, here)
    top = jnp.maximum(top, -1e20)
    total = jnp.zeros((1, 1024), F32)
    weighted = jnp.zeros((HEAD_DIM, 1024), F32)
    for b in range(count):
        weights = jnp.exp2(held[b] - top)
        total = total + jnp.sum(weights, axis=0, keepdims=True)
        weighted = weighted + jnp.dot(
            keys[b, 128:256], weights.astype(BF16), preferred_element_type=F32
        )
    some = total > 0.0
    safe = jnp.where(some, total, 1.0)
    out = weighted / safe
    lse = jnp.where(some, top + jnp.log2(safe), NEG_FILL)
    high = lse.astype(BF16)
    rest = lse - high.astype(F32)
    middle = rest.astype(BF16)
    low = (rest - middle.astype(F32)).astype(BF16)
    rows = jnp.concatenate(
        [high.astype(F32), middle.astype(F32), low.astype(F32), jnp.zeros((13, 1024), F32)], axis=0
    ).astype(BF16)
    for place, d in enumerate(order):
        here = slice(256 * place, 256 * place + 256)
        target = lax.rem(at[1] + 4 - d, 4)
        messages[target, :128] = out[:, here].astype(BF16)
        messages[target, 128:144] = rows[:, here]


def merge_kernel(got, out):
    lses, parts = [], []
    for d in range(4):
        rows = got[d, 128:144].astype(F32)
        lses.append(rows[0:1] + rows[1:2] + rows[2:3])
        parts.append(got[d, :128].astype(F32))
    top = functools.reduce(jnp.maximum, lses)
    weights = [jnp.exp2(lse - top) for lse in lses]
    total = sum(weights[1:], weights[0])
    value = None
    for weight, part in zip(weights, parts, strict=True):
        term = part * (weight / total)
        value = term if value is None else value + term
    out[...] = value.astype(BF16)


def partial_kernel(own, other, w, messages):
    both = jnp.concatenate([own[...], other[...]], axis=0)
    for x in range(4):
        for z in range(4):
            block, low = 2 * z + x // 2, x % 2
            weights = jnp.concatenate([w[block, 0, low], w[block, 1, low]], axis=1)
            messages[x, z] = jnp.dot(weights, both, preferred_element_type=F32).astype(BF16)


def along_x_kernel(got, out):
    for z in range(4):
        total = got[0, z].astype(F32)
        for x in range(1, 4):
            total = total + got[x, z].astype(F32)
        out[z] = total.astype(BF16)


def exchange(value, axes):
    return lax.all_to_all(value, axes, 0, 0, tiled=True)


def spread(value, axes):
    count = math.prod(SIZES[a] for a in axes)
    return exchange(jnp.broadcast_to(value, (count,) + value.shape), axes)


def body(hidden_in, seg_ids, positions, mod_table, w_qkv, q_gain, k_gain, w_out):
    tok_rows, feat_local = hidden_in.shape
    model_width = feat_local * 32
    heads_width = 4096
    at = jnp.stack(
        [lax.axis_index("c"), lax.axis_index("ya") * 2 + lax.axis_index("yb")]
    ).astype(jnp.int32)

    local = jnp.concatenate([jnp.transpose(w_qkv, (1, 0, 2)), w_out.T[None]], axis=0)
    pair = lax.all_gather(local, "zh", axis=0, tiled=False)
    w_all = lax.all_gather(pair[:, :3], ("ya", "yb", "yc"), axis=0, tiled=False)
    w_all = w_all.reshape(8, 2, 3, 2, 160, 128)

    x_t = hidden_in.T.astype(F32)
    sums = jnp.stack([jnp.sum(x_t, axis=0), jnp.sum(x_t * x_t, axis=0)]).reshape(4, 128)
    sums = jnp.concatenate([sums, jnp.zeros((4, 128), F32)], axis=0)
    sums = jnp.broadcast_to(sums, (32, 8, 128))
    segment_count = mod_table.shape[0]
    onehot = (seg_ids[None, :] == jnp.arange(segment_count, dtype=jnp.int32)[:, None]).astype(F32)
    modulation = lax.dot_general(
        mod_table.reshape(segment_count, 3 * feat_local),
        onehot,
        (((0,), (0,)), ((), ())),
        precision=lax.Precision.HIGHEST,
    ).reshape(3, feat_local, tok_rows)
    part_width = HEAD_DIM // 6
    widths = (HEAD_DIM - 4 * part_width, 2 * part_width, 2 * part_width)
    angles = []
    for axis_number in range(3):
        width = widths[axis_number]
        exponent = jnp.arange(0, width, 2, dtype=F32) / width
        frequency = jnp.repeat(1.0 / 10000.0**exponent, 2)
        angles.append(positions[axis_number].astype(F32)[None, :] * frequency[:, None])
    angle = jnp.concatenate(angles, axis=0)
    cosine, sine = jnp.cos(angle), jnp.sin(angle)
    marks = jnp.broadcast_to(seg_ids[None, :].astype(F32), (16, tok_rows))
    sums = exchange(sums, TP)
    sums = jnp.sum(sums, axis=0)[:4].reshape(2, tok_rows)
    mean_value = sums[0:1] / model_width
    variance = sums[1:2] / model_width - mean_value * mean_value
    normed = (x_t - mean_value) * lax.rsqrt(variance + EPSILON)
    packet = (normed * (1.0 + modulation[1]) + modulation[0]).astype(BF16)

    core = lax.axis_index("c")
    wo_pair = pair[:, 3].reshape(2, 2, 160, 128)
    wo_own = lax.dynamic_index_in_dim(wo_pair, core, axis=1, keepdims=False)
    wo_give = lax.dynamic_index_in_dim(wo_pair, 1 - core, axis=1, keepdims=False)
    packet, wo_own, wo_give = lax.optimization_barrier((packet, wo_own, wo_give))
    wo_other = permute(wo_give, ("c",), lambda c: (1 - c,))
    wo_all = lax.all_gather(jnp.stack([wo_own, wo_other]), ("ya", "yb", "yc"), axis=0, tiled=False)

    held = spread(spread(packet, ("zl",)), ("xh", "xl"))
    theirs = permute(held, ("c",), lambda c: (1 - c,))

    query, key_value, stats = call(
        project_kernel,
        (shaped((128, 256), F32), shaped((2, 128, 256), F32), shaped((32, 8, 128), F32)),
        [held, theirs, w_all],
        scalars=at,
        name="project",
        cost=pl.CostEstimate(flops=2 * 256 * 5120 * 384, bytes_accessed=6 << 20, transcendentals=0),
    )
    stats = exchange(stats, TP)
    k_cache, v_cache, kv_message = call(
        functools.partial(keys_kernel, heads_width),
        (shaped((256, 128), BF16), shaped((256, 128), BF16), shaped((4, 272, 256), BF16)),
        [stats, key_value, cosine, sine, k_gain.reshape(128, 1), marks],
        name="keys",
    )
    kv_message, stats = lax.optimization_barrier((kv_message, stats))
    q_message = call(
        functools.partial(queries_kernel, heads_width),
        shaped((144, 256), BF16),
        [stats, query, cosine, sine, q_gain.reshape(128, 1), marks],
        name="queries",
    )
    keys = exchange(kv_message, ("yc", "zh"))
    order = (0, 1, 3, 2)
    queries = [q_message] + [
        permute(q_message, ("ya", "yb"), lambda ya, yb, d=d: divmod((ya * 2 + yb + d) % 4, 2))
        for d in order[1:]
    ]
    o_messages = call(
        functools.partial(attend_kernel, order),
        shaped((4, 144, 256), BF16),
        queries + [keys],
        scalars=at,
        scratch=[pltpu.VMEM((4, 256, 1024), F32)],
        name="attend",
    )
    o_messages, wo_all = lax.optimization_barrier((o_messages, wo_all))
    own = call(
        merge_kernel, shaped((128, 256), BF16), [exchange(o_messages, ("ya", "yb"))], name="merge"
    )
    other = permute(own, ("c",), lambda c: (1 - c,))
    partials = call(
        partial_kernel, shaped((4, 4, 160, 256), BF16), [own, other, wo_all], name="partial"
    )
    partials = call(
        along_x_kernel,
        shaped((4, 160, 256), BF16),
        [exchange(partials, ("xh", "xl"))],
        name="along_x",
    )
    mixed = jnp.sum(exchange(partials, ("zl",)).astype(F32), axis=0)
    hidden_out = (x_t + modulation[2] * mixed).T.astype(BF16)
    return (hidden_out, k_cache, v_cache)


def solution(mesh):
    split = Mesh(mesh.devices.reshape(tuple(SIZES.values())), tuple(SIZES))
    in_specs = (
        P(SEQ, TP),
        P(SEQ),
        P(None, SEQ),
        P(None, None, TP),
        P(SEQ, None, TP),
        P(TP),
        P(TP),
        P(TP, SEQ),
    )
    out_specs = (P(SEQ, TP), P(SEQ, TP), P(SEQ, TP))
    return jax.shard_map(body, mesh=split, in_specs=in_specs, out_specs=out_specs, check_vma=False)
```

```python
import functools
import itertools
import math

import jax
import jax.numpy as jnp
import numpy as np
from jax import lax
from jax.experimental import pallas as pl
from jax.experimental.pallas import tpu as pltpu
from jax.sharding import Mesh
from jax.sharding import PartitionSpec as P

HEAD_DIM = 128
EPSILON = 1e-06
NEG_FILL = -1e30
LOG2E = 1.4426950408889634

SEQ = ("ya", "yb", "yc", "zh")
TP = ("zl", "xh", "xl", "c")
SIZES = {"ya": 2, "yb": 2, "yc": 2, "zh": 2, "zl": 4, "xh": 2, "xl": 2, "c": 2}

F32 = jnp.float32
BF16 = jnp.bfloat16
VMEM_LIMIT = 48 << 20


def permute(value, axes, move):
    sizes = [SIZES[a] for a in axes]
    pairs = []
    for at in itertools.product(*[range(n) for n in sizes]):
        to = move(*at)
        pairs.append((int(np.ravel_multi_index(at, sizes)), int(np.ravel_multi_index(to, sizes))))
    return lax.ppermute(value, axes, pairs)


def contract_first(lhs, rhs):
    return lax.dot_general(lhs, rhs, (((0,), (0,)), ((), ())), preferred_element_type=F32)


def call(kernel, out_shape, operands, scalars=None, scratch=(), name=None, cost=None):
    vmem = pl.BlockSpec(memory_space=pltpu.VMEM)
    smem = pl.BlockSpec(memory_space=pltpu.SMEM)
    specs = ([] if scalars is None else [smem]) + [vmem] * len(operands)
    args = ([] if scalars is None else [scalars]) + list(operands)
    return pl.pallas_call(
        kernel,
        out_shape=out_shape,
        in_specs=specs,
        out_specs=jax.tree.map(lambda _: vmem, out_shape),
        scratch_shapes=list(scratch),
        compiler_params=pltpu.CompilerParams(vmem_limit_bytes=VMEM_LIMIT),
        cost_estimate=cost,
        name=name,
    )(*args)


def shaped(shape, dtype):
    return jax.ShapeDtypeStruct(shape, dtype)


def project_kernel(at, mine, theirs, w, out_q, out_kv, stats):
    c = at[0]
    total = None
    for i, held in enumerate((mine, theirs)):
        core = lax.rem(c + i, 2)
        for x in range(4):
            rows = [w.at[2 * z + x // 2, x % 2] for z in range(4)]
            weights = jnp.concatenate(
                [jnp.concatenate([part[p, core] for part in rows], axis=0) for p in range(3)], axis=1
            )
            features = jnp.concatenate([held[x, z] for z in range(4)], axis=0)
            term = contract_first(weights, features)
            total = term if total is None else total + term
    query, key, value = total[:128], total[128:256], total[256:]
    out_q[...] = query
    out_kv[0] = key
    out_kv[1] = value
    rows = []
    for part in (query, key):
        row = jnp.sum(part * part, axis=0, keepdims=True)
        rows += [row[:, :128], row[:, 128:]]
    packed = jnp.concatenate(rows + [jnp.zeros((4, 128), F32)], axis=0)
    for t in range(stats.shape[0]):
        stats[t] = packed


def rotated(value, gain, totals, cos, sin, width):
    even = lax.rem(lax.broadcasted_iota(jnp.int32, (HEAD_DIM, 256), 0), 2) == 0
    factor = jnp.concatenate([totals[0:1], totals[1:2]], axis=1)
    factor = lax.rsqrt(factor / width + EPSILON)
    normed = value * factor * gain
    after = pltpu.roll(normed, HEAD_DIM - 1, 0)
    before = pltpu.roll(normed, 1, 0)
    partner = jnp.where(even, -after, before)
    return normed * cos + partner * sin


def keys_kernel(width, got, kv, cosine, sine, kg, marks, k_cache, v_cache, message):
    totals = jnp.sum(got[...], axis=0)[2:4]
    k_rot = rotated(kv[0], kg[...], totals, cosine[...], sine[...], width)
    value = kv[1]
    k_low = k_rot.astype(BF16)
    v_low = value.astype(BF16)
    extra = marks[...].astype(BF16)
    for t in range(message.shape[0]):
        message[t, :128] = k_low
        message[t, 128:256] = v_low
        message[t, 256:272] = extra
    k_cache[...] = k_rot.T.astype(BF16)
    v_cache[...] = value.T.astype(BF16)


def queries_kernel(width, got, q, cosine, sine, qg, marks, message):
    totals = jnp.sum(got[...], axis=0)[:2]
    q_low = rotated(q[...], qg[...], totals, cosine[...], sine[...], width).astype(BF16)
    extra = marks[...].astype(BF16)
    message[:128] = q_low
    message[128:144] = extra


def attend_kernel(order, at, q0, q1, q2, q3, keys, messages, held):
    count = keys.shape[0]
    scale = LOG2E / math.sqrt(HEAD_DIM)
    parts = (q0, q1, q2, q3)
    q_low = jnp.concatenate([q[:128] for q in parts], axis=1)
    seg_q = jnp.concatenate([q[128:144] for q in parts], axis=1).astype(F32)[:1]
    top = None
    for b in range(count):
        seg_k = keys[b, 256:272].astype(F32).T[:, :1]
        scores = contract_first(keys[b, :128], q_low) * scale
        scores = jnp.where(seg_k == seg_q, scores, NEG_FILL)
        held[b] = scores
        here = jnp.max(scores, axis=0, keepdims=True)
        top = here if top is None else jnp.maximum(top, here)
    top = jnp.maximum(top, -1e20)
    total = jnp.zeros((1, 1024), F32)
    weighted = jnp.zeros((HEAD_DIM, 1024), F32)
    for b in range(count):
        weights = jnp.exp2(held[b] - top)
        total = total + jnp.sum(weights, axis=0, keepdims=True)
        weighted = weighted + jnp.dot(
            keys[b, 128:256], weights.astype(BF16), preferred_element_type=F32
        )
    some = total > 0.0
    safe = jnp.where(some, total, 1.0)
    out = weighted / safe
    lse = jnp.where(some, top + jnp.log2(safe), NEG_FILL)
    high = lse.astype(BF16)
    rest = lse - high.astype(F32)
    middle = rest.astype(BF16)
    low = (rest - middle.astype(F32)).astype(BF16)
    rows = jnp.concatenate(
        [high.astype(F32), middle.astype(F32), low.astype(F32), jnp.zeros((13, 1024), F32)], axis=0
    ).astype(BF16)
    for place, d in enumerate(order):
        here = slice(256 * place, 256 * place + 256)
        target = lax.rem(at[1] + 4 - d, 4)
        messages[target, :128] = out[:, here].astype(BF16)
        messages[target, 128:144] = rows[:, here]


def merge_kernel(got, out):
    lses, parts = [], []
    for d in range(4):
        rows = got[d, 128:144].astype(F32)
        lses.append(rows[0:1] + rows[1:2] + rows[2:3])
        parts.append(got[d, :128].astype(F32))
    top = functools.reduce(jnp.maximum, lses)
    weights = [jnp.exp2(lse - top) for lse in lses]
    total = sum(weights[1:], weights[0])
    value = None
    for weight, part in zip(weights, parts, strict=True):
        term = part * (weight / total)
        value = term if value is None else value + term
    out[...] = value.astype(BF16)


def partial_kernel(own, other, w, messages):
    both = jnp.concatenate([own[...], other[...]], axis=0)
    for x in range(4):
        for z in range(4):
            block, low = 2 * z + x // 2, x % 2
            weights = jnp.concatenate([w[block, 0, low], w[block, 1, low]], axis=1)
            messages[x, z] = jnp.dot(weights, both, preferred_element_type=F32).astype(BF16)


def along_x_kernel(got, out):
    for z in range(4):
        total = got[0, z].astype(F32)
        for x in range(1, 4):
            total = total + got[x, z].astype(F32)
        out[z] = total.astype(BF16)


def exchange(value, axes):
    return lax.all_to_all(value, axes, 0, 0, tiled=True)


def spread(value, axes):
    count = math.prod(SIZES[a] for a in axes)
    return exchange(jnp.broadcast_to(value, (count,) + value.shape), axes)


def body(hidden_in, seg_ids, positions, mod_table, w_qkv, q_gain, k_gain, w_out):
    tok_rows, feat_local = hidden_in.shape
    model_width = feat_local * 32
    heads_width = 4096
    at = jnp.stack(
        [lax.axis_index("c"), lax.axis_index("ya") * 2 + lax.axis_index("yb")]
    ).astype(jnp.int32)

    w_pair = lax.all_gather(jnp.transpose(w_qkv, (1, 0, 2)), "zh", axis=0, tiled=False)
    wo_pair = lax.all_gather(w_out.T, "zh", axis=0, tiled=False)
    w_all = lax.all_gather(w_pair, ("ya", "yb", "yc"), axis=0, tiled=False)
    w_all = w_all.reshape(8, 2, 3, 2, 160, 128)

    x_t = hidden_in.T.astype(F32)
    sums = jnp.stack([jnp.sum(x_t, axis=0), jnp.sum(x_t * x_t, axis=0)]).reshape(4, 128)
    sums = jnp.concatenate([sums, jnp.zeros((4, 128), F32)], axis=0)
    sums = jnp.broadcast_to(sums, (32, 8, 128))
    segment_count = mod_table.shape[0]
    onehot = (seg_ids[None, :] == jnp.arange(segment_count, dtype=jnp.int32)[:, None]).astype(F32)
    modulation = lax.dot_general(
        mod_table.reshape(segment_count, 3 * feat_local),
        onehot,
        (((0,), (0,)), ((), ())),
        precision=lax.Precision.HIGHEST,
    ).reshape(3, feat_local, tok_rows)
    part_width = HEAD_DIM // 6
    widths = (HEAD_DIM - 4 * part_width, 2 * part_width, 2 * part_width)
    angles = []
    for axis_number in range(3):
        width = widths[axis_number]
        exponent = jnp.arange(0, width, 2, dtype=F32) / width
        frequency = jnp.repeat(1.0 / 10000.0**exponent, 2)
        angles.append(positions[axis_number].astype(F32)[None, :] * frequency[:, None])
    angle = jnp.concatenate(angles, axis=0)
    cosine, sine = jnp.cos(angle), jnp.sin(angle)
    marks = jnp.broadcast_to(seg_ids[None, :].astype(F32), (16, tok_rows))
    sums = exchange(sums, TP)
    sums = jnp.sum(sums, axis=0)[:4].reshape(2, tok_rows)
    mean_value = sums[0:1] / model_width
    variance = sums[1:2] / model_width - mean_value * mean_value
    normed = (x_t - mean_value) * lax.rsqrt(variance + EPSILON)
    packet = (normed * (1.0 + modulation[1]) + modulation[0]).astype(BF16)
    packet, wo_pair = lax.optimization_barrier((packet, wo_pair))

    held = spread(spread(packet, ("zl",)), ("xh", "xl"))
    theirs = permute(held, ("c",), lambda c: (1 - c,))
    theirs, cosine, sine, marks = lax.optimization_barrier((theirs, cosine, sine, marks))

    query, key_value, stats = call(
        project_kernel,
        (shaped((128, 256), F32), shaped((2, 128, 256), F32), shaped((32, 8, 128), F32)),
        [held, theirs, w_all],
        scalars=at,
        name="project",
        cost=pl.CostEstimate(flops=2 * 256 * 5120 * 384, bytes_accessed=6 << 20, transcendentals=0),
    )
    core = lax.axis_index("c")
    wo_pair = wo_pair.reshape(2, 2, 160, 128)
    wo_own = lax.dynamic_index_in_dim(wo_pair, core, axis=1, keepdims=False)
    wo_give = lax.dynamic_index_in_dim(wo_pair, 1 - core, axis=1, keepdims=False)
    wo_own, wo_give, stats = lax.optimization_barrier((wo_own, wo_give, stats))
    wo_other = permute(wo_give, ("c",), lambda c: (1 - c,))
    stats, wo_other = lax.optimization_barrier((exchange(stats, TP), wo_other))
    wo_all = lax.all_gather(jnp.stack([wo_own, wo_other]), ("ya", "yb", "yc"), axis=0, tiled=False)
    k_cache, v_cache, kv_message = call(
        functools.partial(keys_kernel, heads_width),
        (shaped((256, 128), BF16), shaped((256, 128), BF16), shaped((4, 272, 256), BF16)),
        [stats, key_value, cosine, sine, k_gain.reshape(128, 1), marks],
        name="keys",
    )
    kv_message, stats = lax.optimization_barrier((kv_message, stats))
    q_message = call(
        functools.partial(queries_kernel, heads_width),
        shaped((144, 256), BF16),
        [stats, query, cosine, sine, q_gain.reshape(128, 1), marks],
        name="queries",
    )
    keys = exchange(kv_message, ("yc", "zh"))
    order = (0, 1, 3, 2)
    queries = [q_message] + [
        permute(q_message, ("ya", "yb"), lambda ya, yb, d=d: divmod((ya * 2 + yb + d) % 4, 2))
        for d in order[1:]
    ]
    o_messages = call(
        functools.partial(attend_kernel, order),
        shaped((4, 144, 256), BF16),
        queries + [keys],
        scalars=at,
        scratch=[pltpu.VMEM((4, 256, 1024), F32)],
        name="attend",
    )
    o_messages, wo_all = lax.optimization_barrier((o_messages, wo_all))
    own = call(
        merge_kernel, shaped((128, 256), BF16), [exchange(o_messages, ("ya", "yb"))], name="merge"
    )
    other = permute(own, ("c",), lambda c: (1 - c,))
    partials = call(
        partial_kernel, shaped((4, 4, 160, 256), BF16), [own, other, wo_all], name="partial"
    )
    partials = call(
        along_x_kernel,
        shaped((4, 160, 256), BF16),
        [exchange(partials, ("xh", "xl"))],
        name="along_x",
    )
    mixed = jnp.sum(exchange(partials, ("zl",)).astype(F32), axis=0)
    hidden_out = (x_t + modulation[2] * mixed).T.astype(BF16)
    return (hidden_out, k_cache, v_cache)


def solution(mesh):
    split = Mesh(mesh.devices.reshape(tuple(SIZES.values())), tuple(SIZES))
    in_specs = (
        P(SEQ, TP),
        P(SEQ),
        P(None, SEQ),
        P(None, None, TP),
        P(SEQ, None, TP),
        P(TP),
        P(TP),
        P(TP, SEQ),
    )
    out_specs = (P(SEQ, TP), P(SEQ, TP), P(SEQ, TP))
    return jax.shard_map(body, mesh=split, in_specs=in_specs, out_specs=out_specs, check_vma=False)
```

```python
import functools
import itertools
import math

import jax
import jax.numpy as jnp
import numpy as np
from jax import lax
from jax.experimental import pallas as pl
from jax.experimental.pallas import tpu as pltpu
from jax.sharding import Mesh
from jax.sharding import PartitionSpec as P

HEAD_DIM = 128
EPSILON = 1e-06
NEG_FILL = -1e30
LOG2E = 1.4426950408889634

SEQ = ("ya", "yb", "yc", "zh")
TP = ("zl", "xh", "xl", "c")
SIZES = {"ya": 2, "yb": 2, "yc": 2, "zh": 2, "zl": 4, "xh": 2, "xl": 2, "c": 2}

F32 = jnp.float32
BF16 = jnp.bfloat16
VMEM_LIMIT = 48 << 20


def permute(value, axes, move):
    sizes = [SIZES[a] for a in axes]
    pairs = []
    for at in itertools.product(*[range(n) for n in sizes]):
        to = move(*at)
        pairs.append((int(np.ravel_multi_index(at, sizes)), int(np.ravel_multi_index(to, sizes))))
    return lax.ppermute(value, axes, pairs)


def contract_first(lhs, rhs):
    return lax.dot_general(lhs, rhs, (((0,), (0,)), ((), ())), preferred_element_type=F32)


def call(kernel, out_shape, operands, scalars=None, scratch=(), name=None, cost=None):
    vmem = pl.BlockSpec(memory_space=pltpu.VMEM)
    smem = pl.BlockSpec(memory_space=pltpu.SMEM)
    specs = ([] if scalars is None else [smem]) + [vmem] * len(operands)
    args = ([] if scalars is None else [scalars]) + list(operands)
    return pl.pallas_call(
        kernel,
        out_shape=out_shape,
        in_specs=specs,
        out_specs=jax.tree.map(lambda _: vmem, out_shape),
        scratch_shapes=list(scratch),
        compiler_params=pltpu.CompilerParams(vmem_limit_bytes=VMEM_LIMIT),
        cost_estimate=cost,
        name=name,
    )(*args)


def shaped(shape, dtype):
    return jax.ShapeDtypeStruct(shape, dtype)


def project_kernel(at, mine, theirs, w, out_q, out_kv, stats):
    c = at[0]
    total = None
    for i, held in enumerate((mine, theirs)):
        core = lax.rem(c + i, 2)
        for x in range(4):
            rows = [w.at[2 * z + x // 2, x % 2] for z in range(4)]
            weights = jnp.concatenate(
                [jnp.concatenate([part[p, core] for part in rows], axis=0) for p in range(3)], axis=1
            )
            features = jnp.concatenate([held[x, z] for z in range(4)], axis=0)
            term = contract_first(weights, features)
            total = term if total is None else total + term
    query, key, value = total[:128], total[128:256], total[256:]
    out_q[...] = query
    out_kv[0] = key
    out_kv[1] = value
    rows = []
    for part in (query, key):
        row = jnp.sum(part * part, axis=0, keepdims=True)
        rows += [row[:, :128], row[:, 128:]]
    packed = jnp.concatenate(rows + [jnp.zeros((4, 128), F32)], axis=0)
    for t in range(stats.shape[0]):
        stats[t] = packed


def rotated(value, gain, totals, cos, sin, width):
    even = lax.rem(lax.broadcasted_iota(jnp.int32, (HEAD_DIM, 256), 0), 2) == 0
    factor = jnp.concatenate([totals[0:1], totals[1:2]], axis=1)
    factor = lax.rsqrt(factor / width + EPSILON)
    normed = value * factor * gain
    after = pltpu.roll(normed, HEAD_DIM - 1, 0)
    before = pltpu.roll(normed, 1, 0)
    partner = jnp.where(even, -after, before)
    return normed * cos + partner * sin


def keys_kernel(width, got, kv, cosine, sine, kg, marks, k_cache, v_cache, message):
    totals = jnp.sum(got[...], axis=0)[2:4]
    k_rot = rotated(kv[0], kg[...], totals, cosine[...], sine[...], width)
    value = kv[1]
    k_low = k_rot.astype(BF16)
    v_low = value.astype(BF16)
    extra = marks[...].astype(BF16)
    for t in range(message.shape[0]):
        message[t, :128] = k_low
        message[t, 128:256] = v_low
        message[t, 256:272] = extra
    k_cache[...] = k_rot.T.astype(BF16)
    v_cache[...] = value.T.astype(BF16)


def queries_kernel(width, got, q, cosine, sine, qg, marks, message):
    totals = jnp.sum(got[...], axis=0)[:2]
    q_low = rotated(q[...], qg[...], totals, cosine[...], sine[...], width).astype(BF16)
    extra = marks[...].astype(BF16)
    message[:128] = q_low
    message[128:144] = extra


def attend_kernel(order, at, q0, q1, q2, q3, keys, messages, held):
    count = keys.shape[0]
    scale = LOG2E / math.sqrt(HEAD_DIM)
    parts = (q0, q1, q2, q3)
    q_low = jnp.concatenate([q[:128] for q in parts], axis=1)
    seg_q = jnp.concatenate([q[128:144] for q in parts], axis=1).astype(F32)[:1]
    top = None
    for b in range(count):
        seg_k = keys[b, 256:272].astype(F32).T[:, :1]
        scores = contract_first(keys[b, :128], q_low) * scale
        scores = jnp.where(seg_k == seg_q, scores, NEG_FILL)
        held[b] = scores
        here = jnp.max(scores, axis=0, keepdims=True)
        top = here if top is None else jnp.maximum(top, here)
    top = jnp.maximum(top, -1e20)
    total = jnp.zeros((1, 1024), F32)
    weighted = jnp.zeros((HEAD_DIM, 1024), F32)
    for b in range(count):
        weights = jnp.exp2(held[b] - top)
        total = total + jnp.sum(weights, axis=0, keepdims=True)
        weighted = weighted + jnp.dot(
            keys[b, 128:256], weights.astype(BF16), preferred_element_type=F32
        )
    some = total > 0.0
    safe = jnp.where(some, total, 1.0)
    out = weighted / safe
    lse = jnp.where(some, top + jnp.log2(safe), NEG_FILL)
    high = lse.astype(BF16)
    rest = lse - high.astype(F32)
    middle = rest.astype(BF16)
    low = (rest - middle.astype(F32)).astype(BF16)
    rows = jnp.concatenate(
        [high.astype(F32), middle.astype(F32), low.astype(F32), jnp.zeros((13, 1024), F32)], axis=0
    ).astype(BF16)
    for place, d in enumerate(order):
        here = slice(256 * place, 256 * place + 256)
        target = lax.rem(at[1] + 4 - d, 4)
        messages[target, :128] = out[:, here].astype(BF16)
        messages[target, 128:144] = rows[:, here]


def merge_kernel(got, out):
    lses, parts = [], []
    for d in range(4):
        rows = got[d, 128:144].astype(F32)
        lses.append(rows[0:1] + rows[1:2] + rows[2:3])
        parts.append(got[d, :128].astype(F32))
    top = functools.reduce(jnp.maximum, lses)
    weights = [jnp.exp2(lse - top) for lse in lses]
    total = sum(weights[1:], weights[0])
    value = None
    for weight, part in zip(weights, parts, strict=True):
        term = part * (weight / total)
        value = term if value is None else value + term
    out[...] = value.astype(BF16)


def partial_kernel(own, other, w, messages):
    both = jnp.concatenate([own[...], other[...]], axis=0)
    for x in range(4):
        for z in range(4):
            block, low = 2 * z + x // 2, x % 2
            weights = jnp.concatenate([w[block, 0, low], w[block, 1, low]], axis=1)
            messages[x, z] = jnp.dot(weights, both, preferred_element_type=F32).astype(BF16)


def along_x_kernel(got, out):
    for z in range(4):
        total = got[0, z].astype(F32)
        for x in range(1, 4):
            total = total + got[x, z].astype(F32)
        out[z] = total.astype(BF16)


def exchange(value, axes):
    return lax.all_to_all(value, axes, 0, 0, tiled=True)


def spread(value, axes):
    count = math.prod(SIZES[a] for a in axes)
    return exchange(jnp.broadcast_to(value, (count,) + value.shape), axes)


def body(hidden_in, seg_ids, positions, mod_table, w_qkv, q_gain, k_gain, w_out):
    tok_rows, feat_local = hidden_in.shape
    model_width = feat_local * 32
    heads_width = 4096
    at = jnp.stack(
        [lax.axis_index("c"), lax.axis_index("ya") * 2 + lax.axis_index("yb")]
    ).astype(jnp.int32)

    w_pair = lax.all_gather(jnp.transpose(w_qkv, (1, 0, 2)), "zh", axis=0, tiled=False)
    wo_pair = lax.all_gather(w_out.T, "zh", axis=0, tiled=False)
    w_all = lax.all_gather(w_pair, ("ya", "yb", "yc"), axis=0, tiled=False)
    w_all = w_all.reshape(8, 2, 3, 2, 160, 128)

    x_t = hidden_in.T.astype(F32)
    sums = jnp.stack([jnp.sum(x_t, axis=0), jnp.sum(x_t * x_t, axis=0)]).reshape(4, 128)
    sums = jnp.concatenate([sums, jnp.zeros((4, 128), F32)], axis=0)
    sums = jnp.broadcast_to(sums, (32, 8, 128))
    segment_count = mod_table.shape[0]
    onehot = (seg_ids[None, :] == jnp.arange(segment_count, dtype=jnp.int32)[:, None]).astype(F32)
    modulation = lax.dot_general(
        mod_table.reshape(segment_count, 3 * feat_local),
        onehot,
        (((0,), (0,)), ((), ())),
        precision=lax.Precision.HIGHEST,
    ).reshape(3, feat_local, tok_rows)
    part_width = HEAD_DIM // 6
    widths = (HEAD_DIM - 4 * part_width, 2 * part_width, 2 * part_width)
    angles = []
    for axis_number in range(3):
        width = widths[axis_number]
        exponent = jnp.arange(0, width, 2, dtype=F32) / width
        frequency = jnp.repeat(1.0 / 10000.0**exponent, 2)
        angles.append(positions[axis_number].astype(F32)[None, :] * frequency[:, None])
    angle = jnp.concatenate(angles, axis=0)
    cosine, sine = jnp.cos(angle), jnp.sin(angle)
    marks = jnp.broadcast_to(seg_ids[None, :].astype(F32), (16, tok_rows))
    sums = exchange(sums, TP)
    sums = jnp.sum(sums, axis=0)[:4].reshape(2, tok_rows)
    mean_value = sums[0:1] / model_width
    variance = sums[1:2] / model_width - mean_value * mean_value
    normed = (x_t - mean_value) * lax.rsqrt(variance + EPSILON)
    packet = (normed * (1.0 + modulation[1]) + modulation[0]).astype(BF16)
    packet, wo_pair = lax.optimization_barrier((packet, wo_pair))

    held = spread(spread(packet, ("zl",)), ("xh", "xl"))
    theirs = permute(held, ("c",), lambda c: (1 - c,))
    theirs, cosine, sine, marks = lax.optimization_barrier((theirs, cosine, sine, marks))

    query, key_value, stats = call(
        project_kernel,
        (shaped((128, 256), F32), shaped((2, 128, 256), F32), shaped((32, 8, 128), F32)),
        [held, theirs, w_all],
        scalars=at,
        name="project",
        cost=pl.CostEstimate(flops=2 * 256 * 5120 * 384, bytes_accessed=6 << 20, transcendentals=0),
    )
    core = lax.axis_index("c")
    wo_pair = wo_pair.reshape(2, 2, 160, 128)
    wo_own = lax.dynamic_index_in_dim(wo_pair, core, axis=1, keepdims=False)
    wo_give = lax.dynamic_index_in_dim(wo_pair, 1 - core, axis=1, keepdims=False)
    wo_own, wo_give, stats = lax.optimization_barrier((wo_own, wo_give, stats))
    wo_other = permute(wo_give, ("c",), lambda c: (1 - c,))
    stats, wo_other = lax.optimization_barrier((exchange(stats, TP), wo_other))
    wo_all = lax.all_gather(jnp.stack([wo_own, wo_other]), ("ya", "yb", "yc"), axis=0, tiled=False)
    k_cache, v_cache, kv_message = call(
        functools.partial(keys_kernel, heads_width),
        (shaped((256, 128), BF16), shaped((256, 128), BF16), shaped((4, 272, 256), BF16)),
        [stats, key_value, cosine, sine, k_gain.reshape(128, 1), marks],
        name="keys",
    )
    kv_message, stats = lax.optimization_barrier((kv_message, stats))
    q_message = call(
        functools.partial(queries_kernel, heads_width),
        shaped((144, 256), BF16),
        [stats, query, cosine, sine, q_gain.reshape(128, 1), marks],
        name="queries",
    )
    keys = exchange(kv_message, ("yc", "zh"))
    order = (0, 1, 3, 2)
    queries = [q_message] + [
        permute(q_message, ("ya", "yb"), lambda ya, yb, d=d: divmod((ya * 2 + yb + d) % 4, 2))
        for d in order[1:]
    ]
    o_messages = call(
        functools.partial(attend_kernel, order),
        shaped((4, 144, 256), BF16),
        queries + [keys],
        scalars=at,
        scratch=[pltpu.VMEM((4, 256, 1024), F32)],
        name="attend",
    )
    own = call(
        merge_kernel, shaped((128, 256), BF16), [exchange(o_messages, ("ya", "yb"))], name="merge"
    )
    other = permute(own, ("c",), lambda c: (1 - c,))
    partials = call(
        partial_kernel, shaped((4, 4, 160, 256), BF16), [own, other, wo_all], name="partial"
    )
    partials = call(
        along_x_kernel,
        shaped((4, 160, 256), BF16),
        [exchange(partials, ("xh", "xl"))],
        name="along_x",
    )
    mixed = jnp.sum(exchange(partials, ("zl",)).astype(F32), axis=0)
    hidden_out = (x_t + modulation[2] * mixed).T.astype(BF16)
    return (hidden_out, k_cache, v_cache)


def solution(mesh):
    split = Mesh(mesh.devices.reshape(tuple(SIZES.values())), tuple(SIZES))
    in_specs = (
        P(SEQ, TP),
        P(SEQ),
        P(None, SEQ),
        P(None, None, TP),
        P(SEQ, None, TP),
        P(TP),
        P(TP),
        P(TP, SEQ),
    )
    out_specs = (P(SEQ, TP), P(SEQ, TP), P(SEQ, TP))
    return jax.shard_map(body, mesh=split, in_specs=in_specs, out_specs=out_specs, check_vma=False)
```
